32 devices in a mesh: img: 8 (over z, x), head: 4 (over y, core).
Axes of the slice: x: 2, y: 2, z: 4, core: 2. Of those that a mesh axis runs over, the one named last changes fastest.
Arguments:
- media_patches: bfloat16 [32, 5, 256, 1024], P(('img', 'head')), may hold values from -6 to 6
- latent_rows: bfloat16 [32, 5, 64, 1024], P(('img', 'head')), may hold values from -6 to 6
- media_counts: int32 [32], P(('img', 'head')), may hold values from 1 to 5, as said below
- norm_gains: bfloat16 [3, 1024], P(None, ('img', 'head')), may hold values from 0.5 to 1.5
- norm_biases: bfloat16 [3, 1024], P(None, ('img', 'head')), may hold values from -3 to 3
- query_weight: bfloat16 [1024, 512], P(('img', 'head')), may hold values from -0.375 to 0.375
- key_value_weight: bfloat16 [1024, 1024], P(('img', 'head')), may hold values from -0.1875 to 0.1875
- output_weight: bfloat16 [512, 1024], P(('img', 'head')), may hold values from -0.75 to 0.75
- up_weight: bfloat16 [1024, 4096], P('img', 'head'), may hold values from -0.1875 to 0.1875
- down_weight: bfloat16 [4096, 1024], P('head', 'img'), may hold values from -0.125 to 0.125
- cotangent: bfloat16 [32, 5, 64, 1024], P(('img', 'head')), may hold values from -6 to 6
Outputs:
- new_latents: bfloat16 [32, 5, 64, 1024], P(('img', 'head'))
- media_grad: bfloat16 [32, 5, 256, 1024], P(('img', 'head'))
- latent_grad: bfloat16 [32, 5, 64, 1024], P(('img', 'head'))
- gains_grad: float32 [3, 1024], P(None, ('img', 'head'))
- biases_grad: float32 [3, 1024], P(None, ('img', 'head'))
- query_grad: float32 [1024, 512], P(('img', 'head'))
- key_value_grad: float32 [1024, 1024], P(('img', 'head'))
- output_grad: float32 [512, 1024], P(('img', 'head'))
- up_grad: float32 [1024, 4096], P('img', 'head')
- down_grad: float32 [4096, 1024], P('head', 'img')
The draws below stay inside these ranges and needn't reach their ends.
Inputs may be any that keep to these rules, and one draw needn't show every extreme that they name: `media_counts`: each sample has 5 media slots; the slots whose index is below its count hold images, the others are empty; every draw has a sample with all 5 slots filled and one with a single image.
All inputs are finite; a program needn't handle non-finite values.
Results may differ from the reference program's by a relative error of at most 0.015.
The reference program's roundings to bfloat16 on the way count: a program that leaves them out, or rounds other values in their place, can miss the bound.
Values may be sent and summed in bfloat16 or wider, within the bound.
A program may use at most 192 MiB of HBM per device.

```python
import jax
import jax.numpy as jnp
from jax import lax

D = 1024
HEADS = 8
HD = 64
FF = 4096
LATENTS = 64
PATCHES = 256
MEDIA = 5
INNER = 512
SAMPLES = 32


def draw_media_counts(key, part):
    first_key, second_key, third_key = jax.random.split(jax.random.fold_in(key, 17), 3)
    upper_draw = jax.random.randint(first_key, (SAMPLES,), 1, MEDIA + 1)
    lower_draw = jax.random.randint(second_key, (SAMPLES,), 2, MEDIA + 2)
    counted = jnp.minimum(upper_draw, lower_draw)
    places = jax.random.permutation(third_key, SAMPLES)
    counted = counted.at[places[0]].set(MEDIA)
    counted = counted.at[places[1]].set(1)
    return counted.astype(jnp.int32)


def raised(result, own_key, source, target, blocks, factor):
    def block_of(axis_at):
        return (jnp.arange(result.shape[axis_at]) // (result.shape[axis_at] // blocks)).reshape((-1,) + (1,) * (result.ndim - 1 - axis_at))

    one_side = jax.random.permutation(own_key, blocks)[block_of(target)]
    second = (block_of(target) + blocks // 2) % blocks
    return jnp.where((block_of(source) == one_side) | (block_of(source) == second), factor * result, result)


def block_scale(own_key, extent, shards, smallest, high):
    def one(axis_at, shards_of):
        steps = jax.random.uniform(jax.random.fold_in(jax.random.fold_in(own_key, 6), axis_at), (shards_of,), jnp.float32, smallest / len(shards), high / len(shards))
        return jnp.repeat(jnp.exp(steps), extent[axis_at] // shards_of).reshape((-1,) + (1,) * (len(extent) - axis_at - 1))

    loudness = one(*shards[0])
    for cut in shards[1:]:
        loudness = loudness * one(*cut)
    return loudness


def normal_values(key, dims, width, limit, cuts=(), dtype=jnp.bfloat16):
    gain = block_scale(key, dims, cuts, -0.22, 0.18) if cuts else 1.0
    entries = jax.random.normal(key, dims, jnp.float32) * width * gain
    return jnp.minimum(jnp.maximum(entries, -limit), limit).astype(dtype)


def bell_draw_with(rng, shape, width, reach, cuts, heavy, dtype=jnp.bfloat16):
    values = width * jax.random.normal(rng, shape, jnp.float32)
    if cuts:
        values = values * block_scale(rng, shape, cuts, -0.22, 0.18)
    return jnp.clip(raised(values, jax.random.fold_in(rng, 3), *heavy), -reach, reach).astype(dtype)


def setup_inputs(seed: int = 0) -> dict:
    key_list = jax.random.split(jax.random.key(seed), 12)
    return {
        "media_patches": bell_draw_with(key_list[0], (SAMPLES, MEDIA, PATCHES, D), 1.0, 6.0, ((0, 32),), (0, 3, 32, 2.75)),
        "latent_rows": normal_values(key_list[1], (SAMPLES, MEDIA, LATENTS, D), 1.0, 6.0, ((0, 32),)),
        "media_counts": draw_media_counts(jax.random.fold_in(key_list[11], 71), 0),
        "norm_gains": jnp.clip(1.0 + 0.1 * jax.random.normal(key_list[3], (3, D), jnp.float32), 0.5, 1.5).astype(jnp.bfloat16),
        "norm_biases": normal_values(key_list[4], (3, D), 0.5, 3.0, ((1, 32),)),
        "query_weight": normal_values(key_list[5], (D, INNER), (D // 4) ** -0.5, 0.375, ((0, 32),)),
        "key_value_weight": normal_values(key_list[6], (D, 2 * INNER), D ** -0.5, 0.1875, ((0, 32),)),
        "output_weight": normal_values(key_list[7], (INNER, D), (INNER // 8) ** -0.5, 0.75, ((0, 32),)),
        "up_weight": normal_values(key_list[8], (D, FF), D ** -0.5, 0.1875, ((0, 8), (1, 4))),
        "down_weight": normal_values(key_list[9], (FF, D), (FF // 2) ** -0.5, 0.125, ((0, 4), (1, 8))),
        "cotangent": bell_draw_with(key_list[10], (SAMPLES, MEDIA, LATENTS, D), 1.0, 6.0, ((0, 32),), (0, 3, 32, 2.75)),
    }


@jax.custom_vjp
def low(v):
    return lax.optimization_barrier(v.astype(jnp.bfloat16)).astype(jnp.float32)

@jax.custom_vjp
def low_back(v):
    return v

def low_keep(v):
    return (low(v), None)

def low_pass(kept, grad):
    return (grad,)

def back_keep(v):
    return (v, None)

def back_low(kept, grad):
    return (low(grad),)
low.defvjp(low_keep, low_pass)
low_back.defvjp(back_keep, back_low)

def layer_norm(values, norm_gain, norm_shift):
    centered = values - lax.optimization_barrier(jnp.mean(values, axis=-1, keepdims=True))
    variance = lax.optimization_barrier(jnp.mean(centered * centered, axis=-1, keepdims=True))
    return centered * lax.rsqrt(variance + 1e-05) * norm_gain + norm_shift

def product(spec_text, left_side, right_side):
    return jnp.einsum(spec_text, left_side, right_side, precision=lax.Precision.HIGHEST)

def block_forward(params, media_block, latent_block, mask_block):
    norm_gain, norm_shift, query_weight, key_value_weight, output_weight, up_weight, down_weight = params
    images = media_block.shape[0]
    inner_width = HEADS * HD
    score_scale = HD ** (-0.5)
    media_norm = low(layer_norm(media_block, norm_gain[0], norm_shift[0]))
    latent_norm = low(layer_norm(latent_block, norm_gain[1], norm_shift[1]))
    queries = low(low_back(product('ild,de->ile', latent_norm, query_weight) * score_scale))
    key_input = jnp.concatenate([media_norm, latent_norm], axis=1)
    key_values = low(low_back(product('ikd,de->ike', key_input, key_value_weight)))
    keys_all = key_values[:, :, :inner_width].reshape(images, PATCHES + LATENTS, HEADS, HD)
    values_all = key_values[:, :, inner_width:].reshape(images, PATCHES + LATENTS, HEADS, HD)
    query_heads = queries.reshape(images, LATENTS, HEADS, HD)
    scores = low_back(product('iqhe,ikhe->ihqk', query_heads, keys_all))
    row_max = lax.optimization_barrier(jnp.max(scores, axis=-1, keepdims=True))
    weights = jnp.exp(scores - row_max)
    probabilities = low(weights / lax.optimization_barrier(jnp.sum(weights, axis=-1, keepdims=True)))
    attended = product('ihqk,ikhe->iqhe', probabilities, values_all).reshape(images, LATENTS, inner_width)
    attended = low(low_back(attended))
    attn_delta = low_back(product('ile,ed->ild', attended, output_weight))
    mid_latent = latent_block + attn_delta
    hidden_in = low(layer_norm(mid_latent, norm_gain[2], norm_shift[2]))
    pre_act = low_back(product('ild,df->ilf', hidden_in, up_weight))
    act_low = low(jax.nn.gelu(pre_act, approximate=False))
    branch_out = low_back(product('ilf,fd->ild', act_low, down_weight))
    return mask_block[:, None, None] * (mid_latent + branch_out)

def reference(media_patches, latent_rows, media_counts, norm_gains, norm_biases, query_weight, key_value_weight, output_weight, up_weight, down_weight, cotangent):
    slot_mask = (jnp.arange(MEDIA)[None, :] < media_counts[:, None]).astype(jnp.float32)
    block_count = SAMPLES // 2
    group_size = 2 * MEDIA
    mask_blocks = slot_mask.reshape(block_count, group_size)
    params = (norm_gains.astype(jnp.float32), norm_biases.astype(jnp.float32), query_weight.astype(jnp.float32), key_value_weight.astype(jnp.float32), output_weight.astype(jnp.float32), up_weight.astype(jnp.float32), down_weight.astype(jnp.float32))

    def forward(weights_all, media_full, latent_full):
        media_blocks = media_full.reshape(block_count, group_size, PATCHES, D)
        latent_blocks = latent_full.reshape(block_count, group_size, LATENTS, D)

        def one_block(operands):
            return block_forward(weights_all, operands[0], operands[1], operands[2])
        outputs = lax.map(jax.checkpoint(one_block), (media_blocks, latent_blocks, mask_blocks))
        return outputs.reshape(SAMPLES, MEDIA, LATENTS, D)
    media_full = media_patches.astype(jnp.float32)
    latent_full = latent_rows.astype(jnp.float32)
    new_latents, pullback = jax.vjp(forward, params, media_full, latent_full)
    param_grads, media_grad, latent_grad = pullback(cotangent.astype(jnp.float32))
    return (new_latents.astype(jnp.bfloat16), media_grad.astype(jnp.bfloat16), latent_grad.astype(jnp.bfloat16), param_grads[0], param_grads[1], param_grads[2], param_grads[3], param_grads[4], param_grads[5], param_grads[6])
```

```python
import jax
import jax.numpy as jnp
from jax import lax
from jax.experimental import pallas as pl
from jax.experimental.pallas import tpu as pltpu
from jax.sharding import PartitionSpec as P

HEADS = 8


def layer_norm(values, norm_gain, norm_shift):
    centered = values - jnp.mean(values, axis=-1, keepdims=True)
    variance = jnp.mean(centered * centered, axis=-1, keepdims=True)
    return centered * lax.rsqrt(variance + 1e-05) * norm_gain + norm_shift


def norm_backward(values, norm_gain, norm_shift, upstream):
    primal, pullback = jax.vjp(layer_norm, values, norm_gain, norm_shift)
    return pullback(upstream)


def exact_gelu(values):
    return jax.nn.gelu(values, approximate=False)


def gelu_backward(values, upstream):
    primal, pullback = jax.vjp(exact_gelu, values)
    return pullback(upstream)[0]


def contract_rows(left_side, right_side):
    return lax.dot_general(
        left_side, right_side, (((0,), (0,)), ((), ())), preferred_element_type=jnp.float32
    )


def contract_cols(left_side, right_side):
    return lax.dot_general(
        left_side, right_side, (((1,), (1,)), ((), ())), preferred_element_type=jnp.float32
    )


def gathered_plan(
    media_patches,
    latent_rows,
    media_counts,
    norm_gains,
    norm_biases,
    query_weight,
    key_value_weight,
    output_weight,
    up_weight,
    down_weight,
    cotangent,
):
    samp_local, media_slots, patches, model_width = media_patches.shape
    queries_per = latent_rows.shape[2]
    images = samp_local * media_slots
    keys_per = patches + queries_per
    rows_local = images * queries_per
    gathered = (
        lax.all_gather(query_weight, ("img", "head"), axis=0, tiled=True),
        lax.all_gather(key_value_weight, ("img", "head"), axis=0, tiled=True),
        lax.all_gather(output_weight, ("img", "head"), axis=0, tiled=True),
        lax.all_gather(norm_gains, ("img", "head"), axis=1, tiled=True),
        lax.all_gather(norm_biases, ("img", "head"), axis=1, tiled=True),
    )
    query_full, key_value_full, output_full, gains_low, biases_low = gathered
    norm_gain = gains_low.astype(jnp.float32)
    norm_shift = biases_low.astype(jnp.float32)
    inner_width = query_full.shape[1]
    head_size = inner_width // HEADS
    score_scale = head_size ** (-0.5)
    up_part, down_part = (
        lax.all_gather(up_weight, "img", axis=0, tiled=True),
        lax.all_gather(down_weight, "img", axis=1, tiled=True),
    )
    media_full = media_patches.reshape(images, patches, model_width).astype(jnp.float32)
    latent_full = latent_rows.reshape(images, queries_per, model_width).astype(jnp.float32)
    media_norm = layer_norm(media_full, norm_gain[0], norm_shift[0]).astype(jnp.bfloat16)
    latent_norm = layer_norm(latent_full, norm_gain[1], norm_shift[1]).astype(jnp.bfloat16)
    query_rows = (
        jnp.einsum("ild,de->ile", latent_norm, query_full, preferred_element_type=jnp.float32)
        * score_scale
    ).astype(jnp.bfloat16)
    key_input = jnp.concatenate([media_norm, latent_norm], axis=1)
    key_value_rows = jnp.einsum(
        "ikd,de->ike", key_input, key_value_full, preferred_element_type=jnp.float32
    ).astype(jnp.bfloat16)
    query_heads = (
        query_rows.reshape(images, queries_per, HEADS, head_size)
        .transpose(2, 0, 1, 3)
        .reshape(HEADS, images, queries_per * head_size)
    )
    key_value_heads = (
        key_value_rows.reshape(images, keys_per, 2, HEADS, head_size)
        .transpose(3, 0, 1, 2, 4)
        .reshape(HEADS, images, keys_per, 2 * head_size)
    )
    query_group, key_value_group = (
        lax.all_to_all(query_heads, "head", split_axis=0, concat_axis=1, tiled=True),
        lax.all_to_all(key_value_heads, "head", split_axis=0, concat_axis=1, tiled=True),
    )
    heads_dev = query_group.shape[0]
    group_images = query_group.shape[1]
    query_block = query_group.reshape(heads_dev, group_images, queries_per, head_size)
    key_block = key_value_group[:, :, :, :head_size]
    value_block = key_value_group[:, :, :, head_size:]
    scores = jnp.einsum(
        "hgqe,hgke->hgqk", query_block, key_block, preferred_element_type=jnp.float32
    )
    row_max = jnp.max(scores, axis=-1, keepdims=True)
    weights = jnp.exp(scores - row_max)
    totals = jnp.sum(weights, axis=-1, keepdims=True)
    log_total = row_max + jnp.log(totals)
    probabilities = (weights / totals).astype(jnp.bfloat16)
    attended = jnp.einsum(
        "hgqk,hgke->hgqe", probabilities, value_block, preferred_element_type=jnp.float32
    ).astype(jnp.bfloat16)
    attended_back = lax.all_to_all(
        attended.reshape(heads_dev, group_images, queries_per * head_size),
        "head",
        split_axis=1,
        concat_axis=0,
        tiled=True,
    )
    attended_local = (
        attended_back.reshape(HEADS, images, queries_per, head_size)
        .transpose(1, 2, 0, 3)
        .reshape(images, queries_per, inner_width)
    )
    attn_delta = jnp.einsum(
        "ile,ed->ild", attended_local, output_full, preferred_element_type=jnp.float32
    )
    mid_latent = latent_full + attn_delta
    hidden_in = (
        layer_norm(mid_latent, norm_gain[2], norm_shift[2])
        .astype(jnp.bfloat16)
        .reshape(rows_local, model_width)
    )
    slot_mask = (
        (jnp.arange(media_slots)[None, :] < media_counts[:, None])
        .astype(jnp.float32)
        .reshape(images, 1, 1)
    )
    up_full, down_full = (
        lax.all_gather(up_part, "head", axis=1, tiled=True),
        lax.all_gather(down_part, "head", axis=0, tiled=True),
    )
    pre_act = jnp.dot(hidden_in, up_full, preferred_element_type=jnp.float32)
    act_low = exact_gelu(pre_act).astype(jnp.bfloat16)
    branch_out = jnp.dot(act_low, down_full, preferred_element_type=jnp.float32)
    result = slot_mask * (mid_latent + branch_out.reshape(images, queries_per, model_width))
    new_latents = result.astype(jnp.bfloat16).reshape(latent_rows.shape)
    out_grad = slot_mask * cotangent.reshape(images, queries_per, model_width).astype(jnp.float32)
    branch_grad = out_grad.astype(jnp.bfloat16).reshape(rows_local, model_width)
    act_grad = contract_cols(branch_grad, down_full)
    pre_grad = gelu_backward(pre_act, act_grad).astype(jnp.bfloat16)
    down_grad_whole = contract_rows(act_low, branch_grad)
    up_grad_whole = contract_rows(hidden_in, pre_grad)
    hidden_grad = contract_cols(pre_grad, up_full)
    up_grad_part, down_grad_part = (
        lax.psum_scatter(
            up_grad_whole.astype(jnp.bfloat16), "head", scatter_dimension=1, tiled=True
        ).astype(jnp.float32),
        lax.psum_scatter(
            down_grad_whole.astype(jnp.bfloat16), "head", scatter_dimension=0, tiled=True
        ).astype(jnp.float32),
    )
    up_grad, down_grad = (
        lax.psum_scatter(
            up_grad_part.astype(jnp.bfloat16), "img", scatter_dimension=0, tiled=True
        ).astype(jnp.float32),
        lax.psum_scatter(
            down_grad_part.astype(jnp.bfloat16), "img", scatter_dimension=1, tiled=True
        ).astype(jnp.float32),
    )
    mid_from_norm, gain_ff, bias_ff = norm_backward(
        mid_latent,
        norm_gain[2],
        norm_shift[2],
        hidden_grad.reshape(images, queries_per, model_width),
    )
    mid_grad = out_grad + mid_from_norm
    delta_low = mid_grad.astype(jnp.bfloat16)
    output_weight_grad = jnp.einsum(
        "ile,ild->ed", attended_local, delta_low, preferred_element_type=jnp.float32
    )
    attended_grad = jnp.einsum(
        "ild,ed->ile", delta_low, output_full, preferred_element_type=jnp.float32
    ).astype(jnp.bfloat16)
    grad_heads = (
        attended_grad.reshape(images, queries_per, HEADS, head_size)
        .transpose(2, 0, 1, 3)
        .reshape(HEADS, images, queries_per * head_size)
    )
    grad_group = lax.all_to_all(
        grad_heads, "head", split_axis=0, concat_axis=1, tiled=True
    ).reshape(heads_dev, group_images, queries_per, head_size)
    scores_again = jnp.einsum(
        "hgqe,hgke->hgqk", query_block, key_block, preferred_element_type=jnp.float32
    )
    probs_again = jnp.exp(scores_again - log_total)
    probs_again_low = probs_again.astype(jnp.bfloat16)
    prob_grad = jnp.einsum(
        "hgqe,hgke->hgqk", grad_group, value_block, preferred_element_type=jnp.float32
    )
    value_grad = jnp.einsum(
        "hgqk,hgqe->hgke", probs_again_low, grad_group, preferred_element_type=jnp.float32
    )
    row_dot = jnp.sum(prob_grad * probs_again, axis=-1, keepdims=True)
    score_grad = (probs_again * (prob_grad - row_dot)).astype(jnp.bfloat16)
    query_grad_group = jnp.einsum(
        "hgqk,hgke->hgqe", score_grad, key_block, preferred_element_type=jnp.float32
    ).astype(jnp.bfloat16)
    key_grad = jnp.einsum(
        "hgqk,hgqe->hgke", score_grad, query_block, preferred_element_type=jnp.float32
    )
    key_value_grad_group = jnp.concatenate([key_grad, value_grad], axis=-1).astype(jnp.bfloat16)
    query_back, key_value_back = (
        lax.all_to_all(
            query_grad_group.reshape(heads_dev, group_images, queries_per * head_size),
            "head",
            split_axis=1,
            concat_axis=0,
            tiled=True,
        ),
        lax.all_to_all(key_value_grad_group, "head", split_axis=1, concat_axis=0, tiled=True),
    )
    query_local = (
        query_back.reshape(HEADS, images, queries_per, head_size)
        .transpose(1, 2, 0, 3)
        .reshape(images, queries_per, inner_width)
    )
    key_value_local = (
        key_value_back.reshape(HEADS, images, keys_per, 2, head_size)
        .transpose(1, 2, 3, 0, 4)
        .reshape(images, keys_per, 2 * inner_width)
    )
    query_weight_grad = (
        jnp.einsum("ild,ile->de", latent_norm, query_local, preferred_element_type=jnp.float32)
        * score_scale
    )
    key_value_weight_grad = jnp.einsum(
        "ikd,ike->de", key_input, key_value_local, preferred_element_type=jnp.float32
    )
    key_input_grad = jnp.einsum(
        "ike,de->ikd", key_value_local, key_value_full, preferred_element_type=jnp.float32
    )
    latent_norm_grad = (
        jnp.einsum("ile,de->ild", query_local, query_full, preferred_element_type=jnp.float32)
        * score_scale
        + key_input_grad[:, patches:]
    )
    media_grad_full, gain_media, bias_media = norm_backward(
        media_full, norm_gain[0], norm_shift[0], key_input_grad[:, :patches]
    )
    latent_from_norm, gain_latent, bias_latent = norm_backward(
        latent_full, norm_gain[1], norm_shift[1], latent_norm_grad
    )
    latent_grad_full = mid_grad + latent_from_norm
    gain_terms = jnp.stack([gain_media, gain_latent, gain_ff])
    bias_terms = jnp.stack([bias_media, bias_latent, bias_ff])
    summed = (
        lax.psum_scatter(query_weight_grad, ("img", "head"), scatter_dimension=0, tiled=True),
        lax.psum_scatter(key_value_weight_grad, ("img", "head"), scatter_dimension=0, tiled=True),
        lax.psum_scatter(output_weight_grad, ("img", "head"), scatter_dimension=0, tiled=True),
        lax.psum_scatter(gain_terms, ("img", "head"), scatter_dimension=1, tiled=True),
        lax.psum_scatter(bias_terms, ("img", "head"), scatter_dimension=1, tiled=True),
    )
    media_grad = media_grad_full.astype(jnp.bfloat16).reshape(media_patches.shape)
    latent_grad = latent_grad_full.astype(jnp.bfloat16).reshape(latent_rows.shape)
    return (
        new_latents,
        media_grad,
        latent_grad,
        summed[3],
        summed[4],
        summed[0],
        summed[1],
        summed[2],
        up_grad,
        down_grad,
    )


def tpose(values):
    return jnp.transpose(values, (1, 0))


def dot_nn(left_side, right_side):
    return jnp.dot(left_side, right_side, preferred_element_type=jnp.float32)


def block_kernel(
    counts,
    media_in,
    latent_in,
    cot_in,
    query_in,
    key_value_in,
    output_in,
    up_in,
    down_in,
    norm_in,
    new_out,
    media_out,
    latent_out,
    norm_out,
    query_out,
    key_value_out,
    output_out,
    up_out,
    down_out,
    slab,
    query_full,
    wide,
    hid,
    cotr,
    turned,
    media_v,
    media_n,
    latent_v,
    latent_n,
    media_t,
    latent_t,
    kv_media,
    kv_latent,
    query_v,
    att_v,
    att_t,
    mid_v,
    pair,
    grads,
    xrecv,
    zrecv,
    hsend,
    hrecv,
    hysend,
    hyrecv,
    hown,
    delta_v,
    attg_v,
    qgrad_v,
    upstream,
    normg,
    normv,
    gacc,
    gsend,
    gyr,
    gzr,
    gzr_v,
    loc,
    at_z,
    at_x,
    at_y,
    at_c,
    ff_z,
    ff_x,
    nb_z,
    nb_x,
    nb_y,
    nb_c,
    hd_y,
    hd_c,
    hd_f,
    bg_y,
    bg_c,
    hp_c,
    hp_y,
    rf_x,
    rf_z,
    ra_c,
    ra_y,
    ra_x,
    ra_z,
    gr_c,
    gr_z,
    sent,
    outs,
):
    n_z, n_x, n_head = 4, 2, 4
    img = lax.axis_index("img")
    head = lax.axis_index("head")
    z = img // n_x
    x = img % n_x
    y = head // 2
    c = head % 2
    xp, yp, cp = 1 - x, 1 - y, 1 - c
    xdev = (z * n_x + xp, head)
    ydev = (img, yp * 2 + c)
    cdev = (img, y * 2 + cp)
    near = (1, 3, 2)

    def zat(k):
        return (z + k) % n_z

    def zdev(zz):
        return (zz * n_x + x, head)

    width = media_v.shape[2]
    slots = latent_v.shape[0]
    queries = latent_v.shape[1]
    hidden = up_in.shape[2]
    inner = query_full.shape[3]
    f32 = jnp.float32
    bf16 = jnp.bfloat16
    scale = (inner // HEADS) ** (-0.5)

    def rcopy(src, dst, sem_s, sem_r, dev):
        return pltpu.make_async_remote_copy(
            src_ref=src,
            dst_ref=dst,
            send_sem=sem_s,
            recv_sem=sem_r,
            device_id=dev,
            device_id_type=pl.DeviceIdType.MESH,
        )

    def send(src, dst, sem_s, sem_r, dev):
        rcopy(src, dst, sem_s, sem_r, dev).start()

    def arrived(ref, sem):
        pltpu.make_async_copy(ref, ref, sem).wait()

    unit = img * n_head + head
    local = [
        pltpu.make_async_copy(key_value_in, slab.at[unit, 0:32], loc.at[0]),
        pltpu.make_async_copy(output_in, slab.at[unit, 32:48], loc.at[1]),
        pltpu.make_async_copy(query_in.at[0:16], slab.at[unit, 48:64, 0:inner], loc.at[2]),
        pltpu.make_async_copy(query_in.at[16:32], slab.at[unit, 48:64, inner:width], loc.at[3]),
        pltpu.make_async_copy(norm_in, normg.at[head, :, pl.ds(pl.multiple_of(img * 128, 128), 128)], loc.at[4]),
        pltpu.make_async_copy(up_in, wide.at[pl.ds(img * 4, 4), :, 0:hidden], loc.at[5]),
        pltpu.make_async_copy(cot_in, pair.at[0:slots], loc.at[6]),
        pltpu.make_async_copy(latent_in, latent_v, loc.at[7]),
        pltpu.make_async_copy(media_in, media_v, loc.at[8]),
    ]
    for copy in local:
        copy.start()

    barrier = pltpu.get_barrier_semaphore()
    peers = [zdev(zat(k)) for k in near] + [xdev, ydev, cdev]
    for dev in peers:
        pl.semaphore_signal(barrier, inc=1, device_id=dev, device_id_type=pl.DeviceIdType.MESH)
    pl.semaphore_wait(barrier, len(peers))

    def lanes(ii):
        return pl.ds(pl.multiple_of(ii * 128, 128), 128)

    local[4].wait()
    for k in near:
        send(norm_in, normg.at[head, :, lanes(img)], sent.at[0], nb_z.at[z], zdev(zat(k)))
    for copy in local[0:4]:
        copy.wait()

    def put_slab(uu, sem, dev):
        send(slab.at[uu], slab.at[uu], sent.at[1], sem, dev)

    for k in near:
        put_slab(unit, at_z.at[z], zdev(zat(k)))
    put_slab(unit, at_x.at[z], xdev)
    put_slab(unit, at_y.at[img], ydev)
    put_slab(unit, at_c.at[img, y], cdev)

    local[5].wait()
    down = down_in[...]
    for j in range(hidden // 128):
        wide[pl.ds(img * 4, 4), :, hidden + j * 128 : hidden + (j + 1) * 128] = tpose(
            down[j * 128 : (j + 1) * 128, :]
        ).reshape(4, 32, 128)

    local[6].wait()
    filled = counts[0]
    for m in range(slots):
        keep = jnp.clip(filled - m, 0, 1).astype(f32)
        cotr[head * slots + m] = (pair[m].astype(f32) * keep).astype(bf16)

    def nb_wait(kind, idx, ref):
        arrived(ref, kind.at[idx])

    for k in near:
        zz = zat(k)
        arrived(normg.at[head, :, lanes(zz * n_x + x)], nb_z.at[zz])
    for k in (0,) + near:
        zz = zat(k)
        ii = zz * n_x + x
        send(normg.at[head, :, lanes(ii)], normg.at[head, :, lanes(ii)], sent.at[2], nb_x.at[zz], xdev)

    def at_forward_z(k):
        zz = zat(k)
        uu = (zz * n_x + x) * n_head + head
        arrived(slab.at[uu], at_z.at[zz])
        put_slab(uu, at_x.at[zz], xdev)
        put_slab(uu, at_y.at[zz * n_x + x], ydev)
        put_slab(uu, at_c.at[zz * n_x + x, y], cdev)

    def at_forward_x(k):
        zz = zat(k)
        ii = zz * n_x + xp
        uu = ii * n_head + head
        arrived(slab.at[uu], at_x.at[zz])
        put_slab(uu, at_y.at[ii], ydev)
        put_slab(uu, at_c.at[ii, y], cdev)

    def at_forward_y(ii):
        uu = ii * n_head + yp * 2 + c
        arrived(slab.at[uu], at_y.at[ii])
        put_slab(uu, at_c.at[ii, yp], cdev)

    at_forward_z(1)
    at_forward_x(0)
    at_forward_z(3)
    for k in (0,) + near:
        zz = zat(k)
        arrived(normg.at[head, :, lanes(zz * n_x + xp)], nb_x.at[zz])
    send(normg.at[head], normg.at[head], sent.at[3], nb_y.at[0], ydev)
    send(normg.at[head], normg.at[head], sent.at[4], nb_c.at[y], cdev)
    at_forward_z(2)

    def ff_unit(ii, q):
        return wide.at[ii * 4 + q]

    for q in range(4):
        for k in near:
            send(ff_unit(img, q), ff_unit(img, q), sent.at[5], ff_z.at[z, q], zdev(zat(k)))
    at_forward_x(1)
    arrived(normg.at[yp * 2 + c], nb_y.at[0])
    send(normg.at[yp * 2 + c], normg.at[yp * 2 + c], sent.at[4], nb_c.at[yp], cdev)
    at_forward_x(3)
    for q in range(4):
        send(ff_unit(img, q), ff_unit(img, q), sent.at[6], ff_x.at[z, q], xdev)
    at_forward_x(2)
    own_cot = cotr.at[pl.ds(head * slots, slots)]
    send(own_cot, own_cot, sent.at[7], bg_y.at[0], ydev)
    send(own_cot, own_cot, sent.at[7], bg_c.at[y], cdev)

    arrived(normg.at[y * 2 + cp], nb_c.at[y])
    arrived(normg.at[yp * 2 + cp], nb_c.at[yp])
    normv[...] = normg[0] + normg[1] + normg[2] + normg[3]

    def gain(j):
        return normv[j : j + 1, :]

    def shift(j):
        return normv[3 + j : 4 + j, :]

    def statistics(values):
        centered = values - jnp.mean(values, axis=-1, keepdims=True)
        inverse = lax.rsqrt(jnp.mean(centered * centered, axis=-1, keepdims=True) + 1e-05)
        return centered * inverse, inverse

    def norm_rows(values, j):
        return (statistics(values)[0] * gain(j) + shift(j)).astype(bf16)

    half = queries // 2

    def norm_latent(m, carry):
        for r in range(2):
            rows = slice(r * half, (r + 1) * half)
            latent_n[m, rows, :] = norm_rows(latent_v[m, rows, :].astype(f32), 1)
        return carry

    def norm_media(m, carry):
        for r in range(2):
            rows = slice(r * half, (r + 1) * half)
            media_n[m, rows, :] = norm_rows(media_v[m, rows, :].astype(f32), 0)
        return carry

    local[7].wait()
    lax.fori_loop(0, slots, norm_latent, 0)
    at_forward_y(img)
    at_forward_y(zat(1) * n_x + x)
    local[8].wait()
    blocks = media_v.shape[0]
    step = blocks // 4
    order = [z * n_x + xp, zat(3) * n_x + x, zat(2) * n_x + x, zat(1) * n_x + xp, zat(3) * n_x + xp, zat(2) * n_x + xp]
    for r in range(4):
        lax.fori_loop(r * step, (r + 1) * step, norm_media, 0)
        at_forward_y(order[r])

    def turn_media(r, carry):
        block = media_n[pl.ds(r * 2, 2)].reshape(128, width)
        for d in range(width // 128):
            media_t[d * 128 : (d + 1) * 128, pl.ds(pl.multiple_of(r * 128, 128), 128)] = tpose(
                block[:, d * 128 : (d + 1) * 128]
            )
        return carry

    rows_latent = slots * queries

    def turn_latent(source, target, columns):
        whole = source[...].reshape(rows_latent, columns)
        for r in range(0, rows_latent, 128):
            stop = min(r + 128, rows_latent)
            for d in range(columns // 128):
                target[d * 128 : (d + 1) * 128, r:stop] = tpose(
                    whole[r:stop, d * 128 : (d + 1) * 128]
                )

    turn_latent(latent_n, latent_t, width)
    at_forward_y(order[4])
    lax.fori_loop(0, blocks * queries // 128, turn_media, 0)
    at_forward_y(order[5])

    def ff_forward(e):
        q = e // 3
        step_k = e % 3
        kk = step_k + 1
        zz = (z + kk) % n_z
        piece = ff_unit(zz * n_x + x, q)
        arrived(piece, ff_z.at[zz, q])
        send(piece, piece, sent.at[6], ff_x.at[zz, q], xdev)

    for e in range(3):
        ff_forward(e)
    for ii in range(8):
        for yy in range(2):
            arrived(slab.at[ii * n_head + yy * 2 + cp], at_c.at[ii, yy])
    ff_forward(3)

    query_full[:, 0] = slab[:, 48:64, 0:inner]
    query_full[:, 1] = slab[:, 48:64, inner:width]

    def query_tile(cols):
        return query_full[:, :, :, cols].reshape(width, -1)

    def kv_tile(cols):
        return slab[:, 0:32, cols].reshape(width, -1)

    def out_tile(cols):
        return slab[:, 32:48, cols].reshape(inner, -1)

    latent_rows_n = latent_n[...].reshape(rows_latent, width)

    def tile(t):
        return pl.ds(pl.multiple_of(t * 256, 256), 256)

    def query_step(t, carry):
        query_v[:, :, tile(t)] = (
            (dot_nn(latent_rows_n, query_full[:, :, :, tile(t)].reshape(width, 256)) * scale)
            .astype(bf16)
            .reshape(slots, queries, 256)
        )
        return carry

    lax.fori_loop(0, inner // 256, query_step, 0)
    groups = kv_media.shape[0]

    def kv_step(t, carry):
        weight = kv_tile(tile(t))
        kv_latent[:, :, tile(t)] = dot_nn(latent_rows_n, weight).astype(bf16).reshape(slots, queries, 256)

        def over_media(m, carry2):
            rows = media_n[pl.ds(m * 4, 4)].reshape(256, width)
            kv_media[m, :, tile(t)] = dot_nn(rows, weight).astype(bf16)
            return carry2

        return lax.fori_loop(0, groups, over_media, carry)

    lax.fori_loop(0, width // 256, kv_step, 0)
    ff_forward(4)

    def lane_mask(hh, dtype):
        lane = lax.broadcasted_iota(jnp.int32, (1, 256), 1)
        return (lane // queries == hh).astype(f32).astype(dtype)

    def spread(rows):
        return jnp.concatenate([rows * lane_mask(hh, bf16) for hh in range(4)], axis=0)

    def fold(rows):
        total = rows[0:queries] * lane_mask(0, f32)
        for hh in range(1, 4):
            total = total + rows[hh * queries : (hh + 1) * queries] * lane_mask(hh, f32)
        return total

    def probabilities(m, g):
        q_rows = spread(query_v[m, :, tile(g)])
        k_media = kv_media[m, :, tile(g)]
        k_latent = kv_latent[m, :, tile(g)]
        s_media = contract_cols(q_rows, k_media)
        s_latent = contract_cols(q_rows, k_latent)
        top = jnp.maximum(
            jnp.max(s_media, axis=-1, keepdims=True), jnp.max(s_latent, axis=-1, keepdims=True)
        )
        e_media = jnp.exp(s_media - top)
        e_latent = jnp.exp(s_latent - top)
        total = jnp.sum(e_media, axis=-1, keepdims=True) + jnp.sum(e_latent, axis=-1, keepdims=True)
        inverse = 1.0 / total
        return q_rows, k_media, k_latent, e_media * inverse, e_latent * inverse

    def attend(m, g):
        p_media, p_latent = probabilities(m, g)[3:]
        v_media = kv_media[m, :, tile(g + 2)]
        v_latent = kv_latent[m, :, tile(g + 2)]
        rows = dot_nn(p_media.astype(bf16), v_media) + dot_nn(p_latent.astype(bf16), v_latent)
        att_v[m, :, tile(g)] = fold(rows).astype(bf16)

    def forward_image(m, carry):
        attend(m, 0)
        attend(m, 1)
        mid_v[m] = latent_v[m].astype(f32) + dot_nn(att_v[m], out_tile(slice(0, width)))
        for r in range(2):
            rows = slice(r * half, (r + 1) * half)
            hid[head * slots + m, rows, :] = norm_rows(mid_v[m, rows, :], 2)
        piece = hid.at[head * slots + m]
        send(piece, piece, sent.at[8], hd_y.at[m], ydev)
        send(piece, piece, sent.at[8], hd_c.at[m], cdev)
        ff_forward(m + 5)
        return carry

    lax.fori_loop(0, slots, forward_image, 0)

    other = yp * 2 + c
    cot_other = cotr.at[pl.ds(other * slots, slots)]
    arrived(cot_other, bg_y.at[0])
    send(cot_other, cot_other, sent.at[7], bg_c.at[yp], cdev)
    turn_latent(att_v, att_t, inner)
    ff_forward(10)
    for yy in (y, yp):
        arrived(cotr.at[pl.ds((yy * 2 + cp) * slots, slots)], bg_c.at[yy])

    all_rows = n_head * slots * queries

    def turn_rows(source, slot):
        def body(r, carry):
            block = source[pl.ds(r * 2, 2)].reshape(128, width)
            for d in range(width // 128):
                turned[slot, d * 128 : (d + 1) * 128, pl.ds(pl.multiple_of(r * 128, 128), 128)] = tpose(
                    block[:, d * 128 : (d + 1) * 128]
                )
            return carry

        lax.fori_loop(0, all_rows // 128, body, 0)

    turn_rows(cotr, 1)
    ff_forward(11)

    def hid_forward(m, carry):
        piece = hid.at[other * slots + m]
        arrived(piece, hd_y.at[m])
        send(piece, piece, sent.at[8], hd_f.at[m], cdev)
        return carry

    lax.fori_loop(0, slots, hid_forward, 0)

    def hid_arrived(m, carry):
        arrived(hid.at[(y * 2 + cp) * slots + m], hd_c.at[m])
        arrived(hid.at[(yp * 2 + cp) * slots + m], hd_f.at[m])
        return carry

    lax.fori_loop(0, slots, hid_arrived, 0)
    turn_rows(hid, 0)

    def ff_arrived(e, carry):
        zz = e // 4
        q = e % 4
        arrived(ff_unit(zz * n_x + xp, q), ff_x.at[zz, q])
        return carry

    lax.fori_loop(0, 16, ff_arrived, 0)

    act_at = 4 * slots
    row_blocks = all_rows // 256

    def wide_tile(start):
        return wide[:, :, pl.ds(pl.multiple_of(start, 256), 256)].reshape(width, 256)

    def ff_step(t, carry):
        up = wide_tile(t * 256)
        dn = wide_tile(hidden + t * 256)

        def over_rows(r, carry2):
            rows = pl.ds(r * 4, 4)
            pre = dot_nn(hid[rows].reshape(256, width), up)
            grad = dot_nn(cotr[rows].reshape(256, width), dn)
            below = 0.5 * (1.0 + lax.erf(pre * 0.7071067811865476))
            slope = below + pre * (jnp.exp(-0.5 * pre * pre) * 0.3989422804014327)
            pair[rows, :, tile(t)] = (grad * slope).astype(bf16).reshape(4, 64, 256)
            pair[pl.ds(act_at + r * 4, 4), :, tile(t)] = (pre * below).astype(bf16).reshape(4, 64, 256)
            return carry2

        return lax.fori_loop(0, row_blocks, over_rows, carry)

    lax.fori_loop(0, hidden // 256, ff_step, 0)

    def wide_rows(part, t):
        return wide[pl.ds(t * 8, 8), :, part * hidden : (part + 1) * hidden].reshape(256, hidden)

    def head_sum(part):
        def rows_of(hh):
            return pair[pl.ds(part * act_at + hh * slots, slots)].reshape(rows_latent, hidden)

        for slot, hh in enumerate((yp * 2 + cp, y * 2 + cp)):
            left = rows_of(hh)

            def to_core(t, carry, left=left, slot=slot):
                value = contract_cols(left, wide_rows(part, t))
                hsend[part, slot, :, :, tile(t)] = value.astype(bf16).reshape(slots, queries, 256)
                return carry

            lax.fori_loop(0, width // 256, to_core, 0)
            send(hsend.at[part, slot], hrecv.at[part, slot], sent.at[9], hp_c.at[part, slot], cdev)
        left_y = rows_of(yp * 2 + c)
        arrived(hrecv.at[part, 0], hp_c.at[part, 0])

        def to_y(t, carry):
            value = contract_cols(left_y, wide_rows(part, t)).reshape(slots, queries, 256)
            hysend[part, :, :, tile(t)] = (value + hrecv[part, 0, :, :, tile(t)].astype(f32)).astype(bf16)
            return carry

        lax.fori_loop(0, width // 256, to_y, 0)
        send(hysend.at[part], hyrecv.at[part], sent.at[10], hp_y.at[part], ydev)
        left_own = rows_of(head)
        arrived(hrecv.at[part, 1], hp_c.at[part, 1])

        def to_own(t, carry):
            value = contract_cols(left_own, wide_rows(part, t)).reshape(slots, queries, 256)
            hown[part, :, :, tile(t)] = value + hrecv[part, 1, :, :, tile(t)].astype(f32)
            return carry

        lax.fori_loop(0, width // 256, to_own, 0)

    arrived(hid.at[0 : 3 * slots], sent.at[8])
    head_sum(0)

    def grad_unit(u, carry):
        zz = (z + 1 + u // 2) % n_z
        part = u % 2
        left = turned[part, pl.ds(pl.multiple_of(zz * 256, 256), 256), :]

        def over_cols(t, carry2):
            right = pair[pl.ds(part * act_at, act_at), :, tile(t)].reshape(all_rows, 256)
            value = dot_nn(left, right).astype(bf16).reshape(2, 128, 256)
            grads[zz, 0, part, :, tile(t)] = value[0]
            grads[zz, 1, part, :, tile(t)] = value[1]
            return carry2

        lax.fori_loop(0, hidden // 256, over_cols, 0)
        send(grads.at[zz, xp, part], xrecv.at[zz, part], sent.at[11], rf_x.at[zz, part], xdev)
        return carry

    def sum_unit(u):
        zz = (z + 1 + u // 2) % n_z
        part = u % 2
        arrived(xrecv.at[zz, part], rf_x.at[zz, part])

        def over(r, carry2):
            rows = pl.ds(pl.multiple_of(r * 16, 16), 16)
            grads[zz, x, part, rows, :] = (
                grads[zz, x, part, rows, :].astype(f32) + xrecv[zz, part, rows, :].astype(f32)
            ).astype(bf16)
            return carry2

        lax.fori_loop(0, 8, over, 0)
        send(grads.at[zz, x, part], zrecv.at[z, part], sent.at[12], rf_z.at[z, part], zdev(zz))

    def grad_and_sum(u, carry):
        grad_unit(u, carry)
        sum_unit(u - 4)
        return carry

    lax.fori_loop(0, 4, grad_unit, 0)
    lax.fori_loop(4, 8, grad_and_sum, 0)
    head_sum(1)
    sum_unit(4)

    gacc[...] = jnp.zeros_like(gacc)

    def tally(j, upper, xhat):
        gacc[j] += jnp.sum((upper * xhat).reshape(-1, 8, width), axis=0)
        gacc[3 + j] += jnp.sum(upper.reshape(-1, 8, width), axis=0)

    def norm_back(values, j, upper):
        xhat, inverse = statistics(values)
        tally(j, upper, xhat)
        g = upper * gain(j)
        return inverse * (
            g - jnp.mean(g, axis=-1, keepdims=True) - xhat * jnp.mean(g * xhat, axis=-1, keepdims=True)
        )

    arrived(hyrecv.at[0], hp_y.at[0])

    def mid_back(m, carry):
        for r in range(4):
            rows = slice(r * 16, (r + 1) * 16)
            upper = hown[0, m, rows, :] + hyrecv[0, m, rows, :].astype(f32)
            back = norm_back(mid_v[m, rows, :], 2, upper)
            total = cotr[head * slots + m, rows, :].astype(f32) + back
            hown[0, m, rows, :] = total
            delta_v[m, rows, :] = total.astype(bf16)
        return carry

    lax.fori_loop(0, slots, mid_back, 0)
    delta_rows = delta_v[...].reshape(rows_latent, width)

    def att_back(t, carry):
        weight = slab[pl.ds(t * 16, 16), 32:48, :].reshape(256, width)
        attg_v[:, :, tile(t)] = contract_cols(delta_rows, weight).astype(bf16).reshape(slots, queries, 256)
        return carry

    lax.fori_loop(0, inner // 256, att_back, 0)

    gslab = pair

    def gunit(ii, hh_y, hh_c):
        return ii * 4 + hh_c * 2 + hh_y

    def out_grad_step(t, carry):
        right = delta_v[:, :, tile(t)].reshape(rows_latent, 256)
        value = dot_nn(att_t[...], right).astype(bf16)
        for ii in range(8):
            for hh in range(4):
                at = (ii * 4 + hh) * 16
                gslab[gunit(ii, hh // 2, hh % 2), 32:48, tile(t)] = value[at : at + 16]
        return carry

    lax.fori_loop(0, width // 256, out_grad_step, 0)
    sum_unit(5)

    def back_pair(m, g):
        q_rows, k_media, k_latent, p_media, p_latent = probabilities(m, g)
        v_media = kv_media[m, :, tile(g + 2)]
        v_latent = kv_latent[m, :, tile(g + 2)]
        up_rows = spread(attg_v[m, :, tile(g)])
        g_media = contract_cols(up_rows, v_media)
        g_latent = contract_cols(up_rows, v_latent)
        dotted = jnp.sum(g_media * p_media, axis=-1, keepdims=True) + jnp.sum(
            g_latent * p_latent, axis=-1, keepdims=True
        )
        d_media = (p_media * (g_media - dotted)).astype(bf16)
        d_latent = (p_latent * (g_latent - dotted)).astype(bf16)
        qgrad_v[m, :, tile(g)] = fold(dot_nn(d_media, k_media) + dot_nn(d_latent, k_latent)).astype(bf16)
        kv_media[m, :, tile(g)] = contract_rows(d_media, q_rows).astype(bf16)
        kv_latent[m, :, tile(g)] = contract_rows(d_latent, q_rows).astype(bf16)
        kv_media[m, :, tile(g + 2)] = contract_rows(p_media.astype(bf16), up_rows).astype(bf16)
        kv_latent[m, :, tile(g + 2)] = contract_rows(p_latent.astype(bf16), up_rows).astype(bf16)

    def back_image(m, carry):
        back_pair(m, 0)
        back_pair(m, 1)
        return carry

    lax.fori_loop(0, slots, back_image, 0)

    gcr = hid
    gyr_v = media_n

    def kv_grad_chunk(zz):
        rows = pl.ds(pl.multiple_of(zz * 256, 256), 256)
        left_media = media_t[rows, :]
        left_latent = latent_t[rows, :]

        def over_kv(t, carry):
            value = dot_nn(left_media, kv_media[:, :, tile(t)].reshape(groups * 256, 256)) + dot_nn(
                left_latent, kv_latent[:, :, tile(t)].reshape(rows_latent, 256)
            )
            value = value.astype(bf16)
            for xx in range(2):
                for hh in range(4):
                    at = (xx * 4 + hh) * 32
                    gslab[gunit(zz * n_x + xx, hh // 2, hh % 2), 0:32, tile(t)] = value[at : at + 32]
            return carry

        lax.fori_loop(0, width // 256, over_kv, 0)

        def over_q(t, carry):
            value = dot_nn(left_latent, qgrad_v[:, :, tile(t)].reshape(rows_latent, 256)) * scale
            value = value.astype(bf16)
            for xx in range(2):
                for hh in range(4):
                    at = (xx * 4 + hh) * 32
                    uu = gunit(zz * n_x + xx, hh // 2, hh % 2)
                    gslab[uu, 48:64, pl.ds(pl.multiple_of(t * 256, 256), 256)] = value[at : at + 16]
                    gslab[uu, 48:64, pl.ds(pl.multiple_of(inner + t * 256, 256), 256)] = value[at + 16 : at + 32]
            return carry

        lax.fori_loop(0, inner // 256, over_q, 0)
        for xx in range(2):
            ii = zz * n_x + xx
            send(
                gslab.at[pl.ds(ii * 4 + cp * 2, 2)],
                gcr.at[pl.ds(ii * 2, 2)],
                sent.at[13],
                ra_c.at[ii],
                cdev,
            )

    def stage_y(zz):
        for xx in range(2):
            ii = zz * n_x + xx
            arrived(gcr.at[pl.ds(ii * 2, 2)], ra_c.at[ii])
            uu = gunit(ii, yp, c)
            gslab[uu] = (gslab[uu].astype(f32) + gcr[ii * 2 + yp].astype(f32)).astype(bf16)
            send(gslab.at[uu], gyr_v.at[ii], sent.at[14], ra_y.at[ii], ydev)

    def upto_y(ii):
        return (
            gslab[gunit(ii, y, c)].astype(f32) + gcr[ii * 2 + y].astype(f32) + gyr_v[ii].astype(f32)
        )

    def stage_x(zz):
        ii = zz * n_x + xp
        arrived(gyr_v.at[ii], ra_y.at[ii])
        uu = gunit(ii, y, c)
        gslab[uu] = upto_y(ii).astype(bf16)
        send(gslab.at[uu], gyr_v.at[8 + zz], sent.at[15], ra_x.at[zz], xdev)

    def stage_z(zz, last):
        ii = zz * n_x + x
        arrived(gyr_v.at[ii], ra_y.at[ii])
        arrived(gyr_v.at[8 + zz], ra_x.at[zz])
        if last:
            return upto_y(ii) + gyr_v[8 + zz].astype(f32)
        uu = gunit(ii, y, c)
        gslab[uu] = (upto_y(ii) + gyr_v[8 + zz].astype(f32)).astype(bf16)
        send(gslab.at[uu], gzr_v.at[z], sent.at[16], ra_z.at[z], zdev(zz))
        return None

    chunk = [zat(1), zat(3), zat(2), z]
    kv_grad_chunk(chunk[0])
    kv_grad_chunk(chunk[1])
    stage_y(chunk[0])
    kv_grad_chunk(chunk[2])
    stage_y(chunk[1])
    kv_grad_chunk(chunk[3])
    stage_y(chunk[2])

    arrived(hyrecv.at[1], hp_y.at[1])
    new_v = delta_v

    for m in range(slots):
        keep = jnp.clip(filled - m, 0, 1).astype(f32)
        for r in range(2):
            rows = slice(r * half, (r + 1) * half)
            branch = hown[1, m, rows, :] + hyrecv[1, m, rows, :].astype(f32)
            new_v[m, rows, :] = ((mid_v[m, rows, :] + branch) * keep).astype(bf16)
    new_copy = pltpu.make_async_copy(new_v, new_out, outs.at[0])
    new_copy.start()
    stage_y(chunk[3])

    def media_back(m, carry):
        rows = kv_media[m]

        def over(t, carry2):
            weight = slab[pl.ds(t * 8, 8), 0:32, :].reshape(256, width)
            upstream[:, tile(t)] = contract_cols(rows, weight)
            return carry2

        lax.fori_loop(0, width // 256, over, 0)

        def over_rows(r, carry2):
            at = pl.ds(pl.multiple_of(r * 16, 16), 16)
            block = m * 4 + r // 4
            inside = pl.ds(pl.multiple_of((r % 4) * 16, 16), 16)
            back = norm_back(media_v[block, inside, :].astype(f32), 0, upstream[at, :])
            media_v[block, inside, :] = back.astype(bf16)
            return carry2

        lax.fori_loop(0, 16, over_rows, 0)
        pltpu.make_async_copy(media_v.at[pl.ds(m * 4, 4)], media_out.at[pl.ds(m * 4, 4)], outs.at[1]).start()
        return carry

    def latent_back_tiles(m, carry):
        rows = kv_latent[m]
        query_rows = qgrad_v[m]

        def over(t, carry2):
            weight = slab[pl.ds(t * 8, 8), 0:32, :].reshape(256, width)
            query_weight = query_full[pl.ds(t * 8, 8)].reshape(256, inner)
            upstream[0:queries, tile(t)] = (
                contract_cols(rows, weight) + contract_cols(query_rows, query_weight) * scale
            )
            return carry2

        lax.fori_loop(0, width // 256, over, 0)
        for r in range(4):
            at = slice(r * 16, (r + 1) * 16)
            back = norm_back(latent_v[m, at, :].astype(f32), 1, upstream[at, :])
            latent_v[m, at, :] = (hown[0, m, at, :] + back).astype(bf16)
        return carry

    lax.fori_loop(0, slots, latent_back_tiles, 0)
    latent_copy = pltpu.make_async_copy(latent_v, latent_out, outs.at[2])
    latent_copy.start()
    lax.fori_loop(0, 2, media_back, 0)
    stage_x(chunk[0])
    stage_x(chunk[1])
    lax.fori_loop(2, 4, media_back, 0)
    stage_x(chunk[2])
    stage_z(chunk[0], False)
    stage_z(chunk[1], False)
    lax.fori_loop(4, 5, media_back, 0)
    stage_x(chunk[3])
    stage_z(chunk[2], False)

    for j in range(6):
        gsend[0, j : j + 1, :] = jnp.sum(gacc[j], axis=0, keepdims=True)
    gsend[0, 6:8, :] = jnp.zeros((2, width), f32)
    send(gsend.at[0], gyr.at[0], sent.at[17], gr_c.at[0], cdev)
    arrived(gyr.at[0], gr_c.at[0])
    gsend[1] = gsend[0] + gyr[0]
    send(gsend.at[1], gyr.at[1], sent.at[17], gr_c.at[1], ydev)
    arrived(gyr.at[1], gr_c.at[1])
    gsend[2] = gsend[1] + gyr[1]
    send(gsend.at[2], gyr.at[2], sent.at[17], gr_c.at[2], xdev)
    arrived(gyr.at[2], gr_c.at[2])
    gsend[3] = gsend[2] + gyr[2]
    for k in near:
        zz = zat(k)
        send(gsend.at[3, :, lanes(zz * n_x + x)], gzr.at[z], sent.at[18], gr_z.at[z], zdev(zz))
    total = gsend[3, :, lanes(img)]
    for k in near:
        zz = zat(k)
        arrived(gzr.at[zz], gr_z.at[zz])
        total = total + gzr[zz]
    norm_out[...] = total

    for part in range(2):
        arrived(xrecv.at[z, part], rf_x.at[z, part])
        for k in near:
            arrived(zrecv.at[zat(k), part], rf_z.at[zat(k), part])

    def up_last(r, carry):
        rows = pl.ds(pl.multiple_of(r * 16, 16), 16)
        value = grads[z, x, 0, rows, :].astype(f32) + xrecv[z, 0, rows, :].astype(f32)
        for k in near:
            value = value + zrecv[zat(k), 0, rows, :].astype(f32)
        up_out[rows, :] = value
        return carry

    lax.fori_loop(0, 8, up_last, 0)

    def down_last(j, carry):
        cols = pl.ds(pl.multiple_of(j * 128, 128), 128)
        value = grads[z, x, 1, :, cols].astype(f32) + xrecv[z, 1, :, cols].astype(f32)
        for k in near:
            value = value + zrecv[zat(k), 1, :, cols].astype(f32)
        down_out[cols, :] = tpose(value)
        return carry

    lax.fori_loop(0, hidden // 128, down_last, 0)

    final = stage_z(chunk[3], True)
    for k in near:
        zz = zat(k)
        arrived(gzr_v.at[zz], ra_z.at[zz])
        final = final + gzr_v[zz].astype(f32)
    key_value_out[...] = final[0:32]
    output_out[...] = final[32:48]
    query_out[0:16, :] = final[48:64, 0:inner]
    query_out[16:32, :] = final[48:64, inner:width]

    new_copy.wait()
    latent_copy.wait()
    arrived(media_v, outs.at[1])
    arrived(normg.at[0, :, 0:384], sent.at[0])
    arrived(slab.at[0:31], sent.at[1])
    arrived(normg.at[0, :, 0:512], sent.at[2])
    arrived(normg.at[0], sent.at[3])
    arrived(normg.at[0:2], sent.at[4])
    arrived(wide.at[0:12], sent.at[5])
    arrived(wide.at[0:16], sent.at[6])
    arrived(cotr.at[0 : 3 * slots], sent.at[7])
    arrived(hsend, sent.at[9])
    arrived(hysend, sent.at[10])
    arrived(xrecv, sent.at[11])
    arrived(zrecv.at[0:3], sent.at[12])
    arrived(gcr.at[0:16], sent.at[13])
    arrived(gyr_v.at[0:8], sent.at[14])
    arrived(gyr_v.at[0:4], sent.at[15])
    arrived(gyr_v.at[0:3], sent.at[16])
    arrived(gyr, sent.at[17])
    arrived(gzr.at[0:3], sent.at[18])


def block_plan(
    media_patches,
    latent_rows,
    media_counts,
    norm_gains,
    norm_biases,
    query_weight,
    key_value_weight,
    output_weight,
    up_weight,
    down_weight,
    cotangent,
):
    slots, patches, width = media_patches.shape[1:]
    queries = latent_rows.shape[2]
    inner = query_weight.shape[1]
    hidden = up_weight.shape[1]
    rows_up = up_weight.shape[0]
    part = norm_gains.shape[1]
    head = lax.axis_index("head")
    norm_rows = jnp.concatenate([norm_gains, norm_biases], axis=0).astype(jnp.float32)
    norm_tile = lax.dynamic_update_slice(
        jnp.zeros((8, 128), jnp.float32), norm_rows, (0, head * part)
    )
    blocks = slots * patches // 64
    bf16, f32 = jnp.bfloat16, jnp.float32
    shape = jax.ShapeDtypeStruct
    hbm = pl.BlockSpec(memory_space=pl.ANY)
    vmem = pl.BlockSpec(memory_space=pltpu.VMEM)
    smem = pl.BlockSpec(memory_space=pltpu.SMEM)
    dma = pltpu.SemaphoreType.DMA
    all_rows = 4 * slots * queries
    rows_latent = slots * queries
    outs = pl.pallas_call(
        block_kernel,
        out_shape=(
            shape((slots, queries, width), bf16),
            shape((blocks, 64, width), bf16),
            shape((slots, queries, width), bf16),
            shape((8, 128), f32),
            shape(query_weight.shape, f32),
            shape(key_value_weight.shape, f32),
            shape(output_weight.shape, f32),
            shape(up_weight.shape, f32),
            shape(down_weight.shape, f32),
        ),
        in_specs=[smem] + [hbm] * 7 + [vmem, hbm],
        out_specs=(hbm, hbm, hbm, vmem, vmem, vmem, vmem, vmem, vmem),
        scratch_shapes=[
            pltpu.VMEM((32, 64, width), bf16),
            pltpu.VMEM((32, 2, 16, inner), bf16),
            pltpu.VMEM((32, 32, 2 * hidden), bf16),
            pltpu.VMEM((4 * slots, queries, width), bf16),
            pltpu.VMEM((4 * slots, queries, width), bf16),
            pltpu.VMEM((2, width, all_rows), bf16),
            pltpu.VMEM((blocks, 64, width), bf16),
            pltpu.VMEM((blocks, 64, width), bf16),
            pltpu.VMEM((slots, queries, width), bf16),
            pltpu.VMEM((slots, queries, width), bf16),
            pltpu.VMEM((width, slots * patches), bf16),
            pltpu.VMEM((width, rows_latent), bf16),
            pltpu.VMEM((slots, patches, 2 * inner), bf16),
            pltpu.VMEM((slots, queries, 2 * inner), bf16),
            pltpu.VMEM((slots, queries, inner), bf16),
            pltpu.VMEM((slots, queries, inner), bf16),
            pltpu.VMEM((inner, rows_latent), bf16),
            pltpu.VMEM((slots, queries, width), f32),
            pltpu.VMEM((8 * slots, queries, width), bf16),
            pltpu.VMEM((4, 2, 2, rows_up, hidden), bf16),
            pltpu.VMEM((4, 2, rows_up, hidden), bf16),
            pltpu.VMEM((4, 2, rows_up, hidden), bf16),
            pltpu.VMEM((2, 2, slots, queries, width), bf16),
            pltpu.VMEM((2, 2, slots, queries, width), bf16),
            pltpu.VMEM((2, slots, queries, width), bf16),
            pltpu.VMEM((2, slots, queries, width), bf16),
            pltpu.VMEM((2, slots, queries, width), f32),
            pltpu.VMEM((slots, queries, width), bf16),
            pltpu.VMEM((slots, queries, inner), bf16),
            pltpu.VMEM((slots, queries, inner), bf16),
            pltpu.VMEM((patches, width), f32),
            pltpu.VMEM((4, 8, width), f32),
            pltpu.VMEM((8, width), f32),
            pltpu.VMEM((6, 8, width), f32),
            pltpu.VMEM((4, 8, width), f32),
            pltpu.VMEM((3, 8, width), f32),
            pltpu.VMEM((4, 8, 128), f32),
            pltpu.VMEM((4, 64, width), bf16),
            dma((9,)),
            dma((4,)),
            dma((4,)),
            dma((8,)),
            dma((8, 2)),
            dma((4, 4)),
            dma((4, 4)),
            dma((4,)),
            dma((4,)),
            dma((1,)),
            dma((2,)),
            dma((slots,)),
            dma((slots,)),
            dma((slots,)),
            dma((1,)),
            dma((2,)),
            dma((2, 2)),
            dma((2,)),
            dma((4, 2)),
            dma((4, 2)),
            dma((8,)),
            dma((8,)),
            dma((4,)),
            dma((4,)),
            dma((3,)),
            dma((4,)),
            dma((19,)),
            dma((3,)),
        ],
        compiler_params=pltpu.CompilerParams(
            collective_id=0, has_side_effects=True, vmem_limit_bytes=67043328
        ),
    )(
        media_counts,
        media_patches.reshape(blocks, 64, width),
        latent_rows.reshape(slots, queries, width),
        cotangent.reshape(slots, queries, width),
        query_weight,
        key_value_weight,
        output_weight,
        up_weight.reshape(4, rows_up // 4, hidden),
        down_weight,
        norm_tile,
    )
    new, media_grad, latent_grad, norms, query_grad, key_value_grad, output_grad, up_grad, down_grad = outs
    norms = lax.dynamic_slice(norms, (0, head * part), (6, part))
    return (
        new.reshape(latent_rows.shape),
        media_grad.reshape(media_patches.shape),
        latent_grad.reshape(latent_rows.shape),
        norms[0:3],
        norms[3:6],
        query_grad,
        key_value_grad,
        output_grad,
        up_grad,
        down_grad,
    )


def block_fits(mesh):
    return mesh.shape["img"] == 8 and mesh.shape["head"] == 4


def solution(mesh):
    return jax.shard_map(
        block_plan if block_fits(mesh) else gathered_plan,
        mesh=mesh,
        in_specs=(
            P(("img", "head"), None, None, None),
            P(("img", "head"), None, None, None),
            P(("img", "head")),
            P(None, ("img", "head")),
            P(None, ("img", "head")),
            P(("img", "head"), None),
            P(("img", "head"), None),
            P(("img", "head"), None),
            P("img", "head"),
            P("head", "img"),
            P(("img", "head"), None, None, None),
        ),
        out_specs=(
            P(("img", "head"), None, None, None),
            P(("img", "head"), None, None, None),
            P(("img", "head"), None, None, None),
            P(None, ("img", "head")),
            P(None, ("img", "head")),
            P(("img", "head"), None),
            P(("img", "head"), None),
            P(("img", "head"), None),
            P("img", "head"),
            P("head", "img"),
        ),
        check_vma=False,
    )
```

```python
import jax
import jax.numpy as jnp
from jax import lax
from jax.experimental import pallas as pl
from jax.experimental.pallas import tpu as pltpu
from jax.sharding import PartitionSpec as P

HEADS = 8
FF_ROWS = 20


def layer_norm(values, norm_gain, norm_shift):
    centered = values - jnp.mean(values, axis=-1, keepdims=True)
    variance = jnp.mean(centered * centered, axis=-1, keepdims=True)
    return centered * lax.rsqrt(variance + 1e-05) * norm_gain + norm_shift


def norm_backward(values, norm_gain, norm_shift, upstream):
    primal, pullback = jax.vjp(layer_norm, values, norm_gain, norm_shift)
    return pullback(upstream)


def exact_gelu(values):
    return jax.nn.gelu(values, approximate=False)


def gelu_backward(values, upstream):
    primal, pullback = jax.vjp(exact_gelu, values)
    return pullback(upstream)[0]


def contract_rows(left_side, right_side):
    return lax.dot_general(
        left_side, right_side, (((0,), (0,)), ((), ())), preferred_element_type=jnp.float32
    )


def contract_cols(left_side, right_side):
    return lax.dot_general(
        left_side, right_side, (((1,), (1,)), ((), ())), preferred_element_type=jnp.float32
    )


def gathered_plan(
    media_patches,
    latent_rows,
    media_counts,
    norm_gains,
    norm_biases,
    query_weight,
    key_value_weight,
    output_weight,
    up_weight,
    down_weight,
    cotangent,
):
    samp_local, media_slots, patches, model_width = media_patches.shape
    queries_per = latent_rows.shape[2]
    images = samp_local * media_slots
    keys_per = patches + queries_per
    rows_local = images * queries_per
    gathered = (
        lax.all_gather(query_weight, ("img", "head"), axis=0, tiled=True),
        lax.all_gather(key_value_weight, ("img", "head"), axis=0, tiled=True),
        lax.all_gather(output_weight, ("img", "head"), axis=0, tiled=True),
        lax.all_gather(norm_gains, ("img", "head"), axis=1, tiled=True),
        lax.all_gather(norm_biases, ("img", "head"), axis=1, tiled=True),
    )
    query_full, key_value_full, output_full, gains_low, biases_low = gathered
    norm_gain = gains_low.astype(jnp.float32)
    norm_shift = biases_low.astype(jnp.float32)
    inner_width = query_full.shape[1]
    head_size = inner_width // HEADS
    score_scale = head_size ** (-0.5)
    up_part, down_part = (
        lax.all_gather(up_weight, "img", axis=0, tiled=True),
        lax.all_gather(down_weight, "img", axis=1, tiled=True),
    )
    media_full = media_patches.reshape(images, patches, model_width).astype(jnp.float32)
    latent_full = latent_rows.reshape(images, queries_per, model_width).astype(jnp.float32)
    media_norm = layer_norm(media_full, norm_gain[0], norm_shift[0]).astype(jnp.bfloat16)
    latent_norm = layer_norm(latent_full, norm_gain[1], norm_shift[1]).astype(jnp.bfloat16)
    query_rows = (
        jnp.einsum("ild,de->ile", latent_norm, query_full, preferred_element_type=jnp.float32)
        * score_scale
    ).astype(jnp.bfloat16)
    key_input = jnp.concatenate([media_norm, latent_norm], axis=1)
    key_value_rows = jnp.einsum(
        "ikd,de->ike", key_input, key_value_full, preferred_element_type=jnp.float32
    ).astype(jnp.bfloat16)
    query_heads = (
        query_rows.reshape(images, queries_per, HEADS, head_size)
        .transpose(2, 0, 1, 3)
        .reshape(HEADS, images, queries_per * head_size)
    )
    key_value_heads = (
        key_value_rows.reshape(images, keys_per, 2, HEADS, head_size)
        .transpose(3, 0, 1, 2, 4)
        .reshape(HEADS, images, keys_per, 2 * head_size)
    )
    query_group, key_value_group = (
        lax.all_to_all(query_heads, "head", split_axis=0, concat_axis=1, tiled=True),
        lax.all_to_all(key_value_heads, "head", split_axis=0, concat_axis=1, tiled=True),
    )
    heads_dev = query_group.shape[0]
    group_images = query_group.shape[1]
    query_block = query_group.reshape(heads_dev, group_images, queries_per, head_size)
    key_block = key_value_group[:, :, :, :head_size]
    value_block = key_value_group[:, :, :, head_size:]
    scores = jnp.einsum(
        "hgqe,hgke->hgqk", query_block, key_block, preferred_element_type=jnp.float32
    )
    row_max = jnp.max(scores, axis=-1, keepdims=True)
    weights = jnp.exp(scores - row_max)
    totals = jnp.sum(weights, axis=-1, keepdims=True)
    log_total = row_max + jnp.log(totals)
    probabilities = (weights / totals).astype(jnp.bfloat16)
    attended = jnp.einsum(
        "hgqk,hgke->hgqe", probabilities, value_block, preferred_element_type=jnp.float32
    ).astype(jnp.bfloat16)
    attended_back = lax.all_to_all(
        attended.reshape(heads_dev, group_images, queries_per * head_size),
        "head",
        split_axis=1,
        concat_axis=0,
        tiled=True,
    )
    attended_local = (
        attended_back.reshape(HEADS, images, queries_per, head_size)
        .transpose(1, 2, 0, 3)
        .reshape(images, queries_per, inner_width)
    )
    attn_delta = jnp.einsum(
        "ile,ed->ild", attended_local, output_full, preferred_element_type=jnp.float32
    )
    mid_latent = latent_full + attn_delta
    hidden_in = (
        layer_norm(mid_latent, norm_gain[2], norm_shift[2])
        .astype(jnp.bfloat16)
        .reshape(rows_local, model_width)
    )
    slot_mask = (
        (jnp.arange(media_slots)[None, :] < media_counts[:, None])
        .astype(jnp.float32)
        .reshape(images, 1, 1)
    )
    up_full, down_full = (
        lax.all_gather(up_part, "head", axis=1, tiled=True),
        lax.all_gather(down_part, "head", axis=0, tiled=True),
    )
    pre_act = jnp.dot(hidden_in, up_full, preferred_element_type=jnp.float32)
    act_low = exact_gelu(pre_act).astype(jnp.bfloat16)
    branch_out = jnp.dot(act_low, down_full, preferred_element_type=jnp.float32)
    result = slot_mask * (mid_latent + branch_out.reshape(images, queries_per, model_width))
    new_latents = result.astype(jnp.bfloat16).reshape(latent_rows.shape)
    out_grad = slot_mask * cotangent.reshape(images, queries_per, model_width).astype(jnp.float32)
    branch_grad = out_grad.astype(jnp.bfloat16).reshape(rows_local, model_width)
    act_grad = contract_cols(branch_grad, down_full)
    pre_grad = gelu_backward(pre_act, act_grad).astype(jnp.bfloat16)
    down_grad_whole = contract_rows(act_low, branch_grad)
    up_grad_whole = contract_rows(hidden_in, pre_grad)
    hidden_grad = contract_cols(pre_grad, up_full)
    up_grad_part, down_grad_part = (
        lax.psum_scatter(
            up_grad_whole.astype(jnp.bfloat16), "head", scatter_dimension=1, tiled=True
        ).astype(jnp.float32),
        lax.psum_scatter(
            down_grad_whole.astype(jnp.bfloat16), "head", scatter_dimension=0, tiled=True
        ).astype(jnp.float32),
    )
    up_grad, down_grad = (
        lax.psum_scatter(
            up_grad_part.astype(jnp.bfloat16), "img", scatter_dimension=0, tiled=True
        ).astype(jnp.float32),
        lax.psum_scatter(
            down_grad_part.astype(jnp.bfloat16), "img", scatter_dimension=1, tiled=True
        ).astype(jnp.float32),
    )
    mid_from_norm, gain_ff, bias_ff = norm_backward(
        mid_latent,
        norm_gain[2],
        norm_shift[2],
        hidden_grad.reshape(images, queries_per, model_width),
    )
    mid_grad = out_grad + mid_from_norm
    delta_low = mid_grad.astype(jnp.bfloat16)
    output_weight_grad = jnp.einsum(
        "ile,ild->ed", attended_local, delta_low, preferred_element_type=jnp.float32
    )
    attended_grad = jnp.einsum(
        "ild,ed->ile", delta_low, output_full, preferred_element_type=jnp.float32
    ).astype(jnp.bfloat16)
    grad_heads = (
        attended_grad.reshape(images, queries_per, HEADS, head_size)
        .transpose(2, 0, 1, 3)
        .reshape(HEADS, images, queries_per * head_size)
    )
    grad_group = lax.all_to_all(
        grad_heads, "head", split_axis=0, concat_axis=1, tiled=True
    ).reshape(heads_dev, group_images, queries_per, head_size)
    scores_again = jnp.einsum(
        "hgqe,hgke->hgqk", query_block, key_block, preferred_element_type=jnp.float32
    )
    probs_again = jnp.exp(scores_again - log_total)
    probs_again_low = probs_again.astype(jnp.bfloat16)
    prob_grad = jnp.einsum(
        "hgqe,hgke->hgqk", grad_group, value_block, preferred_element_type=jnp.float32
    )
    value_grad = jnp.einsum(
        "hgqk,hgqe->hgke", probs_again_low, grad_group, preferred_element_type=jnp.float32
    )
    row_dot = jnp.sum(prob_grad * probs_again, axis=-1, keepdims=True)
    score_grad = (probs_again * (prob_grad - row_dot)).astype(jnp.bfloat16)
    query_grad_group = jnp.einsum(
        "hgqk,hgke->hgqe", score_grad, key_block, preferred_element_type=jnp.float32
    ).astype(jnp.bfloat16)
    key_grad = jnp.einsum(
        "hgqk,hgqe->hgke", score_grad, query_block, preferred_element_type=jnp.float32
    )
    key_value_grad_group = jnp.concatenate([key_grad, value_grad], axis=-1).astype(jnp.bfloat16)
    query_back, key_value_back = (
        lax.all_to_all(
            query_grad_group.reshape(heads_dev, group_images, queries_per * head_size),
            "head",
            split_axis=1,
            concat_axis=0,
            tiled=True,
        ),
        lax.all_to_all(key_value_grad_group, "head", split_axis=1, concat_axis=0, tiled=True),
    )
    query_local = (
        query_back.reshape(HEADS, images, queries_per, head_size)
        .transpose(1, 2, 0, 3)
        .reshape(images, queries_per, inner_width)
    )
    key_value_local = (
        key_value_back.reshape(HEADS, images, keys_per, 2, head_size)
        .transpose(1, 2, 3, 0, 4)
        .reshape(images, keys_per, 2 * inner_width)
    )
    query_weight_grad = (
        jnp.einsum("ild,ile->de", latent_norm, query_local, preferred_element_type=jnp.float32)
        * score_scale
    )
    key_value_weight_grad = jnp.einsum(
        "ikd,ike->de", key_input, key_value_local, preferred_element_type=jnp.float32
    )
    key_input_grad = jnp.einsum(
        "ike,de->ikd", key_value_local, key_value_full, preferred_element_type=jnp.float32
    )
    latent_norm_grad = (
        jnp.einsum("ile,de->ild", query_local, query_full, preferred_element_type=jnp.float32)
        * score_scale
        + key_input_grad[:, patches:]
    )
    media_grad_full, gain_media, bias_media = norm_backward(
        media_full, norm_gain[0], norm_shift[0], key_input_grad[:, :patches]
    )
    latent_from_norm, gain_latent, bias_latent = norm_backward(
        latent_full, norm_gain[1], norm_shift[1], latent_norm_grad
    )
    latent_grad_full = mid_grad + latent_from_norm
    gain_terms = jnp.stack([gain_media, gain_latent, gain_ff])
    bias_terms = jnp.stack([bias_media, bias_latent, bias_ff])
    summed = (
        lax.psum_scatter(query_weight_grad, ("img", "head"), scatter_dimension=0, tiled=True),
        lax.psum_scatter(key_value_weight_grad, ("img", "head"), scatter_dimension=0, tiled=True),
        lax.psum_scatter(output_weight_grad, ("img", "head"), scatter_dimension=0, tiled=True),
        lax.psum_scatter(gain_terms, ("img", "head"), scatter_dimension=1, tiled=True),
        lax.psum_scatter(bias_terms, ("img", "head"), scatter_dimension=1, tiled=True),
    )
    media_grad = media_grad_full.astype(jnp.bfloat16).reshape(media_patches.shape)
    latent_grad = latent_grad_full.astype(jnp.bfloat16).reshape(latent_rows.shape)
    return (
        new_latents,
        media_grad,
        latent_grad,
        summed[3],
        summed[4],
        summed[0],
        summed[1],
        summed[2],
        up_grad,
        down_grad,
    )


def tpose(values):
    return jnp.transpose(values, (1, 0))


def dot_nn(left_side, right_side):
    return jnp.dot(left_side, right_side, preferred_element_type=jnp.float32)


def block_kernel(
    counts,
    media_in,
    latent_in,
    cot_in,
    query_in,
    key_value_in,
    output_in,
    up_in,
    down_in,
    norm_in,
    new_out,
    media_out,
    latent_out,
    norm_out,
    query_out,
    key_value_out,
    output_out,
    up_out,
    down_out,
    slab,
    query_full,
    wide,
    hid,
    cotr,
    turned,
    media_v,
    media_n,
    latent_v,
    latent_n,
    media_t,
    latent_t,
    kv_media,
    kv_latent,
    query_v,
    att_v,
    att_t,
    mid_v,
    pair,
    grads,
    xrecv,
    zrecv,
    hsend,
    hrecv,
    hysend,
    hyrecv,
    hown,
    delta_v,
    attg_v,
    qgrad_v,
    normg,
    normv,
    gacc,
    gsend,
    gyr,
    gzr,
    gzr_v,
    loc,
    at_z,
    at_x,
    at_y,
    at_c,
    ff_z,
    ff_x,
    nb_z,
    nb_x,
    nb_y,
    nb_c,
    hd_y,
    hd_c,
    hd_f,
    bg_y,
    bg_c,
    hp_c,
    hp_y,
    rf_x,
    rf_z,
    ra_c,
    ra_y,
    ra_x,
    ra_z,
    gr_c,
    gr_z,
    sent,
    outs,
):
    n_z, n_x, n_head = 4, 2, 4
    img = lax.axis_index("img")
    head = lax.axis_index("head")
    z = img // n_x
    x = img % n_x
    y = head // 2
    c = head % 2
    xp, yp, cp = 1 - x, 1 - y, 1 - c
    xdev = (z * n_x + xp, head)
    ydev = (img, yp * 2 + c)
    cdev = (img, y * 2 + cp)
    near = (1, 3, 2)

    def zat(k):
        return (z + k) % n_z

    def zdev(zz):
        return (zz * n_x + x, head)

    width = media_v.shape[2]
    slots = latent_v.shape[0]
    queries = latent_v.shape[1]
    hidden = up_in.shape[2]
    inner = query_full.shape[3]
    f32 = jnp.float32
    bf16 = jnp.bfloat16
    scale = (inner // HEADS) ** (-0.5)

    def rcopy(src, dst, sem_s, sem_r, dev):
        return pltpu.make_async_remote_copy(
            src_ref=src,
            dst_ref=dst,
            send_sem=sem_s,
            recv_sem=sem_r,
            device_id=dev,
            device_id_type=pl.DeviceIdType.MESH,
        )

    def send(src, dst, sem_s, sem_r, dev):
        rcopy(src, dst, sem_s, sem_r, dev).start()

    def arrived(ref, sem):
        pltpu.make_async_copy(ref, ref, sem).wait()

    unit = img * n_head + head
    local = [
        pltpu.make_async_copy(key_value_in, slab.at[unit, 0:32], loc.at[0]),
        pltpu.make_async_copy(output_in, slab.at[unit, 32:48], loc.at[1]),
        pltpu.make_async_copy(query_in.at[0:16], slab.at[unit, 48:64, 0:inner], loc.at[2]),
        pltpu.make_async_copy(query_in.at[16:32], slab.at[unit, 48:64, inner:width], loc.at[3]),
        pltpu.make_async_copy(norm_in, normg.at[head, :, pl.ds(pl.multiple_of(img * 128, 128), 128)], loc.at[4]),
        pltpu.make_async_copy(up_in, wide.at[pl.ds(img * 4, 4), :, 0:hidden], loc.at[5]),
        pltpu.make_async_copy(cot_in, pair.at[0:slots], loc.at[6]),
        pltpu.make_async_copy(latent_in, latent_v, loc.at[7]),
        pltpu.make_async_copy(media_in, media_v, loc.at[8]),
    ]
    for copy in local:
        copy.start()

    barrier = pltpu.get_barrier_semaphore()
    peers = [zdev(zat(k)) for k in near] + [xdev, ydev, cdev]
    for dev in peers:
        pl.semaphore_signal(barrier, inc=1, device_id=dev, device_id_type=pl.DeviceIdType.MESH)
    pl.semaphore_wait(barrier, len(peers))

    def lanes(ii):
        return pl.ds(pl.multiple_of(ii * 128, 128), 128)

    local[4].wait()
    for k in near:
        send(norm_in, normg.at[head, :, lanes(img)], sent.at[0], nb_z.at[z], zdev(zat(k)))
    for copy in local[0:4]:
        copy.wait()

    def put_slab(uu, sem, dev):
        send(slab.at[uu], slab.at[uu], sent.at[1], sem, dev)

    for k in near:
        put_slab(unit, at_z.at[z], zdev(zat(k)))
    put_slab(unit, at_x.at[z], xdev)
    put_slab(unit, at_y.at[img], ydev)
    put_slab(unit, at_c.at[img, y], cdev)

    local[5].wait()
    down = down_in[...]
    for j in range(hidden // 128):
        wide[pl.ds(img * 4, 4), :, hidden + j * 128 : hidden + (j + 1) * 128] = tpose(
            down[j * 128 : (j + 1) * 128, :]
        ).reshape(4, 32, 128)

    local[6].wait()
    filled = counts[0]
    for m in range(slots):
        keep = jnp.clip(filled - m, 0, 1).astype(f32)
        cotr[head * slots + m] = (pair[m].astype(f32) * keep).astype(bf16)

    def nb_wait(kind, idx, ref):
        arrived(ref, kind.at[idx])

    for k in near:
        zz = zat(k)
        arrived(normg.at[head, :, lanes(zz * n_x + x)], nb_z.at[zz])
    for k in (0,) + near:
        zz = zat(k)
        ii = zz * n_x + x
        send(normg.at[head, :, lanes(ii)], normg.at[head, :, lanes(ii)], sent.at[2], nb_x.at[zz], xdev)

    def at_forward_z(k):
        zz = zat(k)
        uu = (zz * n_x + x) * n_head + head
        arrived(slab.at[uu], at_z.at[zz])
        put_slab(uu, at_x.at[zz], xdev)
        put_slab(uu, at_y.at[zz * n_x + x], ydev)
        put_slab(uu, at_c.at[zz * n_x + x, y], cdev)

    def at_forward_x(k):
        zz = zat(k)
        ii = zz * n_x + xp
        uu = ii * n_head + head
        arrived(slab.at[uu], at_x.at[zz])
        put_slab(uu, at_y.at[ii], ydev)
        put_slab(uu, at_c.at[ii, y], cdev)

    def at_forward_y(ii):
        uu = ii * n_head + yp * 2 + c
        arrived(slab.at[uu], at_y.at[ii])
        put_slab(uu, at_c.at[ii, yp], cdev)

    at_forward_z(1)
    at_forward_x(0)
    at_forward_z(3)
    for k in (0,) + near:
        zz = zat(k)
        arrived(normg.at[head, :, lanes(zz * n_x + xp)], nb_x.at[zz])
    send(normg.at[head], normg.at[head], sent.at[3], nb_y.at[0], ydev)
    send(normg.at[head], normg.at[head], sent.at[4], nb_c.at[y], cdev)
    at_forward_z(2)

    def ff_unit(ii, q):
        return wide.at[ii * 4 + q]

    for q in range(4):
        for k in near:
            send(ff_unit(img, q), ff_unit(img, q), sent.at[5], ff_z.at[z, q], zdev(zat(k)))
    at_forward_x(1)
    arrived(normg.at[yp * 2 + c], nb_y.at[0])
    send(normg.at[yp * 2 + c], normg.at[yp * 2 + c], sent.at[4], nb_c.at[yp], cdev)
    at_forward_x(3)
    for q in range(4):
        send(ff_unit(img, q), ff_unit(img, q), sent.at[6], ff_x.at[z, q], xdev)
    at_forward_x(2)
    own_cot = cotr.at[pl.ds(head * slots, slots)]
    send(own_cot, own_cot, sent.at[7], bg_y.at[0], ydev)
    send(own_cot, own_cot, sent.at[7], bg_c.at[y], cdev)

    arrived(normg.at[y * 2 + cp], nb_c.at[y])
    arrived(normg.at[yp * 2 + cp], nb_c.at[yp])
    normv[...] = normg[0] + normg[1] + normg[2] + normg[3]

    def gain(j):
        return normv[j : j + 1, :]

    def shift(j):
        return normv[3 + j : 4 + j, :]

    def statistics(values):
        centered = values - jnp.mean(values, axis=-1, keepdims=True)
        inverse = lax.rsqrt(jnp.mean(centered * centered, axis=-1, keepdims=True) + 1e-05)
        return centered * inverse, inverse

    def norm_rows(values, j):
        return (statistics(values)[0] * gain(j) + shift(j)).astype(bf16)

    half = queries // 2

    def norm_latent(m, carry):
        for r in range(2):
            rows = slice(r * half, (r + 1) * half)
            latent_n[m, rows, :] = norm_rows(latent_v[m, rows, :].astype(f32), 1)
        return carry

    def norm_media(m, carry):
        for r in range(2):
            rows = slice(r * half, (r + 1) * half)
            media_n[m, rows, :] = norm_rows(media_v[m, rows, :].astype(f32), 0)
        return carry

    local[7].wait()
    lax.fori_loop(0, slots, norm_latent, 0)
    at_forward_y(img)
    at_forward_y(zat(1) * n_x + x)
    local[8].wait()
    blocks = media_v.shape[0]
    step = blocks // 4
    order = [z * n_x + xp, zat(3) * n_x + x, zat(2) * n_x + x, zat(1) * n_x + xp, zat(3) * n_x + xp, zat(2) * n_x + xp]
    for r in range(4):
        lax.fori_loop(r * step, (r + 1) * step, norm_media, 0)
        at_forward_y(order[r])

    def turn_media(r, carry):
        block = media_n[pl.ds(r * 2, 2)].reshape(128, width)
        for d in range(width // 128):
            media_t[d * 128 : (d + 1) * 128, pl.ds(pl.multiple_of(r * 128, 128), 128)] = tpose(
                block[:, d * 128 : (d + 1) * 128]
            )
        return carry

    rows_latent = slots * queries

    def turn_latent(source, target, columns):
        whole = source[...].reshape(rows_latent, columns)
        for r in range(0, rows_latent, 128):
            stop = min(r + 128, rows_latent)
            for d in range(columns // 128):
                target[d * 128 : (d + 1) * 128, r:stop] = tpose(
                    whole[r:stop, d * 128 : (d + 1) * 128]
                )

    turn_latent(latent_n, latent_t, width)
    at_forward_y(order[4])
    lax.fori_loop(0, blocks * queries // 128, turn_media, 0)
    at_forward_y(order[5])

    def ff_forward(e):
        q = e // 3
        step_k = e % 3
        kk = step_k + 1
        zz = (z + kk) % n_z
        piece = ff_unit(zz * n_x + x, q)
        arrived(piece, ff_z.at[zz, q])
        send(piece, piece, sent.at[6], ff_x.at[zz, q], xdev)

    for e in range(3):
        ff_forward(e)
    for ii in range(8):
        for yy in range(2):
            arrived(slab.at[ii * n_head + yy * 2 + cp], at_c.at[ii, yy])
    ff_forward(3)

    query_full[:, 0] = slab[:, 48:64, 0:inner]
    query_full[:, 1] = slab[:, 48:64, inner:width]

    def query_tile(cols):
        return query_full[:, :, :, cols].reshape(width, -1)

    def kv_tile(cols):
        return slab[:, 0:32, cols].reshape(width, -1)

    def out_tile(cols):
        return slab[:, 32:48, cols].reshape(inner, -1)

    latent_rows_n = latent_n[...].reshape(rows_latent, width)

    def tile(t):
        return pl.ds(pl.multiple_of(t * 256, 256), 256)

    query_v[...] = (
        (dot_nn(latent_rows_n, query_full[...].reshape(width, inner)) * scale)
        .astype(bf16)
        .reshape(slots, queries, inner)
    )
    groups = kv_media.shape[0]
    media_rows_n = media_n[...].reshape(groups * 256, width)

    def kv_step(t, carry):
        weight = kv_tile(tile(t))
        kv_latent[:, :, tile(t)] = dot_nn(latent_rows_n, weight).astype(bf16).reshape(slots, queries, 256)
        kv_media[:, :, tile(t)] = dot_nn(media_rows_n, weight).astype(bf16).reshape(groups, 256, 256)
        return carry

    lax.fori_loop(0, width // 256, kv_step, 0)
    ff_forward(4)

    def lane_mask(hh, dtype):
        lane = lax.broadcasted_iota(jnp.int32, (1, 256), 1)
        return (lane // queries == hh).astype(f32).astype(dtype)

    def spread(rows):
        return jnp.concatenate([rows * lane_mask(hh, bf16) for hh in range(4)], axis=0)

    def fold(rows):
        total = rows[0:queries] * lane_mask(0, f32)
        for hh in range(1, 4):
            total = total + rows[hh * queries : (hh + 1) * queries] * lane_mask(hh, f32)
        return total

    def probabilities(m, g):
        q_rows = spread(query_v[m, :, tile(g)])
        k_media = kv_media[m, :, tile(g)]
        k_latent = kv_latent[m, :, tile(g)]
        s_media = contract_cols(q_rows, k_media)
        s_latent = contract_cols(q_rows, k_latent)
        top = jnp.maximum(
            jnp.max(s_media, axis=-1, keepdims=True), jnp.max(s_latent, axis=-1, keepdims=True)
        )
        e_media = jnp.exp(s_media - top)
        e_latent = jnp.exp(s_latent - top)
        total = jnp.sum(e_media, axis=-1, keepdims=True) + jnp.sum(e_latent, axis=-1, keepdims=True)
        inverse = 1.0 / total
        return q_rows, k_media, k_latent, e_media * inverse, e_latent * inverse

    def attend(m, g):
        p_media, p_latent = probabilities(m, g)[3:]
        v_media = kv_media[m, :, tile(g + 2)]
        v_latent = kv_latent[m, :, tile(g + 2)]
        rows = dot_nn(p_media.astype(bf16), v_media) + dot_nn(p_latent.astype(bf16), v_latent)
        att_v[m, :, tile(g)] = fold(rows).astype(bf16)

    def forward_image(m, carry):
        attend(m, 0)
        attend(m, 1)
        mid_v[m] = latent_v[m].astype(f32) + dot_nn(att_v[m], out_tile(slice(0, width)))
        for r in range(2):
            rows = slice(r * half, (r + 1) * half)
            hid[head * slots + m, rows, :] = norm_rows(mid_v[m, rows, :], 2)
        piece = hid.at[head * slots + m]
        send(piece, piece, sent.at[8], hd_y.at[m], ydev)
        send(piece, piece, sent.at[8], hd_c.at[m], cdev)
        ff_forward(m + 5)
        return carry

    lax.fori_loop(0, slots, forward_image, 0)

    other = yp * 2 + c
    cot_other = cotr.at[pl.ds(other * slots, slots)]
    arrived(cot_other, bg_y.at[0])
    send(cot_other, cot_other, sent.at[7], bg_c.at[yp], cdev)
    turn_latent(att_v, att_t, inner)
    ff_forward(10)
    for yy in (y, yp):
        arrived(cotr.at[pl.ds((yy * 2 + cp) * slots, slots)], bg_c.at[yy])

    all_rows = n_head * slots * queries

    def turn_rows(source, slot):
        def body(r, carry):
            block = source[pl.ds(r * 2, 2)].reshape(128, width)
            for d in range(width // 128):
                turned[slot, d * 128 : (d + 1) * 128, pl.ds(pl.multiple_of(r * 128, 128), 128)] = tpose(
                    block[:, d * 128 : (d + 1) * 128]
                )
            return carry

        lax.fori_loop(0, all_rows // 128, body, 0)

    turn_rows(cotr, 1)
    ff_forward(11)

    def hid_forward(m, carry):
        piece = hid.at[other * slots + m]
        arrived(piece, hd_y.at[m])
        send(piece, piece, sent.at[8], hd_f.at[m], cdev)
        return carry

    lax.fori_loop(0, slots, hid_forward, 0)

    def hid_arrived(m, carry):
        arrived(hid.at[(y * 2 + cp) * slots + m], hd_c.at[m])
        arrived(hid.at[(yp * 2 + cp) * slots + m], hd_f.at[m])
        return carry

    lax.fori_loop(0, slots, hid_arrived, 0)
    turn_rows(hid, 0)

    def ff_arrived(e, carry):
        zz = e // 4
        q = e % 4
        arrived(ff_unit(zz * n_x + xp, q), ff_x.at[zz, q])
        return carry

    lax.fori_loop(0, 16, ff_arrived, 0)

    act_at = 4 * slots

    def wide_tile(start):
        return wide[:, :, pl.ds(pl.multiple_of(start, 256), 256)].reshape(width, 256)

    def ff_step(t, carry):
        up = wide_tile(t * 256)
        dn = wide_tile(hidden + t * 256)

        def over_rows(r, carry2):
            rows = pl.ds(r * FF_ROWS, FF_ROWS)
            pre = dot_nn(hid[rows].reshape(FF_ROWS * 64, width), up)
            grad = dot_nn(cotr[rows].reshape(FF_ROWS * 64, width), dn)
            below = 0.5 * (1.0 + lax.erf(pre * 0.7071067811865476))
            slope = below + pre * (jnp.exp(-0.5 * pre * pre) * 0.3989422804014327)
            pair[rows, :, tile(t)] = (grad * slope).astype(bf16).reshape(FF_ROWS, 64, 256)
            pair[pl.ds(act_at + r * FF_ROWS, FF_ROWS), :, tile(t)] = (
                (pre * below).astype(bf16).reshape(FF_ROWS, 64, 256)
            )
            return carry2

        return lax.fori_loop(0, act_at // FF_ROWS, over_rows, carry)

    lax.fori_loop(0, hidden // 256, ff_step, 0)

    def wide_rows(part, t):
        return wide[pl.ds(t * 16, 16), :, part * hidden : (part + 1) * hidden].reshape(512, hidden)

    def broad(t):
        return pl.ds(pl.multiple_of(t * 512, 512), 512)

    def head_sum(part):
        def rows_of(hh):
            return pair[pl.ds(part * act_at + hh * slots, slots)].reshape(rows_latent, hidden)

        for slot, hh in enumerate((yp * 2 + cp, y * 2 + cp)):
            left = rows_of(hh)

            def to_core(t, carry, left=left, slot=slot):
                value = contract_cols(left, wide_rows(part, t))
                hsend[part, slot, :, :, broad(t)] = value.astype(bf16).reshape(slots, queries, 512)
                return carry

            lax.fori_loop(0, width // 512, to_core, 0)
            send(hsend.at[part, slot], hrecv.at[part, slot], sent.at[9], hp_c.at[part, slot], cdev)
        left_y = rows_of(yp * 2 + c)
        arrived(hrecv.at[part, 0], hp_c.at[part, 0])

        def to_y(t, carry):
            value = contract_cols(left_y, wide_rows(part, t)).reshape(slots, queries, 512)
            hysend[part, :, :, broad(t)] = (value + hrecv[part, 0, :, :, broad(t)].astype(f32)).astype(bf16)
            return carry

        lax.fori_loop(0, width // 512, to_y, 0)
        send(hysend.at[part], hyrecv.at[part], sent.at[10], hp_y.at[part], ydev)
        left_own = rows_of(head)
        arrived(hrecv.at[part, 1], hp_c.at[part, 1])

        def to_own(t, carry):
            value = contract_cols(left_own, wide_rows(part, t)).reshape(slots, queries, 512)
            hown[part, :, :, broad(t)] = value + hrecv[part, 1, :, :, broad(t)].astype(f32)
            return carry

        lax.fori_loop(0, width // 512, to_own, 0)

    arrived(hid.at[0 : 3 * slots], sent.at[8])
    head_sum(0)

    def grad_unit(u, carry):
        zz = (z + 1 + u // 2) % n_z
        part = u % 2
        left = turned[part, pl.ds(pl.multiple_of(zz * 256, 256), 256), :]

        right = pair[pl.ds(part * act_at, act_at)].reshape(all_rows, hidden)
        value = dot_nn(left, right).astype(bf16).reshape(2, 128, hidden)
        grads[zz, 0, part] = value[0]
        grads[zz, 1, part] = value[1]
        send(grads.at[zz, xp, part], xrecv.at[zz, part], sent.at[11], rf_x.at[zz, part], xdev)
        return carry

    def sum_unit(u):
        zz = (z + 1 + u // 2) % n_z
        part = u % 2
        arrived(xrecv.at[zz, part], rf_x.at[zz, part])

        def over(r, carry2):
            rows = pl.ds(pl.multiple_of(r * 16, 16), 16)
            grads[zz, x, part, rows, :] = (
                grads[zz, x, part, rows, :].astype(f32) + xrecv[zz, part, rows, :].astype(f32)
            ).astype(bf16)
            return carry2

        lax.fori_loop(0, 8, over, 0)
        send(grads.at[zz, x, part], zrecv.at[z, part], sent.at[12], rf_z.at[z, part], zdev(zz))

    def grad_and_sum(u, carry):
        grad_unit(u, carry)
        sum_unit(u - 4)
        return carry

    lax.fori_loop(0, 4, grad_unit, 0)
    lax.fori_loop(4, 8, grad_and_sum, 0)
    head_sum(1)
    sum_unit(4)

    gacc[...] = jnp.zeros_like(gacc)

    def tally(j, upper, xhat):
        gacc[j] += jnp.sum((upper * xhat).reshape(-1, 8, width), axis=0)
        gacc[3 + j] += jnp.sum(upper.reshape(-1, 8, width), axis=0)

    def norm_back(values, j, upper):
        xhat, inverse = statistics(values)
        tally(j, upper, xhat)
        g = upper * gain(j)
        return inverse * (
            g - jnp.mean(g, axis=-1, keepdims=True) - xhat * jnp.mean(g * xhat, axis=-1, keepdims=True)
        )

    arrived(hyrecv.at[0], hp_y.at[0])

    def mid_back(m, carry):
        upper = hown[0, m] + hyrecv[0, m].astype(f32)
        back = norm_back(mid_v[m], 2, upper)
        total = cotr[head * slots + m].astype(f32) + back
        hown[0, m] = total
        delta_v[m] = total.astype(bf16)
        return carry

    lax.fori_loop(0, slots, mid_back, 0)
    delta_rows = delta_v[...].reshape(rows_latent, width)

    attg_v[...] = (
        contract_cols(delta_rows, out_tile(slice(0, width))).astype(bf16).reshape(slots, queries, inner)
    )

    gslab = pair

    def gunit(ii, hh_y, hh_c):
        return ii * 4 + hh_c * 2 + hh_y

    def out_grad_step(t, carry):
        right = delta_v[:, :, broad(t)].reshape(rows_latent, 512)
        value = dot_nn(att_t[...], right).astype(bf16)
        for ii in range(8):
            for hh in range(4):
                at = (ii * 4 + hh) * 16
                gslab[gunit(ii, hh // 2, hh % 2), 32:48, broad(t)] = value[at : at + 16]
        return carry

    lax.fori_loop(0, width // 512, out_grad_step, 0)
    sum_unit(5)

    def back_pair(m, g):
        q_rows, k_media, k_latent, p_media, p_latent = probabilities(m, g)
        v_media = kv_media[m, :, tile(g + 2)]
        v_latent = kv_latent[m, :, tile(g + 2)]
        up_rows = spread(attg_v[m, :, tile(g)])
        g_media = contract_cols(up_rows, v_media)
        g_latent = contract_cols(up_rows, v_latent)
        dotted = jnp.sum(g_media * p_media, axis=-1, keepdims=True) + jnp.sum(
            g_latent * p_latent, axis=-1, keepdims=True
        )
        d_media = (p_media * (g_media - dotted)).astype(bf16)
        d_latent = (p_latent * (g_latent - dotted)).astype(bf16)
        qgrad_v[m, :, tile(g)] = fold(dot_nn(d_media, k_media) + dot_nn(d_latent, k_latent)).astype(bf16)
        kv_media[m, :, tile(g)] = contract_rows(d_media, q_rows).astype(bf16)
        kv_latent[m, :, tile(g)] = contract_rows(d_latent, q_rows).astype(bf16)
        kv_media[m, :, tile(g + 2)] = contract_rows(p_media.astype(bf16), up_rows).astype(bf16)
        kv_latent[m, :, tile(g + 2)] = contract_rows(p_latent.astype(bf16), up_rows).astype(bf16)

    def back_image(m, carry):
        back_pair(m, 0)
        back_pair(m, 1)
        return carry

    lax.fori_loop(0, slots, back_image, 0)

    gcr = hid
    gyr_v = media_n

    def kv_grad_chunk(zz):
        rows = pl.ds(pl.multiple_of(zz * 256, 256), 256)
        left_media = media_t[rows, :]
        left_latent = latent_t[rows, :]

        value = dot_nn(left_media, kv_media[...].reshape(groups * 256, width)) + dot_nn(
            left_latent, kv_latent[...].reshape(rows_latent, width)
        )
        value = value.astype(bf16)
        value_q = dot_nn(left_latent, qgrad_v[...].reshape(rows_latent, inner)) * scale
        value_q = value_q.astype(bf16)
        for xx in range(2):
            for hh in range(4):
                at = (xx * 4 + hh) * 32
                uu = gunit(zz * n_x + xx, hh // 2, hh % 2)
                gslab[uu, 0:32, :] = value[at : at + 32]
                gslab[uu, 48:64, 0:inner] = value_q[at : at + 16]
                gslab[uu, 48:64, inner:width] = value_q[at + 16 : at + 32]
        for xx in range(2):
            ii = zz * n_x + xx
            send(
                gslab.at[pl.ds(ii * 4 + cp * 2, 2)],
                gcr.at[pl.ds(ii * 2, 2)],
                sent.at[13],
                ra_c.at[ii],
                cdev,
            )

    def stage_y(zz):
        for xx in range(2):
            ii = zz * n_x + xx
            arrived(gcr.at[pl.ds(ii * 2, 2)], ra_c.at[ii])
            uu = gunit(ii, yp, c)
            gslab[uu] = (gslab[uu].astype(f32) + gcr[ii * 2 + yp].astype(f32)).astype(bf16)
            send(gslab.at[uu], gyr_v.at[ii], sent.at[14], ra_y.at[ii], ydev)

    def upto_y(ii):
        return (
            gslab[gunit(ii, y, c)].astype(f32) + gcr[ii * 2 + y].astype(f32) + gyr_v[ii].astype(f32)
        )

    def stage_x(zz):
        ii = zz * n_x + xp
        arrived(gyr_v.at[ii], ra_y.at[ii])
        uu = gunit(ii, y, c)
        gslab[uu] = upto_y(ii).astype(bf16)
        send(gslab.at[uu], gyr_v.at[8 + zz], sent.at[15], ra_x.at[zz], xdev)

    def stage_z(zz, last):
        ii = zz * n_x + x
        arrived(gyr_v.at[ii], ra_y.at[ii])
        arrived(gyr_v.at[8 + zz], ra_x.at[zz])
        if last:
            return upto_y(ii) + gyr_v[8 + zz].astype(f32)
        uu = gunit(ii, y, c)
        gslab[uu] = (upto_y(ii) + gyr_v[8 + zz].astype(f32)).astype(bf16)
        send(gslab.at[uu], gzr_v.at[z], sent.at[16], ra_z.at[z], zdev(zz))
        return None

    chunk = [zat(1), zat(3), zat(2), z]
    kv_grad_chunk(chunk[0])
    kv_grad_chunk(chunk[1])
    stage_y(chunk[0])
    kv_grad_chunk(chunk[2])
    stage_y(chunk[1])
    kv_grad_chunk(chunk[3])
    stage_y(chunk[2])

    arrived(hyrecv.at[1], hp_y.at[1])
    new_v = delta_v

    for m in range(slots):
        keep = jnp.clip(filled - m, 0, 1).astype(f32)
        for r in range(2):
            rows = slice(r * half, (r + 1) * half)
            branch = hown[1, m, rows, :] + hyrecv[1, m, rows, :].astype(f32)
            new_v[m, rows, :] = ((mid_v[m, rows, :] + branch) * keep).astype(bf16)
    new_copy = pltpu.make_async_copy(new_v, new_out, outs.at[0])
    new_copy.start()
    stage_y(chunk[3])

    def media_back(m, carry):
        hown[1, 0:4] = contract_cols(kv_media[m], kv_tile(slice(0, width))).reshape(4, 64, width)

        def over_rows(r, carry2):
            block = m * 4 + r
            back = norm_back(media_v[block].astype(f32), 0, hown[1, r])
            media_v[block] = back.astype(bf16)
            return carry2

        lax.fori_loop(0, 4, over_rows, 0)
        pltpu.make_async_copy(media_v.at[pl.ds(m * 4, 4)], media_out.at[pl.ds(m * 4, 4)], outs.at[1]).start()
        return carry

    def latent_back_tiles(t, carry):
        weight = slab[pl.ds(t * 16, 16), 0:32, :].reshape(512, width)
        query_weight = query_full[pl.ds(t * 16, 16)].reshape(512, inner)
        hown[1, :, :, broad(t)] = (
            contract_cols(kv_latent[...].reshape(rows_latent, width), weight)
            + contract_cols(qgrad_v[...].reshape(rows_latent, inner), query_weight) * scale
        ).reshape(slots, queries, 512)
        return carry

    def latent_back(m, carry):
        back = norm_back(latent_v[m].astype(f32), 1, hown[1, m])
        latent_v[m] = (hown[0, m] + back).astype(bf16)
        return carry

    lax.fori_loop(0, width // 512, latent_back_tiles, 0)
    lax.fori_loop(0, slots, latent_back, 0)
    latent_copy = pltpu.make_async_copy(latent_v, latent_out, outs.at[2])
    latent_copy.start()
    lax.fori_loop(0, 2, media_back, 0)
    stage_x(chunk[0])
    stage_x(chunk[1])
    lax.fori_loop(2, 4, media_back, 0)
    stage_x(chunk[2])
    stage_z(chunk[0], False)
    stage_z(chunk[1], False)
    lax.fori_loop(4, 5, media_back, 0)
    stage_x(chunk[3])
    stage_z(chunk[2], False)

    for j in range(6):
        gsend[0, j : j + 1, :] = jnp.sum(gacc[j], axis=0, keepdims=True)
    gsend[0, 6:8, :] = jnp.zeros((2, width), f32)
    send(gsend.at[0], gyr.at[0], sent.at[17], gr_c.at[0], cdev)
    arrived(gyr.at[0], gr_c.at[0])
    gsend[1] = gsend[0] + gyr[0]
    send(gsend.at[1], gyr.at[1], sent.at[17], gr_c.at[1], ydev)
    arrived(gyr.at[1], gr_c.at[1])
    gsend[2] = gsend[1] + gyr[1]
    send(gsend.at[2], gyr.at[2], sent.at[17], gr_c.at[2], xdev)
    arrived(gyr.at[2], gr_c.at[2])
    gsend[3] = gsend[2] + gyr[2]
    for k in near:
        zz = zat(k)
        send(gsend.at[3, :, lanes(zz * n_x + x)], gzr.at[z], sent.at[18], gr_z.at[z], zdev(zz))
    total = gsend[3, :, lanes(img)]
    for k in near:
        zz = zat(k)
        arrived(gzr.at[zz], gr_z.at[zz])
        total = total + gzr[zz]
    norm_out[...] = total

    for part in range(2):
        arrived(xrecv.at[z, part], rf_x.at[z, part])
        for k in near:
            arrived(zrecv.at[zat(k), part], rf_z.at[zat(k), part])

    def up_last(r, carry):
        rows = pl.ds(pl.multiple_of(r * 16, 16), 16)
        value = grads[z, x, 0, rows, :].astype(f32) + xrecv[z, 0, rows, :].astype(f32)
        for k in near:
            value = value + zrecv[zat(k), 0, rows, :].astype(f32)
        up_out[rows, :] = value
        return carry

    lax.fori_loop(0, 8, up_last, 0)

    def down_last(j, carry):
        cols = pl.ds(pl.multiple_of(j * 128, 128), 128)
        value = grads[z, x, 1, :, cols].astype(f32) + xrecv[z, 1, :, cols].astype(f32)
        for k in near:
            value = value + zrecv[zat(k), 1, :, cols].astype(f32)
        down_out[cols, :] = tpose(value)
        return carry

    lax.fori_loop(0, hidden // 128, down_last, 0)

    final = stage_z(chunk[3], True)
    for k in near:
        zz = zat(k)
        arrived(gzr_v.at[zz], ra_z.at[zz])
        final = final + gzr_v[zz].astype(f32)
    key_value_out[...] = final[0:32]
    output_out[...] = final[32:48]
    query_out[0:16, :] = final[48:64, 0:inner]
    query_out[16:32, :] = final[48:64, inner:width]

    new_copy.wait()
    latent_copy.wait()
    arrived(media_v, outs.at[1])
    arrived(normg.at[0, :, 0:384], sent.at[0])
    arrived(slab.at[0:31], sent.at[1])
    arrived(normg.at[0, :, 0:512], sent.at[2])
    arrived(normg.at[0], sent.at[3])
    arrived(normg.at[0:2], sent.at[4])
    arrived(wide.at[0:12], sent.at[5])
    arrived(wide.at[0:16], sent.at[6])
    arrived(cotr.at[0 : 3 * slots], sent.at[7])
    arrived(hsend, sent.at[9])
    arrived(hysend, sent.at[10])
    arrived(xrecv, sent.at[11])
    arrived(zrecv.at[0:3], sent.at[12])
    arrived(gcr.at[0:16], sent.at[13])
    arrived(gyr_v.at[0:8], sent.at[14])
    arrived(gyr_v.at[0:4], sent.at[15])
    arrived(gyr_v.at[0:3], sent.at[16])
    arrived(gyr, sent.at[17])
    arrived(gzr.at[0:3], sent.at[18])


def block_plan(
    media_patches,
    latent_rows,
    media_counts,
    norm_gains,
    norm_biases,
    query_weight,
    key_value_weight,
    output_weight,
    up_weight,
    down_weight,
    cotangent,
):
    slots, patches, width = media_patches.shape[1:]
    queries = latent_rows.shape[2]
    inner = query_weight.shape[1]
    hidden = up_weight.shape[1]
    rows_up = up_weight.shape[0]
    part = norm_gains.shape[1]
    head = lax.axis_index("head")
    norm_rows = jnp.concatenate([norm_gains, norm_biases], axis=0).astype(jnp.float32)
    norm_tile = lax.dynamic_update_slice(
        jnp.zeros((8, 128), jnp.float32), norm_rows, (0, head * part)
    )
    blocks = slots * patches // 64
    bf16, f32 = jnp.bfloat16, jnp.float32
    shape = jax.ShapeDtypeStruct
    hbm = pl.BlockSpec(memory_space=pl.ANY)
    vmem = pl.BlockSpec(memory_space=pltpu.VMEM)
    smem = pl.BlockSpec(memory_space=pltpu.SMEM)
    dma = pltpu.SemaphoreType.DMA
    all_rows = 4 * slots * queries
    rows_latent = slots * queries
    outs = pl.pallas_call(
        block_kernel,
        out_shape=(
            shape((slots, queries, width), bf16),
            shape((blocks, 64, width), bf16),
            shape((slots, queries, width), bf16),
            shape((8, 128), f32),
            shape(query_weight.shape, f32),
            shape(key_value_weight.shape, f32),
            shape(output_weight.shape, f32),
            shape(up_weight.shape, f32),
            shape(down_weight.shape, f32),
        ),
        in_specs=[smem] + [hbm] * 7 + [vmem, hbm],
        out_specs=(hbm, hbm, hbm, vmem, vmem, vmem, vmem, vmem, vmem),
        scratch_shapes=[
            pltpu.VMEM((32, 64, width), bf16),
            pltpu.VMEM((32, 2, 16, inner), bf16),
            pltpu.VMEM((32, 32, 2 * hidden), bf16),
            pltpu.VMEM((4 * slots, queries, width), bf16),
            pltpu.VMEM((4 * slots, queries, width), bf16),
            pltpu.VMEM((2, width, all_rows), bf16),
            pltpu.VMEM((blocks, 64, width), bf16),
            pltpu.VMEM((blocks, 64, width), bf16),
            pltpu.VMEM((slots, queries, width), bf16),
            pltpu.VMEM((slots, queries, width), bf16),
            pltpu.VMEM((width, slots * patches), bf16),
            pltpu.VMEM((width, rows_latent), bf16),
            pltpu.VMEM((slots, patches, 2 * inner), bf16),
            pltpu.VMEM((slots, queries, 2 * inner), bf16),
            pltpu.VMEM((slots, queries, inner), bf16),
            pltpu.VMEM((slots, queries, inner), bf16),
            pltpu.VMEM((inner, rows_latent), bf16),
            pltpu.VMEM((slots, queries, width), f32),
            pltpu.VMEM((8 * slots, queries, width), bf16),
            pltpu.VMEM((4, 2, 2, rows_up, hidden), bf16),
            pltpu.VMEM((4, 2, rows_up, hidden), bf16),
            pltpu.VMEM((4, 2, rows_up, hidden), bf16),
            pltpu.VMEM((2, 2, slots, queries, width), bf16),
            pltpu.VMEM((2, 2, slots, queries, width), bf16),
            pltpu.VMEM((2, slots, queries, width), bf16),
            pltpu.VMEM((2, slots, queries, width), bf16),
            pltpu.VMEM((2, slots, queries, width), f32),
            pltpu.VMEM((slots, queries, width), bf16),
            pltpu.VMEM((slots, queries, inner), bf16),
            pltpu.VMEM((slots, queries, inner), bf16),
            pltpu.VMEM((4, 8, width), f32),
            pltpu.VMEM((8, width), f32),
            pltpu.VMEM((6, 8, width), f32),
            pltpu.VMEM((4, 8, width), f32),
            pltpu.VMEM((3, 8, width), f32),
            pltpu.VMEM((4, 8, 128), f32),
            pltpu.VMEM((4, 64, width), bf16),
            dma((9,)),
            dma((4,)),
            dma((4,)),
            dma((8,)),
            dma((8, 2)),
            dma((4, 4)),
            dma((4, 4)),
            dma((4,)),
            dma((4,)),
            dma((1,)),
            dma((2,)),
            dma((slots,)),
            dma((slots,)),
            dma((slots,)),
            dma((1,)),
            dma((2,)),
            dma((2, 2)),
            dma((2,)),
            dma((4, 2)),
            dma((4, 2)),
            dma((8,)),
            dma((8,)),
            dma((4,)),
            dma((4,)),
            dma((3,)),
            dma((4,)),
            dma((19,)),
            dma((3,)),
        ],
        compiler_params=pltpu.CompilerParams(
            collective_id=0, has_side_effects=True, vmem_limit_bytes=67043328
        ),
    )(
        media_counts,
        media_patches.reshape(blocks, 64, width),
        latent_rows.reshape(slots, queries, width),
        cotangent.reshape(slots, queries, width),
        query_weight,
        key_value_weight,
        output_weight,
        up_weight.reshape(4, rows_up // 4, hidden),
        down_weight,
        norm_tile,
    )
    new, media_grad, latent_grad, norms, query_grad, key_value_grad, output_grad, up_grad, down_grad = outs
    norms = lax.dynamic_slice(norms, (0, head * part), (6, part))
    return (
        new.reshape(latent_rows.shape),
        media_grad.reshape(media_patches.shape),
        latent_grad.reshape(latent_rows.shape),
        norms[0:3],
        norms[3:6],
        query_grad,
        key_value_grad,
        output_grad,
        up_grad,
        down_grad,
    )


def block_fits(mesh):
    return mesh.shape["img"] == 8 and mesh.shape["head"] == 4


def solution(mesh):
    return jax.shard_map(
        block_plan if block_fits(mesh) else gathered_plan,
        mesh=mesh,
        in_specs=(
            P(("img", "head"), None, None, None),
            P(("img", "head"), None, None, None),
            P(("img", "head")),
            P(None, ("img", "head")),
            P(None, ("img", "head")),
            P(("img", "head"), None),
            P(("img", "head"), None),
            P(("img", "head"), None),
            P("img", "head"),
            P("head", "img"),
            P(("img", "head"), None, None, None),
        ),
        out_specs=(
            P(("img", "head"), None, None, None),
            P(("img", "head"), None, None, None),
            P(("img", "head"), None, None, None),
            P(None, ("img", "head")),
            P(None, ("img", "head")),
            P(("img", "head"), None),
            P(("img", "head"), None),
            P(("img", "head"), None),
            P("img", "head"),
            P("head", "img"),
        ),
        check_vma=False,
    )
```

```python
import jax
import jax.numpy as jnp
from jax import lax
from jax.experimental import pallas as pl
from jax.experimental.pallas import tpu as pltpu
from jax.sharding import PartitionSpec as P

HEADS = 8


def layer_norm(values, norm_gain, norm_shift):
    centered = values - jnp.mean(values, axis=-1, keepdims=True)
    variance = jnp.mean(centered * centered, axis=-1, keepdims=True)
    return centered * lax.rsqrt(variance + 1e-05) * norm_gain + norm_shift


def norm_backward(values, norm_gain, norm_shift, upstream):
    primal, pullback = jax.vjp(layer_norm, values, norm_gain, norm_shift)
    return pullback(upstream)


def exact_gelu(values):
    return jax.nn.gelu(values, approximate=False)


def gelu_backward(values, upstream):
    primal, pullback = jax.vjp(exact_gelu, values)
    return pullback(upstream)[0]


def contract_rows(left_side, right_side):
    return lax.dot_general(
        left_side, right_side, (((0,), (0,)), ((), ())), preferred_element_type=jnp.float32
    )


def contract_cols(left_side, right_side):
    return lax.dot_general(
        left_side, right_side, (((1,), (1,)), ((), ())), preferred_element_type=jnp.float32
    )


def gathered_plan(
    media_patches,
    latent_rows,
    media_counts,
    norm_gains,
    norm_biases,
    query_weight,
    key_value_weight,
    output_weight,
    up_weight,
    down_weight,
    cotangent,
):
    samp_local, media_slots, patches, model_width = media_patches.shape
    queries_per = latent_rows.shape[2]
    images = samp_local * media_slots
    keys_per = patches + queries_per
    rows_local = images * queries_per
    gathered = (
        lax.all_gather(query_weight, ("img", "head"), axis=0, tiled=True),
        lax.all_gather(key_value_weight, ("img", "head"), axis=0, tiled=True),
        lax.all_gather(output_weight, ("img", "head"), axis=0, tiled=True),
        lax.all_gather(norm_gains, ("img", "head"), axis=1, tiled=True),
        lax.all_gather(norm_biases, ("img", "head"), axis=1, tiled=True),
    )
    query_full, key_value_full, output_full, gains_low, biases_low = gathered
    norm_gain = gains_low.astype(jnp.float32)
    norm_shift = biases_low.astype(jnp.float32)
    inner_width = query_full.shape[1]
    head_size = inner_width // HEADS
    score_scale = head_size ** (-0.5)
    up_part, down_part = (
        lax.all_gather(up_weight, "img", axis=0, tiled=True),
        lax.all_gather(down_weight, "img", axis=1, tiled=True),
    )
    media_full = media_patches.reshape(images, patches, model_width).astype(jnp.float32)
    latent_full = latent_rows.reshape(images, queries_per, model_width).astype(jnp.float32)
    media_norm = layer_norm(media_full, norm_gain[0], norm_shift[0]).astype(jnp.bfloat16)
    latent_norm = layer_norm(latent_full, norm_gain[1], norm_shift[1]).astype(jnp.bfloat16)
    query_rows = (
        jnp.einsum("ild,de->ile", latent_norm, query_full, preferred_element_type=jnp.float32)
        * score_scale
    ).astype(jnp.bfloat16)
    key_input = jnp.concatenate([media_norm, latent_norm], axis=1)
    key_value_rows = jnp.einsum(
        "ikd,de->ike", key_input, key_value_full, preferred_element_type=jnp.float32
    ).astype(jnp.bfloat16)
    query_heads = (
        query_rows.reshape(images, queries_per, HEADS, head_size)
        .transpose(2, 0, 1, 3)
        .reshape(HEADS, images, queries_per * head_size)
    )
    key_value_heads = (
        key_value_rows.reshape(images, keys_per, 2, HEADS, head_size)
        .transpose(3, 0, 1, 2, 4)
        .reshape(HEADS, images, keys_per, 2 * head_size)
    )
    query_group, key_value_group = (
        lax.all_to_all(query_heads, "head", split_axis=0, concat_axis=1, tiled=True),
        lax.all_to_all(key_value_heads, "head", split_axis=0, concat_axis=1, tiled=True),
    )
    heads_dev = query_group.shape[0]
    group_images = query_group.shape[1]
    query_block = query_group.reshape(heads_dev, group_images, queries_per, head_size)
    key_block = key_value_group[:, :, :, :head_size]
    value_block = key_value_group[:, :, :, head_size:]
    scores = jnp.einsum(
        "hgqe,hgke->hgqk", query_block, key_block, preferred_element_type=jnp.float32
    )
    row_max = jnp.max(scores, axis=-1, keepdims=True)
    weights = jnp.exp(scores - row_max)
    totals = jnp.sum(weights, axis=-1, keepdims=True)
    log_total = row_max + jnp.log(totals)
    probabilities = (weights / totals).astype(jnp.bfloat16)
    attended = jnp.einsum(
        "hgqk,hgke->hgqe", probabilities, value_block, preferred_element_type=jnp.float32
    ).astype(jnp.bfloat16)
    attended_back = lax.all_to_all(
        attended.reshape(heads_dev, group_images, queries_per * head_size),
        "head",
        split_axis=1,
        concat_axis=0,
        tiled=True,
    )
    attended_local = (
        attended_back.reshape(HEADS, images, queries_per, head_size)
        .transpose(1, 2, 0, 3)
        .reshape(images, queries_per, inner_width)
    )
    attn_delta = jnp.einsum(
        "ile,ed->ild", attended_local, output_full, preferred_element_type=jnp.float32
    )
    mid_latent = latent_full + attn_delta
    hidden_in = (
        layer_norm(mid_latent, norm_gain[2], norm_shift[2])
        .astype(jnp.bfloat16)
        .reshape(rows_local, model_width)
    )
    slot_mask = (
        (jnp.arange(media_slots)[None, :] < media_counts[:, None])
        .astype(jnp.float32)
        .reshape(images, 1, 1)
    )
    up_full, down_full = (
        lax.all_gather(up_part, "head", axis=1, tiled=True),
        lax.all_gather(down_part, "head", axis=0, tiled=True),
    )
    pre_act = jnp.dot(hidden_in, up_full, preferred_element_type=jnp.float32)
    act_low = exact_gelu(pre_act).astype(jnp.bfloat16)
    branch_out = jnp.dot(act_low, down_full, preferred_element_type=jnp.float32)
    result = slot_mask * (mid_latent + branch_out.reshape(images, queries_per, model_width))
    new_latents = result.astype(jnp.bfloat16).reshape(latent_rows.shape)
    out_grad = slot_mask * cotangent.reshape(images, queries_per, model_width).astype(jnp.float32)
    branch_grad = out_grad.astype(jnp.bfloat16).reshape(rows_local, model_width)
    act_grad = contract_cols(branch_grad, down_full)
    pre_grad = gelu_backward(pre_act, act_grad).astype(jnp.bfloat16)
    down_grad_whole = contract_rows(act_low, branch_grad)
    up_grad_whole = contract_rows(hidden_in, pre_grad)
    hidden_grad = contract_cols(pre_grad, up_full)
    up_grad_part, down_grad_part = (
        lax.psum_scatter(
            up_grad_whole.astype(jnp.bfloat16), "head", scatter_dimension=1, tiled=True
        ).astype(jnp.float32),
        lax.psum_scatter(
            down_grad_whole.astype(jnp.bfloat16), "head", scatter_dimension=0, tiled=True
        ).astype(jnp.float32),
    )
    up_grad, down_grad = (
        lax.psum_scatter(
            up_grad_part.astype(jnp.bfloat16), "img", scatter_dimension=0, tiled=True
        ).astype(jnp.float32),
        lax.psum_scatter(
            down_grad_part.astype(jnp.bfloat16), "img", scatter_dimension=1, tiled=True
        ).astype(jnp.float32),
    )
    mid_from_norm, gain_ff, bias_ff = norm_backward(
        mid_latent,
        norm_gain[2],
        norm_shift[2],
        hidden_grad.reshape(images, queries_per, model_width),
    )
    mid_grad = out_grad + mid_from_norm
    delta_low = mid_grad.astype(jnp.bfloat16)
    output_weight_grad = jnp.einsum(
        "ile,ild->ed", attended_local, delta_low, preferred_element_type=jnp.float32
    )
    attended_grad = jnp.einsum(
        "ild,ed->ile", delta_low, output_full, preferred_element_type=jnp.float32
    ).astype(jnp.bfloat16)
    grad_heads = (
        attended_grad.reshape(images, queries_per, HEADS, head_size)
        .transpose(2, 0, 1, 3)
        .reshape(HEADS, images, queries_per * head_size)
    )
    grad_group = lax.all_to_all(
        grad_heads, "head", split_axis=0, concat_axis=1, tiled=True
    ).reshape(heads_dev, group_images, queries_per, head_size)
    scores_again = jnp.einsum(
        "hgqe,hgke->hgqk", query_block, key_block, preferred_element_type=jnp.float32
    )
    probs_again = jnp.exp(scores_again - log_total)
    probs_again_low = probs_again.astype(jnp.bfloat16)
    prob_grad = jnp.einsum(
        "hgqe,hgke->hgqk", grad_group, value_block, preferred_element_type=jnp.float32
    )
    value_grad = jnp.einsum(
        "hgqk,hgqe->hgke", probs_again_low, grad_group, preferred_element_type=jnp.float32
    )
    row_dot = jnp.sum(prob_grad * probs_again, axis=-1, keepdims=True)
    score_grad = (probs_again * (prob_grad - row_dot)).astype(jnp.bfloat16)
    query_grad_group = jnp.einsum(
        "hgqk,hgke->hgqe", score_grad, key_block, preferred_element_type=jnp.float32
    ).astype(jnp.bfloat16)
    key_grad = jnp.einsum(
        "hgqk,hgqe->hgke", score_grad, query_block, preferred_element_type=jnp.float32
    )
    key_value_grad_group = jnp.concatenate([key_grad, value_grad], axis=-1).astype(jnp.bfloat16)
    query_back, key_value_back = (
        lax.all_to_all(
            query_grad_group.reshape(heads_dev, group_images, queries_per * head_size),
            "head",
            split_axis=1,
            concat_axis=0,
            tiled=True,
        ),
        lax.all_to_all(key_value_grad_group, "head", split_axis=1, concat_axis=0, tiled=True),
    )
    query_local = (
        query_back.reshape(HEADS, images, queries_per, head_size)
        .transpose(1, 2, 0, 3)
        .reshape(images, queries_per, inner_width)
    )
    key_value_local = (
        key_value_back.reshape(HEADS, images, keys_per, 2, head_size)
        .transpose(1, 2, 3, 0, 4)
        .reshape(images, keys_per, 2 * inner_width)
    )
    query_weight_grad = (
        jnp.einsum("ild,ile->de", latent_norm, query_local, preferred_element_type=jnp.float32)
        * score_scale
    )
    key_value_weight_grad = jnp.einsum(
        "ikd,ike->de", key_input, key_value_local, preferred_element_type=jnp.float32
    )
    key_input_grad = jnp.einsum(
        "ike,de->ikd", key_value_local, key_value_full, preferred_element_type=jnp.float32
    )
    latent_norm_grad = (
        jnp.einsum("ile,de->ild", query_local, query_full, preferred_element_type=jnp.float32)
        * score_scale
        + key_input_grad[:, patches:]
    )
    media_grad_full, gain_media, bias_media = norm_backward(
        media_full, norm_gain[0], norm_shift[0], key_input_grad[:, :patches]
    )
    latent_from_norm, gain_latent, bias_latent = norm_backward(
        latent_full, norm_gain[1], norm_shift[1], latent_norm_grad
    )
    latent_grad_full = mid_grad + latent_from_norm
    gain_terms = jnp.stack([gain_media, gain_latent, gain_ff])
    bias_terms = jnp.stack([bias_media, bias_latent, bias_ff])
    summed = (
        lax.psum_scatter(query_weight_grad, ("img", "head"), scatter_dimension=0, tiled=True),
        lax.psum_scatter(key_value_weight_grad, ("img", "head"), scatter_dimension=0, tiled=True),
        lax.psum_scatter(output_weight_grad, ("img", "head"), scatter_dimension=0, tiled=True),
        lax.psum_scatter(gain_terms, ("img", "head"), scatter_dimension=1, tiled=True),
        lax.psum_scatter(bias_terms, ("img", "head"), scatter_dimension=1, tiled=True),
    )
    media_grad = media_grad_full.astype(jnp.bfloat16).reshape(media_patches.shape)
    latent_grad = latent_grad_full.astype(jnp.bfloat16).reshape(latent_rows.shape)
    return (
        new_latents,
        media_grad,
        latent_grad,
        summed[3],
        summed[4],
        summed[0],
        summed[1],
        summed[2],
        up_grad,
        down_grad,
    )


def tpose(values):
    return jnp.transpose(values, (1, 0))


def dot_nn(left_side, right_side):
    return jnp.dot(left_side, right_side, preferred_element_type=jnp.float32)


def block_kernel(
    counts,
    media_in,
    latent_in,
    cot_in,
    query_in,
    key_value_in,
    output_in,
    up_in,
    down_in,
    norm_in,
    new_out,
    media_out,
    latent_out,
    norm_out,
    query_out,
    key_value_out,
    output_out,
    up_out,
    down_out,
    slab,
    query_full,
    wide,
    hid,
    cotr,
    turned,
    media_v,
    media_n,
    latent_v,
    latent_n,
    media_t,
    latent_t,
    kv_media,
    kv_latent,
    query_v,
    att_v,
    att_t,
    mid_v,
    pair,
    grads,
    xrecv,
    zrecv,
    hsend,
    hrecv,
    hysend,
    hyrecv,
    hown,
    delta_v,
    attg_v,
    qgrad_v,
    normg,
    normv,
    gacc,
    gsend,
    gyr,
    gzr,
    gzr_v,
    loc,
    at_z,
    at_x,
    at_y,
    at_c,
    ff_z,
    ff_x,
    nb_z,
    nb_x,
    nb_y,
    nb_c,
    hd_y,
    hd_c,
    hd_f,
    bg_y,
    bg_c,
    hp_c,
    hp_y,
    rf_x,
    rf_z,
    ra_c,
    ra_y,
    ra_x,
    ra_z,
    gr_c,
    gr_z,
    sent,
    outs,
):
    n_z, n_x, n_head = 4, 2, 4
    img = lax.axis_index("img")
    head = lax.axis_index("head")
    z = img // n_x
    x = img % n_x
    y = head // 2
    c = head % 2
    xp, yp, cp = 1 - x, 1 - y, 1 - c
    xdev = (z * n_x + xp, head)
    ydev = (img, yp * 2 + c)
    cdev = (img, y * 2 + cp)
    near = (1, 3, 2)
    z1 = z + 1 - 2 * (z % 2)
    z2 = (z + 2) % n_z
    z3 = n_z - 1 - z
    mid = jnp.logical_and(z >= 1, z <= 2)

    def zat(k):
        return (z + k) % n_z

    def zdev(zz):
        return (zz * n_x + x, head)

    width = media_v.shape[2]
    slots = latent_v.shape[0]
    queries = latent_v.shape[1]
    hidden = up_in.shape[1]
    inner = query_full.shape[3]
    f32 = jnp.float32
    bf16 = jnp.bfloat16
    scale = (inner // HEADS) ** (-0.5)

    def rcopy(src, dst, sem_s, sem_r, dev):
        return pltpu.make_async_remote_copy(
            src_ref=src,
            dst_ref=dst,
            send_sem=sem_s,
            recv_sem=sem_r,
            device_id=dev,
            device_id_type=pl.DeviceIdType.MESH,
        )

    def send(src, dst, sem_s, sem_r, dev):
        rcopy(src, dst, sem_s, sem_r, dev).start()

    def arrived(ref, sem):
        pltpu.make_async_copy(ref, ref, sem).wait()

    unit = img * n_head + head
    local = [
        pltpu.make_async_copy(key_value_in, slab.at[unit, 0:32], loc.at[0]),
        pltpu.make_async_copy(output_in, slab.at[unit, 32:48], loc.at[1]),
        pltpu.make_async_copy(query_in.at[0:16], slab.at[unit, 48:64, 0:inner], loc.at[2]),
        pltpu.make_async_copy(query_in.at[16:32], slab.at[unit, 48:64, inner:width], loc.at[3]),
        pltpu.make_async_copy(norm_in, normg.at[head, :, pl.ds(pl.multiple_of(img * 128, 128), 128)], loc.at[4]),
        pltpu.make_async_copy(up_in.at[:, 0:256], wide.at[0, img, :, 0:256], loc.at[5]),
        pltpu.make_async_copy(cot_in, pair.at[0:slots], loc.at[6]),
        pltpu.make_async_copy(latent_in, latent_v, loc.at[7]),
        pltpu.make_async_copy(media_in, media_v, loc.at[8]),
    ] + [
        pltpu.make_async_copy(
            up_in.at[:, q * 256 : (q + 1) * 256], wide.at[q, img, :, 0:256], loc.at[8 + q]
        )
        for q in range(1, 4)
    ]
    for copy in local:
        copy.start()

    barrier = pltpu.get_barrier_semaphore()
    peers = [zdev(zat(k)) for k in near] + [xdev, ydev, cdev]
    for dev in peers:
        pl.semaphore_signal(barrier, inc=1, device_id=dev, device_id_type=pl.DeviceIdType.MESH)
    pl.semaphore_wait(barrier, len(peers))

    def lanes(ii):
        return pl.ds(pl.multiple_of(ii * 128, 128), 128)

    local[4].wait()
    for k in near:
        send(norm_in, normg.at[head, :, lanes(img)], sent.at[0], nb_z.at[z], zdev(zat(k)))
    for copy in local[0:4]:
        copy.wait()

    def put_slab(uu, sem, dev):
        send(slab.at[uu], slab.at[uu], sent.at[1], sem, dev)

    put_slab(unit, at_z.at[z], zdev(z2))
    put_slab(unit, at_z.at[z], zdev(z1))

    @pl.when(mid)
    def _():
        put_slab(unit, at_z.at[z], zdev(z3))

    put_slab(unit, at_x.at[z], xdev)
    put_slab(unit, at_y.at[img], ydev)
    put_slab(unit, at_c.at[img, y], cdev)

    for copy in [local[5]] + local[9:12]:
        copy.wait()
    down = down_in[...]
    for j in range(hidden // 128):
        at = 256 + (j % 2) * 128
        wide[j // 2, img, :, at : at + 128] = tpose(down[j * 128 : (j + 1) * 128, :])

    local[6].wait()
    filled = counts[0]
    for m in range(slots):
        keep = jnp.clip(filled - m, 0, 1).astype(f32)
        cotr[head * slots + m] = (pair[m].astype(f32) * keep).astype(bf16)

    def nb_wait(kind, idx, ref):
        arrived(ref, kind.at[idx])

    for k in near:
        zz = zat(k)
        arrived(normg.at[head, :, lanes(zz * n_x + x)], nb_z.at[zz])
    for k in (0,) + near:
        zz = zat(k)
        ii = zz * n_x + x
        send(normg.at[head, :, lanes(ii)], normg.at[head, :, lanes(ii)], sent.at[2], nb_x.at[zz], xdev)

    def at_forward_z(zz, onward):
        uu = (zz * n_x + x) * n_head + head
        arrived(slab.at[uu], at_z.at[zz])
        if onward:

            @pl.when(mid)
            def _():
                put_slab(uu, at_z.at[zz], zdev(z1))

        put_slab(uu, at_x.at[zz], xdev)
        put_slab(uu, at_y.at[zz * n_x + x], ydev)
        put_slab(uu, at_c.at[zz * n_x + x, y], cdev)

    def at_forward_x(zz):
        ii = zz * n_x + xp
        uu = ii * n_head + head
        arrived(slab.at[uu], at_x.at[zz])
        put_slab(uu, at_y.at[ii], ydev)
        put_slab(uu, at_c.at[ii, y], cdev)

    def at_forward_y(ii):
        uu = ii * n_head + yp * 2 + c
        arrived(slab.at[uu], at_y.at[ii])
        put_slab(uu, at_c.at[ii, yp], cdev)

    at_forward_z(z2, True)
    at_forward_x(z)
    at_forward_z(z1, False)
    for k in (0,) + near:
        zz = zat(k)
        arrived(normg.at[head, :, lanes(zz * n_x + xp)], nb_x.at[zz])
    send(normg.at[head], normg.at[head], sent.at[3], nb_y.at[0], ydev)
    send(normg.at[head], normg.at[head], sent.at[4], nb_c.at[y], cdev)
    at_forward_z(z3, False)

    def ff_unit(q, ii):
        return wide.at[q, ii]

    def ff_own_z(q):
        piece = ff_unit(q, img)
        send(piece, piece, sent.at[5], ff_z.at[z, q], zdev(z2))
        send(piece, piece, sent.at[5], ff_z.at[z, q], zdev(z1))

        @pl.when(mid)
        def _():
            send(piece, piece, sent.at[5], ff_z.at[z, q], zdev(z3))

    def ff_own_x(q):
        piece = ff_unit(q, img)
        send(piece, piece, sent.at[6], ff_x.at[z, q], xdev)

    def ff_forward(q):
        for zz in (z2, z1, z3):
            piece = ff_unit(q, zz * n_x + x)
            arrived(piece, ff_z.at[zz, q])
            if zz is z2:

                @pl.when(mid)
                def _():
                    send(piece, piece, sent.at[5], ff_z.at[zz, q], zdev(z1))

            send(piece, piece, sent.at[6], ff_x.at[zz, q], xdev)
        if q + 2 < 4:
            ff_own_z(q + 2)
            ff_own_x(q + 2)

    for q in range(2):
        ff_own_z(q)
        ff_own_x(q)
    at_forward_x(z2)
    arrived(normg.at[yp * 2 + c], nb_y.at[0])
    send(normg.at[yp * 2 + c], normg.at[yp * 2 + c], sent.at[4], nb_c.at[yp], cdev)
    at_forward_x(z1)
    at_forward_x(z3)
    own_cot = cotr.at[pl.ds(head * slots, slots)]
    send(own_cot, own_cot, sent.at[7], bg_y.at[0], ydev)
    send(own_cot, own_cot, sent.at[7], bg_c.at[y], cdev)

    arrived(normg.at[y * 2 + cp], nb_c.at[y])
    arrived(normg.at[yp * 2 + cp], nb_c.at[yp])
    normv[...] = normg[0] + normg[1] + normg[2] + normg[3]

    def gain(j):
        return normv[j : j + 1, :]

    def shift(j):
        return normv[3 + j : 4 + j, :]

    def statistics(values):
        centered = values - jnp.mean(values, axis=-1, keepdims=True)
        inverse = lax.rsqrt(jnp.mean(centered * centered, axis=-1, keepdims=True) + 1e-05)
        return centered * inverse, inverse

    def norm_rows(values, j):
        return (statistics(values)[0] * gain(j) + shift(j)).astype(bf16)

    half = queries // 2

    def norm_latent(m, carry):
        for r in range(2):
            rows = slice(r * half, (r + 1) * half)
            latent_n[m, rows, :] = norm_rows(latent_v[m, rows, :].astype(f32), 1)
        return carry

    def norm_media(m, carry):
        for r in range(2):
            rows = slice(r * half, (r + 1) * half)
            media_n[m, rows, :] = norm_rows(media_v[m, rows, :].astype(f32), 0)
        return carry

    local[7].wait()
    lax.fori_loop(0, slots, norm_latent, 0)
    at_forward_y(img)
    at_forward_y(z2 * n_x + x)
    local[8].wait()
    blocks = media_v.shape[0]
    step = blocks // 4
    order = [z * n_x + xp, z1 * n_x + x, z3 * n_x + x, z2 * n_x + xp, z1 * n_x + xp, z3 * n_x + xp]
    for r in range(4):
        lax.fori_loop(r * step, (r + 1) * step, norm_media, 0)
        at_forward_y(order[r])

    def turn_media(r, carry):
        block = media_n[pl.ds(r * 2, 2)].reshape(128, width)
        for d in range(width // 128):
            media_t[d * 128 : (d + 1) * 128, pl.ds(pl.multiple_of(r * 128, 128), 128)] = tpose(
                block[:, d * 128 : (d + 1) * 128]
            )
        return carry

    rows_latent = slots * queries

    def turn_latent(source, target, columns):
        whole = source[...].reshape(rows_latent, columns)
        for r in range(0, rows_latent, 128):
            stop = min(r + 128, rows_latent)
            for d in range(columns // 128):
                target[d * 128 : (d + 1) * 128, r:stop] = tpose(
                    whole[r:stop, d * 128 : (d + 1) * 128]
                )

    turn_latent(latent_n, latent_t, width)
    at_forward_y(order[4])
    lax.fori_loop(0, blocks * queries // 128, turn_media, 0)
    ff_forward(0)
    at_forward_y(order[5])

    for ii in range(8):
        for yy in range(2):
            arrived(slab.at[ii * n_head + yy * 2 + cp], at_c.at[ii, yy])

    query_full[:, 0] = slab[:, 48:64, 0:inner]
    query_full[:, 1] = slab[:, 48:64, inner:width]

    def query_tile(cols):
        return query_full[:, :, :, cols].reshape(width, -1)

    def kv_tile(cols):
        return slab[:, 0:32, cols].reshape(width, -1)

    def out_tile(cols):
        return slab[:, 32:48, cols].reshape(inner, -1)

    latent_rows_n = latent_n[...].reshape(rows_latent, width)

    def tile(t):
        return pl.ds(pl.multiple_of(t * 256, 256), 256)

    query_v[...] = (
        (dot_nn(latent_rows_n, query_full[...].reshape(width, inner)) * scale)
        .astype(bf16)
        .reshape(slots, queries, inner)
    )
    groups = kv_media.shape[0]
    media_rows_n = media_n[...].reshape(groups * 256, width)

    def kv_step(t, carry):
        weight = kv_tile(tile(t))
        kv_latent[:, :, tile(t)] = dot_nn(latent_rows_n, weight).astype(bf16).reshape(slots, queries, 256)
        kv_media[:, :, tile(t)] = dot_nn(media_rows_n, weight).astype(bf16).reshape(groups, 256, 256)
        return carry

    lax.fori_loop(0, width // 512, kv_step, 0)
    ff_forward(1)
    lax.fori_loop(width // 512, width // 256, kv_step, 0)

    def lane_mask(hh, dtype):
        lane = lax.broadcasted_iota(jnp.int32, (1, 256), 1)
        return (lane // queries == hh).astype(f32).astype(dtype)

    def spread(rows):
        return jnp.concatenate([rows * lane_mask(hh, bf16) for hh in range(4)], axis=0)

    def fold(rows):
        total = rows[0:queries] * lane_mask(0, f32)
        for hh in range(1, 4):
            total = total + rows[hh * queries : (hh + 1) * queries] * lane_mask(hh, f32)
        return total

    def probabilities(m, g):
        q_rows = spread(query_v[m, :, tile(g)])
        k_media = kv_media[m, :, tile(g)]
        k_latent = kv_latent[m, :, tile(g)]
        s_media = contract_cols(q_rows, k_media)
        s_latent = contract_cols(q_rows, k_latent)
        top = jnp.maximum(
            jnp.max(s_media, axis=-1, keepdims=True), jnp.max(s_latent, axis=-1, keepdims=True)
        )
        e_media = jnp.exp(s_media - top)
        e_latent = jnp.exp(s_latent - top)
        total = jnp.sum(e_media, axis=-1, keepdims=True) + jnp.sum(e_latent, axis=-1, keepdims=True)
        inverse = 1.0 / total
        return q_rows, k_media, k_latent, e_media * inverse, e_latent * inverse

    def attend(m, g):
        p_media, p_latent = probabilities(m, g)[3:]
        v_media = kv_media[m, :, tile(g + 2)]
        v_latent = kv_latent[m, :, tile(g + 2)]
        rows = dot_nn(p_media.astype(bf16), v_media) + dot_nn(p_latent.astype(bf16), v_latent)
        att_v[m, :, tile(g)] = fold(rows).astype(bf16)

    def forward_image(m, carry):
        attend(m, 0)
        attend(m, 1)
        mid_v[m] = latent_v[m].astype(f32) + dot_nn(att_v[m], out_tile(slice(0, width)))
        for r in range(2):
            rows = slice(r * half, (r + 1) * half)
            hid[head * slots + m, rows, :] = norm_rows(mid_v[m, rows, :], 2)
        piece = hid.at[head * slots + m]
        send(piece, piece, sent.at[8], hd_y.at[m], ydev)
        send(piece, piece, sent.at[8], hd_c.at[m], cdev)
        return carry

    lax.fori_loop(0, 2, forward_image, 0)
    ff_forward(2)
    lax.fori_loop(2, slots, forward_image, 0)

    other = yp * 2 + c
    cot_other = cotr.at[pl.ds(other * slots, slots)]
    arrived(cot_other, bg_y.at[0])
    send(cot_other, cot_other, sent.at[7], bg_c.at[yp], cdev)
    turn_latent(att_v, att_t, inner)
    for yy in (y, yp):
        arrived(cotr.at[pl.ds((yy * 2 + cp) * slots, slots)], bg_c.at[yy])

    all_rows = n_head * slots * queries

    def turn_rows(source, slot):
        def body(r, carry):
            block = source[pl.ds(r * 2, 2)].reshape(128, width)
            for d in range(width // 128):
                turned[slot, d * 128 : (d + 1) * 128, pl.ds(pl.multiple_of(r * 128, 128), 128)] = tpose(
                    block[:, d * 128 : (d + 1) * 128]
                )
            return carry

        lax.fori_loop(0, all_rows // 128, body, 0)

    turn_rows(cotr, 1)
    ff_forward(3)

    act_at = 4 * slots

    def ff_rows(q, start):
        rows = pl.ds(start, 2 * slots)
        pre = dot_nn(hid[rows].reshape(all_rows // 2, width), wide[q, :, :, 0:256].reshape(width, 256))
        grad = dot_nn(cotr[rows].reshape(all_rows // 2, width), wide[q, :, :, 256:512].reshape(width, 256))
        below = 0.5 * (1.0 + lax.erf(pre * 0.7071067811865476))
        slope = below + pre * (jnp.exp(-0.5 * pre * pre) * 0.3989422804014327)
        pair[rows, :, tile(q)] = (grad * slope).astype(bf16).reshape(2 * slots, queries, 256)
        pair[pl.ds(act_at + start, 2 * slots), :, tile(q)] = (
            (pre * below).astype(bf16).reshape(2 * slots, queries, 256)
        )

    def ff_near(q, carry):
        for zz in range(n_z):
            arrived(ff_unit(q, zz * n_x + xp), ff_x.at[zz, q])
        ff_rows(q, y * 2 * slots)
        return carry

    def ff_far(q, carry):
        ff_rows(q, yp * 2 * slots)
        return carry

    def hid_near(m, carry):
        arrived(hid.at[(y * 2 + cp) * slots + m], hd_c.at[m])
        return carry

    def hid_forward(m, carry):
        piece = hid.at[other * slots + m]
        arrived(piece, hd_y.at[m])
        send(piece, piece, sent.at[8], hd_f.at[m], cdev)
        return carry

    def hid_far(m, carry):
        arrived(hid.at[(yp * 2 + cp) * slots + m], hd_f.at[m])
        return carry

    def grad_tile(q, carry):
        def over_parts(part, carry2):
            right = pair[pl.ds(part * act_at, act_at), :, tile(q)].reshape(all_rows, 256)
            value = dot_nn(turned[part], right).astype(bf16).reshape(n_z, n_x, 128, 256)
            grads[q, part, 0] = value[:, 0]
            grads[q, part, 1] = value[:, 1]
            send(grads.at[q, part, xp], xrecv.at[q, part], sent.at[11], rf_x.at[q, part], xdev)
            return carry2

        return lax.fori_loop(0, 2, over_parts, carry)

    lax.fori_loop(0, slots, hid_near, 0)
    lax.fori_loop(0, 3, ff_near, 0)
    lax.fori_loop(0, slots, hid_forward, 0)
    lax.fori_loop(0, slots, hid_far, 0)
    turn_rows(hid, 0)
    ff_far(0, 0)
    grad_tile(0, 0)
    ff_near(3, 0)
    lax.fori_loop(1, 4, ff_far, 0)

    def wide_rows(part, q, t):
        return wide[q, pl.ds(t * 4, 4), :, part * 256 : (part + 1) * 256].reshape(512, 256)

    def broad(t):
        return pl.ds(pl.multiple_of(t * 512, 512), 512)

    def back_rows(left, part, t):
        total = contract_cols(left[:, 0:256], wide_rows(part, 0, t))
        for q in range(1, 4):
            total = total + contract_cols(left[:, q * 256 : (q + 1) * 256], wide_rows(part, q, t))
        return total

    def head_sum(part):
        def rows_of(hh):
            return pair[pl.ds(part * act_at + hh * slots, slots)].reshape(rows_latent, hidden)

        for slot, hh in enumerate((yp * 2 + cp, y * 2 + cp)):
            left = rows_of(hh)

            def to_core(t, carry, left=left, slot=slot):
                value = back_rows(left, part, t)
                hsend[slot, :, :, broad(t)] = value.astype(bf16).reshape(slots, queries, 512)
                return carry

            lax.fori_loop(0, width // 512, to_core, 0)
            send(hsend.at[slot], hrecv.at[part, slot], sent.at[9], hp_c.at[part, slot], cdev)
        left_y = rows_of(yp * 2 + c)
        arrived(hrecv.at[part, 0], hp_c.at[part, 0])

        def to_y(t, carry):
            value = back_rows(left_y, part, t).reshape(slots, queries, 512)
            hysend[part, :, :, broad(t)] = (value + hrecv[part, 0, :, :, broad(t)].astype(f32)).astype(bf16)
            return carry

        lax.fori_loop(0, width // 512, to_y, 0)
        send(hysend.at[part], hyrecv.at[part], sent.at[10], hp_y.at[part], ydev)
        left_own = rows_of(head)
        arrived(hrecv.at[part, 1], hp_c.at[part, 1])

        def to_own(t, carry):
            value = back_rows(left_own, part, t).reshape(slots, queries, 512)
            hown[part, :, :, broad(t)] = value + hrecv[part, 1, :, :, broad(t)].astype(f32)
            return carry

        lax.fori_loop(0, width // 512, to_own, 0)

    arrived(hid.at[0 : 3 * slots], sent.at[8])
    head_sum(0)

    def sum_tile(u):
        q, part = u // 2, u % 2
        arrived(xrecv.at[q, part], rf_x.at[q, part])
        for k, zz in enumerate((z1, z2, z3)):
            grads[q, part, x, zz] = (
                grads[q, part, x, zz].astype(f32) + xrecv[q, part, zz].astype(f32)
            ).astype(bf16)
            send(grads.at[q, part, x, zz], zrecv.at[k, part, q], sent.at[12], rf_z.at[k, part], zdev(zz))

    lax.fori_loop(1, 4, grad_tile, 0)
    sum_tile(0)
    sum_tile(1)
    arrived(hsend, sent.at[9])
    head_sum(1)
    sum_tile(2)

    gacc[...] = jnp.zeros_like(gacc)

    def tally(j, upper, xhat):
        gacc[j] += jnp.sum((upper * xhat).reshape(-1, 8, width), axis=0)
        gacc[3 + j] += jnp.sum(upper.reshape(-1, 8, width), axis=0)

    def norm_back(values, j, upper):
        xhat, inverse = statistics(values)
        tally(j, upper, xhat)
        g = upper * gain(j)
        return inverse * (
            g - jnp.mean(g, axis=-1, keepdims=True) - xhat * jnp.mean(g * xhat, axis=-1, keepdims=True)
        )

    sum_tile(3)
    arrived(hyrecv.at[0], hp_y.at[0])

    def mid_back(m, carry):
        upper = hown[0, m] + hyrecv[0, m].astype(f32)
        back = norm_back(mid_v[m], 2, upper)
        total = cotr[head * slots + m].astype(f32) + back
        hown[0, m] = total
        delta_v[m] = total.astype(bf16)
        return carry

    lax.fori_loop(0, slots, mid_back, 0)
    delta_rows = delta_v[...].reshape(rows_latent, width)

    attg_v[...] = (
        contract_cols(delta_rows, out_tile(slice(0, width))).astype(bf16).reshape(slots, queries, inner)
    )

    gslab = pair

    def gunit(ii, hh_y, hh_c):
        return ii * 4 + hh_c * 2 + hh_y

    def out_grad_step(t, carry):
        right = delta_v[:, :, broad(t)].reshape(rows_latent, 512)
        value = dot_nn(att_t[...], right).astype(bf16)
        for ii in range(8):
            for hh in range(4):
                at = (ii * 4 + hh) * 16
                gslab[gunit(ii, hh // 2, hh % 2), 32:48, broad(t)] = value[at : at + 16]
        return carry

    lax.fori_loop(0, width // 512, out_grad_step, 0)
    sum_tile(4)

    def back_pair(m, g):
        q_rows, k_media, k_latent, p_media, p_latent = probabilities(m, g)
        v_media = kv_media[m, :, tile(g + 2)]
        v_latent = kv_latent[m, :, tile(g + 2)]
        up_rows = spread(attg_v[m, :, tile(g)])
        g_media = contract_cols(up_rows, v_media)
        g_latent = contract_cols(up_rows, v_latent)
        dotted = jnp.sum(g_media * p_media, axis=-1, keepdims=True) + jnp.sum(
            g_latent * p_latent, axis=-1, keepdims=True
        )
        d_media = (p_media * (g_media - dotted)).astype(bf16)
        d_latent = (p_latent * (g_latent - dotted)).astype(bf16)
        qgrad_v[m, :, tile(g)] = fold(dot_nn(d_media, k_media) + dot_nn(d_latent, k_latent)).astype(bf16)
        kv_media[m, :, tile(g)] = contract_rows(d_media, q_rows).astype(bf16)
        kv_latent[m, :, tile(g)] = contract_rows(d_latent, q_rows).astype(bf16)
        kv_media[m, :, tile(g + 2)] = contract_rows(p_media.astype(bf16), up_rows).astype(bf16)
        kv_latent[m, :, tile(g + 2)] = contract_rows(p_latent.astype(bf16), up_rows).astype(bf16)

    def back_image(m, carry):
        back_pair(m, 0)
        back_pair(m, 1)
        return carry

    lax.fori_loop(0, slots, back_image, 0)

    sum_tile(5)

    gcr = hid
    gyr_v = media_n

    def kv_grad_chunk(zz):
        rows = pl.ds(pl.multiple_of(zz * 256, 256), 256)
        left_media = media_t[rows, :]
        left_latent = latent_t[rows, :]

        value = dot_nn(left_media, kv_media[...].reshape(groups * 256, width)) + dot_nn(
            left_latent, kv_latent[...].reshape(rows_latent, width)
        )
        value = value.astype(bf16)
        value_q = dot_nn(left_latent, qgrad_v[...].reshape(rows_latent, inner)) * scale
        value_q = value_q.astype(bf16)
        for xx in range(2):
            for hh in range(4):
                at = (xx * 4 + hh) * 32
                uu = gunit(zz * n_x + xx, hh // 2, hh % 2)
                gslab[uu, 0:32, :] = value[at : at + 32]
                gslab[uu, 48:64, 0:inner] = value_q[at : at + 16]
                gslab[uu, 48:64, inner:width] = value_q[at + 16 : at + 32]
        for xx in range(2):
            ii = zz * n_x + xx
            send(
                gslab.at[pl.ds(ii * 4 + cp * 2, 2)],
                gcr.at[pl.ds(ii * 2, 2)],
                sent.at[13],
                ra_c.at[ii],
                cdev,
            )

    def stage_y(zz):
        for xx in range(2):
            ii = zz * n_x + xx
            arrived(gcr.at[pl.ds(ii * 2, 2)], ra_c.at[ii])
            uu = gunit(ii, yp, c)
            gslab[uu] = (gslab[uu].astype(f32) + gcr[ii * 2 + yp].astype(f32)).astype(bf16)
            send(gslab.at[uu], gyr_v.at[ii], sent.at[14], ra_y.at[ii], ydev)

    def upto_y(ii):
        return (
            gslab[gunit(ii, y, c)].astype(f32) + gcr[ii * 2 + y].astype(f32) + gyr_v[ii].astype(f32)
        )

    def stage_x(zz):
        ii = zz * n_x + xp
        arrived(gyr_v.at[ii], ra_y.at[ii])
        uu = gunit(ii, y, c)
        gslab[uu] = upto_y(ii).astype(bf16)
        send(gslab.at[uu], gyr_v.at[8 + zz], sent.at[15], ra_x.at[zz], xdev)

    def stage_z(zz, last):
        ii = zz * n_x + x
        arrived(gyr_v.at[ii], ra_y.at[ii])
        arrived(gyr_v.at[8 + zz], ra_x.at[zz])
        if last:
            return upto_y(ii) + gyr_v[8 + zz].astype(f32)
        uu = gunit(ii, y, c)
        gslab[uu] = (upto_y(ii) + gyr_v[8 + zz].astype(f32)).astype(bf16)
        send(gslab.at[uu], gzr_v.at[z], sent.at[16], ra_z.at[z], zdev(zz))
        return None

    chunk = [zat(1), zat(3), zat(2), z]
    kv_grad_chunk(chunk[0])
    kv_grad_chunk(chunk[1])
    stage_y(chunk[0])
    kv_grad_chunk(chunk[2])
    stage_y(chunk[1])
    kv_grad_chunk(chunk[3])
    stage_y(chunk[2])
    sum_tile(6)

    arrived(hyrecv.at[1], hp_y.at[1])
    new_v = delta_v

    for m in range(slots):
        keep = jnp.clip(filled - m, 0, 1).astype(f32)
        for r in range(2):
            rows = slice(r * half, (r + 1) * half)
            branch = hown[1, m, rows, :] + hyrecv[1, m, rows, :].astype(f32)
            new_v[m, rows, :] = ((mid_v[m, rows, :] + branch) * keep).astype(bf16)
    new_copy = pltpu.make_async_copy(new_v, new_out, outs.at[0])
    new_copy.start()
    stage_y(chunk[3])

    def media_back(m, carry):
        hown[1, 0:4] = contract_cols(kv_media[m], kv_tile(slice(0, width))).reshape(4, 64, width)

        def over_rows(r, carry2):
            block = m * 4 + r
            back = norm_back(media_v[block].astype(f32), 0, hown[1, r])
            media_v[block] = back.astype(bf16)
            return carry2

        lax.fori_loop(0, 4, over_rows, 0)
        pltpu.make_async_copy(media_v.at[pl.ds(m * 4, 4)], media_out.at[pl.ds(m * 4, 4)], outs.at[1]).start()
        return carry

    def latent_back_tiles(t, carry):
        weight = slab[pl.ds(t * 16, 16), 0:32, :].reshape(512, width)
        query_weight = query_full[pl.ds(t * 16, 16)].reshape(512, inner)
        hown[1, :, :, broad(t)] = (
            contract_cols(kv_latent[...].reshape(rows_latent, width), weight)
            + contract_cols(qgrad_v[...].reshape(rows_latent, inner), query_weight) * scale
        ).reshape(slots, queries, 512)
        return carry

    def latent_back(m, carry):
        back = norm_back(latent_v[m].astype(f32), 1, hown[1, m])
        latent_v[m] = (hown[0, m] + back).astype(bf16)
        return carry

    lax.fori_loop(0, width // 512, latent_back_tiles, 0)
    lax.fori_loop(0, slots, latent_back, 0)
    latent_copy = pltpu.make_async_copy(latent_v, latent_out, outs.at[2])
    latent_copy.start()
    lax.fori_loop(0, 2, media_back, 0)
    sum_tile(7)
    stage_x(chunk[0])
    stage_x(chunk[1])
    lax.fori_loop(2, 4, media_back, 0)
    stage_x(chunk[2])
    stage_z(chunk[0], False)
    stage_z(chunk[1], False)
    lax.fori_loop(4, 5, media_back, 0)
    stage_x(chunk[3])
    stage_z(chunk[2], False)

    for j in range(6):
        gsend[0, j : j + 1, :] = jnp.sum(gacc[j], axis=0, keepdims=True)
    gsend[0, 6:8, :] = jnp.zeros((2, width), f32)
    send(gsend.at[0], gyr.at[0], sent.at[17], gr_c.at[0], cdev)
    arrived(gyr.at[0], gr_c.at[0])
    gsend[1] = gsend[0] + gyr[0]
    send(gsend.at[1], gyr.at[1], sent.at[17], gr_c.at[1], ydev)
    arrived(gyr.at[1], gr_c.at[1])
    gsend[2] = gsend[1] + gyr[1]
    send(gsend.at[2], gyr.at[2], sent.at[17], gr_c.at[2], xdev)
    arrived(gyr.at[2], gr_c.at[2])
    gsend[3] = gsend[2] + gyr[2]
    for k in near:
        zz = zat(k)
        send(gsend.at[3, :, lanes(zz * n_x + x)], gzr.at[z], sent.at[18], gr_z.at[z], zdev(zz))
    total = gsend[3, :, lanes(img)]
    for k in near:
        zz = zat(k)
        arrived(gzr.at[zz], gr_z.at[zz])
        total = total + gzr[zz]
    norm_out[...] = total

    for part in range(2):
        for k in range(3):
            arrived(zrecv.at[k, part], rf_z.at[k, part])

    def own_sum(part, q):
        value = grads[q, part, x, z].astype(f32) + xrecv[q, part, z].astype(f32)
        for k in range(3):
            value = value + zrecv[k, part, q].astype(f32)
        return value

    def last_sums(q, carry):
        up_out[:, tile(q)] = own_sum(0, q)
        value = own_sum(1, q)
        for j in range(2):
            rows = pl.ds(pl.multiple_of(q * 256 + j * 128, 128), 128)
            down_out[rows, :] = tpose(value[:, j * 128 : (j + 1) * 128])
        return carry

    lax.fori_loop(0, hidden // 256, last_sums, 0)

    final = stage_z(chunk[3], True)
    for k in near:
        zz = zat(k)
        arrived(gzr_v.at[zz], ra_z.at[zz])
        final = final + gzr_v[zz].astype(f32)
    key_value_out[...] = final[0:32]
    output_out[...] = final[32:48]
    query_out[0:16, :] = final[48:64, 0:inner]
    query_out[16:32, :] = final[48:64, inner:width]

    new_copy.wait()
    latent_copy.wait()
    arrived(media_v, outs.at[1])
    arrived(normg.at[0, :, 0:384], sent.at[0])
    arrived(slab.at[0:30], sent.at[1])

    @pl.when(mid)
    def _():
        arrived(slab.at[0:2], sent.at[1])
        arrived(wide.at[0], sent.at[5])

    arrived(normg.at[0, :, 0:512], sent.at[2])
    arrived(normg.at[0], sent.at[3])
    arrived(normg.at[0:2], sent.at[4])
    arrived(wide.at[0], sent.at[5])
    arrived(wide.at[0:2], sent.at[6])
    arrived(cotr.at[0 : 3 * slots], sent.at[7])
    arrived(hsend, sent.at[9])
    arrived(hysend, sent.at[10])
    arrived(xrecv, sent.at[11])
    arrived(zrecv, sent.at[12])
    arrived(gcr.at[0:16], sent.at[13])
    arrived(gyr_v.at[0:8], sent.at[14])
    arrived(gyr_v.at[0:4], sent.at[15])
    arrived(gyr_v.at[0:3], sent.at[16])
    arrived(gyr, sent.at[17])
    arrived(gzr.at[0:3], sent.at[18])


def block_plan(
    media_patches,
    latent_rows,
    media_counts,
    norm_gains,
    norm_biases,
    query_weight,
    key_value_weight,
    output_weight,
    up_weight,
    down_weight,
    cotangent,
):
    slots, patches, width = media_patches.shape[1:]
    queries = latent_rows.shape[2]
    inner = query_weight.shape[1]
    hidden = up_weight.shape[1]
    rows_up = up_weight.shape[0]
    part = norm_gains.shape[1]
    head = lax.axis_index("head")
    norm_rows = jnp.concatenate([norm_gains, norm_biases], axis=0).astype(jnp.float32)
    norm_tile = lax.dynamic_update_slice(
        jnp.zeros((8, 128), jnp.float32), norm_rows, (0, head * part)
    )
    blocks = slots * patches // 64
    bf16, f32 = jnp.bfloat16, jnp.float32
    shape = jax.ShapeDtypeStruct
    hbm = pl.BlockSpec(memory_space=pl.ANY)
    vmem = pl.BlockSpec(memory_space=pltpu.VMEM)
    smem = pl.BlockSpec(memory_space=pltpu.SMEM)
    dma = pltpu.SemaphoreType.DMA
    all_rows = 4 * slots * queries
    rows_latent = slots * queries
    outs = pl.pallas_call(
        block_kernel,
        out_shape=(
            shape((slots, queries, width), bf16),
            shape((blocks, 64, width), bf16),
            shape((slots, queries, width), bf16),
            shape((8, 128), f32),
            shape(query_weight.shape, f32),
            shape(key_value_weight.shape, f32),
            shape(output_weight.shape, f32),
            shape(up_weight.shape, f32),
            shape(down_weight.shape, f32),
        ),
        in_specs=[smem] + [hbm] * 7 + [vmem, hbm],
        out_specs=(hbm, hbm, hbm, vmem, vmem, vmem, vmem, vmem, vmem),
        scratch_shapes=[
            pltpu.VMEM((32, 64, width), bf16),
            pltpu.VMEM((32, 2, 16, inner), bf16),
            pltpu.VMEM((4, 8, rows_up, 512), bf16),
            pltpu.VMEM((4 * slots, queries, width), bf16),
            pltpu.VMEM((4 * slots, queries, width), bf16),
            pltpu.VMEM((2, width, all_rows), bf16),
            pltpu.VMEM((blocks, 64, width), bf16),
            pltpu.VMEM((blocks, 64, width), bf16),
            pltpu.VMEM((slots, queries, width), bf16),
            pltpu.VMEM((slots, queries, width), bf16),
            pltpu.VMEM((width, slots * patches), bf16),
            pltpu.VMEM((width, rows_latent), bf16),
            pltpu.VMEM((slots, patches, 2 * inner), bf16),
            pltpu.VMEM((slots, queries, 2 * inner), bf16),
            pltpu.VMEM((slots, queries, inner), bf16),
            pltpu.VMEM((slots, queries, inner), bf16),
            pltpu.VMEM((inner, rows_latent), bf16),
            pltpu.VMEM((slots, queries, width), f32),
            pltpu.VMEM((8 * slots, queries, width), bf16),
            pltpu.VMEM((4, 2, 2, 4, rows_up, 256), bf16),
            pltpu.VMEM((4, 2, 4, rows_up, 256), bf16),
            pltpu.VMEM((3, 2, 4, rows_up, 256), bf16),
            pltpu.VMEM((2, slots, queries, width), bf16),
            pltpu.VMEM((2, 2, slots, queries, width), bf16),
            pltpu.VMEM((2, slots, queries, width), bf16),
            pltpu.VMEM((2, slots, queries, width), bf16),
            pltpu.VMEM((2, slots, queries, width), f32),
            pltpu.VMEM((slots, queries, width), bf16),
            pltpu.VMEM((slots, queries, inner), bf16),
            pltpu.VMEM((slots, queries, inner), bf16),
            pltpu.VMEM((4, 8, width), f32),
            pltpu.VMEM((8, width), f32),
            pltpu.VMEM((6, 8, width), f32),
            pltpu.VMEM((4, 8, width), f32),
            pltpu.VMEM((3, 8, width), f32),
            pltpu.VMEM((4, 8, 128), f32),
            pltpu.VMEM((4, 64, width), bf16),
            dma((12,)),
            dma((4,)),
            dma((4,)),
            dma((8,)),
            dma((8, 2)),
            dma((4, 4)),
            dma((4, 4)),
            dma((4,)),
            dma((4,)),
            dma((1,)),
            dma((2,)),
            dma((slots,)),
            dma((slots,)),
            dma((slots,)),
            dma((1,)),
            dma((2,)),
            dma((2, 2)),
            dma((2,)),
            dma((4, 2)),
            dma((4, 2)),
            dma((8,)),
            dma((8,)),
            dma((4,)),
            dma((4,)),
            dma((3,)),
            dma((4,)),
            dma((19,)),
            dma((3,)),
        ],
        compiler_params=pltpu.CompilerParams(
            collective_id=0, has_side_effects=True, vmem_limit_bytes=67043328
        ),
    )(
        media_counts,
        media_patches.reshape(blocks, 64, width),
        latent_rows.reshape(slots, queries, width),
        cotangent.reshape(slots, queries, width),
        query_weight,
        key_value_weight,
        output_weight,
        up_weight,
        down_weight,
        norm_tile,
    )
    new, media_grad, latent_grad, norms, query_grad, key_value_grad, output_grad, up_grad, down_grad = outs
    norms = lax.dynamic_slice(norms, (0, head * part), (6, part))
    return (
        new.reshape(latent_rows.shape),
        media_grad.reshape(media_patches.shape),
        latent_grad.reshape(latent_rows.shape),
        norms[0:3],
        norms[3:6],
        query_grad,
        key_value_grad,
        output_grad,
        up_grad,
        down_grad,
    )


def block_fits(mesh):
    return mesh.shape["img"] == 8 and mesh.shape["head"] == 4


def solution(mesh):
    return jax.shard_map(
        block_plan if block_fits(mesh) else gathered_plan,
        mesh=mesh,
        in_specs=(
            P(("img", "head"), None, None, None),
            P(("img", "head"), None, None, None),
            P(("img", "head")),
            P(None, ("img", "head")),
            P(None, ("img", "head")),
            P(("img", "head"), None),
            P(("img", "head"), None),
            P(("img", "head"), None),
            P("img", "head"),
            P("head", "img"),
            P(("img", "head"), None, None, None),
        ),
        out_specs=(
            P(("img", "head"), None, None, None),
            P(("img", "head"), None, None, None),
            P(("img", "head"), None, None, None),
            P(None, ("img", "head")),
            P(None, ("img", "head")),
            P(("img", "head"), None),
            P(("img", "head"), None),
            P(("img", "head"), None),
            P("img", "head"),
            P("head", "img"),
        ),
        check_vma=False,
    )
```

```python
import jax
import jax.numpy as jnp
from jax import lax
from jax.experimental import pallas as pl
from jax.experimental.pallas import tpu as pltpu
from jax.sharding import PartitionSpec as P

HEADS = 8


def layer_norm(values, norm_gain, norm_shift):
    centered = values - jnp.mean(values, axis=-1, keepdims=True)
    variance = jnp.mean(centered * centered, axis=-1, keepdims=True)
    return centered * lax.rsqrt(variance + 1e-05) * norm_gain + norm_shift


def norm_backward(values, norm_gain, norm_shift, upstream):
    primal, pullback = jax.vjp(layer_norm, values, norm_gain, norm_shift)
    return pullback(upstream)


def exact_gelu(values):
    return jax.nn.gelu(values, approximate=False)


def gelu_backward(values, upstream):
    primal, pullback = jax.vjp(exact_gelu, values)
    return pullback(upstream)[0]


def contract_rows(left_side, right_side):
    return lax.dot_general(
        left_side, right_side, (((0,), (0,)), ((), ())), preferred_element_type=jnp.float32
    )


def contract_cols(left_side, right_side):
    return lax.dot_general(
        left_side, right_side, (((1,), (1,)), ((), ())), preferred_element_type=jnp.float32
    )


def gathered_plan(
    media_patches,
    latent_rows,
    media_counts,
    norm_gains,
    norm_biases,
    query_weight,
    key_value_weight,
    output_weight,
    up_weight,
    down_weight,
    cotangent,
):
    samp_local, media_slots, patches, model_width = media_patches.shape
    queries_per = latent_rows.shape[2]
    images = samp_local * media_slots
    keys_per = patches + queries_per
    rows_local = images * queries_per
    gathered = (
        lax.all_gather(query_weight, ("img", "head"), axis=0, tiled=True),
        lax.all_gather(key_value_weight, ("img", "head"), axis=0, tiled=True),
        lax.all_gather(output_weight, ("img", "head"), axis=0, tiled=True),
        lax.all_gather(norm_gains, ("img", "head"), axis=1, tiled=True),
        lax.all_gather(norm_biases, ("img", "head"), axis=1, tiled=True),
    )
    query_full, key_value_full, output_full, gains_low, biases_low = gathered
    norm_gain = gains_low.astype(jnp.float32)
    norm_shift = biases_low.astype(jnp.float32)
    inner_width = query_full.shape[1]
    head_size = inner_width // HEADS
    score_scale = head_size ** (-0.5)
    up_part, down_part = (
        lax.all_gather(up_weight, "img", axis=0, tiled=True),
        lax.all_gather(down_weight, "img", axis=1, tiled=True),
    )
    media_full = media_patches.reshape(images, patches, model_width).astype(jnp.float32)
    latent_full = latent_rows.reshape(images, queries_per, model_width).astype(jnp.float32)
    media_norm = layer_norm(media_full, norm_gain[0], norm_shift[0]).astype(jnp.bfloat16)
    latent_norm = layer_norm(latent_full, norm_gain[1], norm_shift[1]).astype(jnp.bfloat16)
    query_rows = (
        jnp.einsum("ild,de->ile", latent_norm, query_full, preferred_element_type=jnp.float32)
        * score_scale
    ).astype(jnp.bfloat16)
    key_input = jnp.concatenate([media_norm, latent_norm], axis=1)
    key_value_rows = jnp.einsum(
        "ikd,de->ike", key_input, key_value_full, preferred_element_type=jnp.float32
    ).astype(jnp.bfloat16)
    query_heads = (
        query_rows.reshape(images, queries_per, HEADS, head_size)
        .transpose(2, 0, 1, 3)
        .reshape(HEADS, images, queries_per * head_size)
    )
    key_value_heads = (
        key_value_rows.reshape(images, keys_per, 2, HEADS, head_size)
        .transpose(3, 0, 1, 2, 4)
        .reshape(HEADS, images, keys_per, 2 * head_size)
    )
    query_group, key_value_group = (
        lax.all_to_all(query_heads, "head", split_axis=0, concat_axis=1, tiled=True),
        lax.all_to_all(key_value_heads, "head", split_axis=0, concat_axis=1, tiled=True),
    )
    heads_dev = query_group.shape[0]
    group_images = query_group.shape[1]
    query_block = query_group.reshape(heads_dev, group_images, queries_per, head_size)
    key_block = key_value_group[:, :, :, :head_size]
    value_block = key_value_group[:, :, :, head_size:]
    scores = jnp.einsum(
        "hgqe,hgke->hgqk", query_block, key_block, preferred_element_type=jnp.float32
    )
    row_max = jnp.max(scores, axis=-1, keepdims=True)
    weights = jnp.exp(scores - row_max)
    totals = jnp.sum(weights, axis=-1, keepdims=True)
    log_total = row_max + jnp.log(totals)
    probabilities = (weights / totals).astype(jnp.bfloat16)
    attended = jnp.einsum(
        "hgqk,hgke->hgqe", probabilities, value_block, preferred_element_type=jnp.float32
    ).astype(jnp.bfloat16)
    attended_back = lax.all_to_all(
        attended.reshape(heads_dev, group_images, queries_per * head_size),
        "head",
        split_axis=1,
        concat_axis=0,
        tiled=True,
    )
    attended_local = (
        attended_back.reshape(HEADS, images, queries_per, head_size)
        .transpose(1, 2, 0, 3)
        .reshape(images, queries_per, inner_width)
    )
    attn_delta = jnp.einsum(
        "ile,ed->ild", attended_local, output_full, preferred_element_type=jnp.float32
    )
    mid_latent = latent_full + attn_delta
    hidden_in = (
        layer_norm(mid_latent, norm_gain[2], norm_shift[2])
        .astype(jnp.bfloat16)
        .reshape(rows_local, model_width)
    )
    slot_mask = (
        (jnp.arange(media_slots)[None, :] < media_counts[:, None])
        .astype(jnp.float32)
        .reshape(images, 1, 1)
    )
    up_full, down_full = (
        lax.all_gather(up_part, "head", axis=1, tiled=True),
        lax.all_gather(down_part, "head", axis=0, tiled=True),
    )
    pre_act = jnp.dot(hidden_in, up_full, preferred_element_type=jnp.float32)
    act_low = exact_gelu(pre_act).astype(jnp.bfloat16)
    branch_out = jnp.dot(act_low, down_full, preferred_element_type=jnp.float32)
    result = slot_mask * (mid_latent + branch_out.reshape(images, queries_per, model_width))
    new_latents = result.astype(jnp.bfloat16).reshape(latent_rows.shape)
    out_grad = slot_mask * cotangent.reshape(images, queries_per, model_width).astype(jnp.float32)
    branch_grad = out_grad.astype(jnp.bfloat16).reshape(rows_local, model_width)
    act_grad = contract_cols(branch_grad, down_full)
    pre_grad = gelu_backward(pre_act, act_grad).astype(jnp.bfloat16)
    down_grad_whole = contract_rows(act_low, branch_grad)
    up_grad_whole = contract_rows(hidden_in, pre_grad)
    hidden_grad = contract_cols(pre_grad, up_full)
    up_grad_part, down_grad_part = (
        lax.psum_scatter(
            up_grad_whole.astype(jnp.bfloat16), "head", scatter_dimension=1, tiled=True
        ).astype(jnp.float32),
        lax.psum_scatter(
            down_grad_whole.astype(jnp.bfloat16), "head", scatter_dimension=0, tiled=True
        ).astype(jnp.float32),
    )
    up_grad, down_grad = (
        lax.psum_scatter(
            up_grad_part.astype(jnp.bfloat16), "img", scatter_dimension=0, tiled=True
        ).astype(jnp.float32),
        lax.psum_scatter(
            down_grad_part.astype(jnp.bfloat16), "img", scatter_dimension=1, tiled=True
        ).astype(jnp.float32),
    )
    mid_from_norm, gain_ff, bias_ff = norm_backward(
        mid_latent,
        norm_gain[2],
        norm_shift[2],
        hidden_grad.reshape(images, queries_per, model_width),
    )
    mid_grad = out_grad + mid_from_norm
    delta_low = mid_grad.astype(jnp.bfloat16)
    output_weight_grad = jnp.einsum(
        "ile,ild->ed", attended_local, delta_low, preferred_element_type=jnp.float32
    )
    attended_grad = jnp.einsum(
        "ild,ed->ile", delta_low, output_full, preferred_element_type=jnp.float32
    ).astype(jnp.bfloat16)
    grad_heads = (
        attended_grad.reshape(images, queries_per, HEADS, head_size)
        .transpose(2, 0, 1, 3)
        .reshape(HEADS, images, queries_per * head_size)
    )
    grad_group = lax.all_to_all(
        grad_heads, "head", split_axis=0, concat_axis=1, tiled=True
    ).reshape(heads_dev, group_images, queries_per, head_size)
    scores_again = jnp.einsum(
        "hgqe,hgke->hgqk", query_block, key_block, preferred_element_type=jnp.float32
    )
    probs_again = jnp.exp(scores_again - log_total)
    probs_again_low = probs_again.astype(jnp.bfloat16)
    prob_grad = jnp.einsum(
        "hgqe,hgke->hgqk", grad_group, value_block, preferred_element_type=jnp.float32
    )
    value_grad = jnp.einsum(
        "hgqk,hgqe->hgke", probs_again_low, grad_group, preferred_element_type=jnp.float32
    )
    row_dot = jnp.sum(prob_grad * probs_again, axis=-1, keepdims=True)
    score_grad = (probs_again * (prob_grad - row_dot)).astype(jnp.bfloat16)
    query_grad_group = jnp.einsum(
        "hgqk,hgke->hgqe", score_grad, key_block, preferred_element_type=jnp.float32
    ).astype(jnp.bfloat16)
    key_grad = jnp.einsum(
        "hgqk,hgqe->hgke", score_grad, query_block, preferred_element_type=jnp.float32
    )
    key_value_grad_group = jnp.concatenate([key_grad, value_grad], axis=-1).astype(jnp.bfloat16)
    query_back, key_value_back = (
        lax.all_to_all(
            query_grad_group.reshape(heads_dev, group_images, queries_per * head_size),
            "head",
            split_axis=1,
            concat_axis=0,
            tiled=True,
        ),
        lax.all_to_all(key_value_grad_group, "head", split_axis=1, concat_axis=0, tiled=True),
    )
    query_local = (
        query_back.reshape(HEADS, images, queries_per, head_size)
        .transpose(1, 2, 0, 3)
        .reshape(images, queries_per, inner_width)
    )
    key_value_local = (
        key_value_back.reshape(HEADS, images, keys_per, 2, head_size)
        .transpose(1, 2, 3, 0, 4)
        .reshape(images, keys_per, 2 * inner_width)
    )
    query_weight_grad = (
        jnp.einsum("ild,ile->de", latent_norm, query_local, preferred_element_type=jnp.float32)
        * score_scale
    )
    key_value_weight_grad = jnp.einsum(
        "ikd,ike->de", key_input, key_value_local, preferred_element_type=jnp.float32
    )
    key_input_grad = jnp.einsum(
        "ike,de->ikd", key_value_local, key_value_full, preferred_element_type=jnp.float32
    )
    latent_norm_grad = (
        jnp.einsum("ile,de->ild", query_local, query_full, preferred_element_type=jnp.float32)
        * score_scale
        + key_input_grad[:, patches:]
    )
    media_grad_full, gain_media, bias_media = norm_backward(
        media_full, norm_gain[0], norm_shift[0], key_input_grad[:, :patches]
    )
    latent_from_norm, gain_latent, bias_latent = norm_backward(
        latent_full, norm_gain[1], norm_shift[1], latent_norm_grad
    )
    latent_grad_full = mid_grad + latent_from_norm
    gain_terms = jnp.stack([gain_media, gain_latent, gain_ff])
    bias_terms = jnp.stack([bias_media, bias_latent, bias_ff])
    summed = (
        lax.psum_scatter(query_weight_grad, ("img", "head"), scatter_dimension=0, tiled=True),
        lax.psum_scatter(key_value_weight_grad, ("img", "head"), scatter_dimension=0, tiled=True),
        lax.psum_scatter(output_weight_grad, ("img", "head"), scatter_dimension=0, tiled=True),
        lax.psum_scatter(gain_terms, ("img", "head"), scatter_dimension=1, tiled=True),
        lax.psum_scatter(bias_terms, ("img", "head"), scatter_dimension=1, tiled=True),
    )
    media_grad = media_grad_full.astype(jnp.bfloat16).reshape(media_patches.shape)
    latent_grad = latent_grad_full.astype(jnp.bfloat16).reshape(latent_rows.shape)
    return (
        new_latents,
        media_grad,
        latent_grad,
        summed[3],
        summed[4],
        summed[0],
        summed[1],
        summed[2],
        up_grad,
        down_grad,
    )


def tpose(values):
    return jnp.transpose(values, (1, 0))


def dot_nn(left_side, right_side):
    return jnp.dot(left_side, right_side, preferred_element_type=jnp.float32)


def block_kernel(
    counts,
    media_in,
    latent_in,
    cot_in,
    query_in,
    key_value_in,
    output_in,
    up_in,
    down_in,
    gain_in,
    bias_in,
    new_out,
    media_out,
    latent_out,
    norm_out,
    query_out,
    key_value_out,
    output_out,
    up_out,
    down_out,
    slab,
    query_full,
    wide,
    hid,
    cotr,
    turned,
    media_v,
    media_n,
    latent_v,
    latent_n,
    media_t,
    latent_t,
    kv_media,
    kv_latent,
    query_v,
    att_v,
    att_t,
    mid_v,
    pair,
    grads,
    xrecv,
    zrecv,
    hsend,
    hrecv,
    hysend,
    hyrecv,
    hown,
    delta_v,
    attg_v,
    qgrad_v,
    normg,
    normv,
    gacc,
    gsend,
    gyr,
    gzr,
    gzr_v,
    loc,
    at_z,
    at_x,
    at_y,
    at_c,
    ff_z,
    ff_x,
    nb_z,
    nb_x,
    nb_y,
    nb_c,
    hd_y,
    hd_c,
    hd_f,
    bg_y,
    bg_c,
    hp_c,
    hp_y,
    rf_x,
    rf_z,
    ra_c,
    ra_y,
    ra_x,
    ra_z,
    gr_c,
    gr_z,
    sent,
    outs,
):
    n_z, n_x, n_head = 4, 2, 4
    img = lax.axis_index("img")
    head = lax.axis_index("head")
    z = img // n_x
    x = img % n_x
    y = head // 2
    c = head % 2
    xp, yp, cp = 1 - x, 1 - y, 1 - c
    xdev = (z * n_x + xp, head)
    ydev = (img, yp * 2 + c)
    cdev = (img, y * 2 + cp)
    near = (1, 3, 2)
    z1 = z + 1 - 2 * (z % 2)
    z2 = (z + 2) % n_z
    z3 = n_z - 1 - z
    mid = jnp.logical_and(z >= 1, z <= 2)

    def zat(k):
        return (z + k) % n_z

    def zdev(zz):
        return (zz * n_x + x, head)

    width = media_v.shape[2]
    slots = latent_v.shape[0]
    queries = latent_v.shape[1]
    hidden = up_in.shape[1]
    inner = query_full.shape[3]
    f32 = jnp.float32
    bf16 = jnp.bfloat16
    scale = (inner // HEADS) ** (-0.5)

    def rcopy(src, dst, sem_s, sem_r, dev):
        return pltpu.make_async_remote_copy(
            src_ref=src,
            dst_ref=dst,
            send_sem=sem_s,
            recv_sem=sem_r,
            device_id=dev,
            device_id_type=pl.DeviceIdType.MESH,
        )

    def send(src, dst, sem_s, sem_r, dev):
        rcopy(src, dst, sem_s, sem_r, dev).start()

    def arrived(ref, sem):
        pltpu.make_async_copy(ref, ref, sem).wait()

    unit = img * n_head + head
    local = [
        pltpu.make_async_copy(key_value_in, slab.at[unit, 0:32], loc.at[0]),
        pltpu.make_async_copy(output_in, slab.at[unit, 32:48], loc.at[1]),
        pltpu.make_async_copy(query_in.at[0:16], slab.at[unit, 48:64, 0:inner], loc.at[2]),
        pltpu.make_async_copy(query_in.at[16:32], slab.at[unit, 48:64, inner:width], loc.at[3]),
        pltpu.make_async_copy(up_in.at[:, 0:256], wide.at[0, img, :, 0:256], loc.at[4]),
        pltpu.make_async_copy(cot_in, pair.at[0:slots], loc.at[5]),
        pltpu.make_async_copy(latent_in, latent_v, loc.at[6]),
        pltpu.make_async_copy(media_in, media_v, loc.at[7]),
    ] + [
        pltpu.make_async_copy(
            up_in.at[:, q * 256 : (q + 1) * 256], wide.at[q, img, :, 0:256], loc.at[7 + q]
        )
        for q in range(1, 4)
    ]
    for copy in local:
        copy.start()

    barrier = pltpu.get_barrier_semaphore()
    peers = [zdev(zat(k)) for k in near] + [xdev, ydev, cdev]
    for dev in peers:
        pl.semaphore_signal(barrier, inc=1, device_id=dev, device_id_type=pl.DeviceIdType.MESH)
    pl.semaphore_wait(barrier, len(peers))

    def lanes(ii):
        return pl.ds(pl.multiple_of(ii * 128, 128), 128)

    part = gain_in.shape[1]
    norm_own = normg.at[head, :, lanes(img)]
    normv[:, 0:128] = jnp.zeros((8, 128), f32)
    normv[0:3, 0:part] = gain_in[...].astype(f32)
    normv[3:6, 0:part] = bias_in[...].astype(f32)
    norm_own[...] = pltpu.roll(normv[:, 0:128], head * part, 1)
    for k in near:
        send(norm_own, norm_own, sent.at[0], nb_z.at[z], zdev(zat(k)))
    for copy in local[0:4]:
        copy.wait()

    def put_slab(uu, sem, dev):
        send(slab.at[uu], slab.at[uu], sent.at[1], sem, dev)

    def put_line(ii):
        uu = ii * n_head + head
        put_slab(uu, at_z.at[z, ii % n_x], zdev(z2))
        put_slab(uu, at_z.at[z, ii % n_x], zdev(z1))

        @pl.when(mid)
        def _():
            put_slab(uu, at_z.at[z, ii % n_x], zdev(z3))

    def put_chip(ii):
        uu = ii * n_head + head
        put_slab(uu, at_y.at[ii], ydev)
        put_slab(uu, at_c.at[ii, y], cdev)

    put_slab(unit, at_x.at[0], xdev)
    put_line(img)
    put_chip(img)

    for copy in [local[4]] + local[8:11]:
        copy.wait()
    down = down_in[...]
    for j in range(hidden // 128):
        at = 256 + (j % 2) * 128
        wide[j // 2, img, :, at : at + 128] = tpose(down[j * 128 : (j + 1) * 128, :])

    local[5].wait()
    filled = counts[0]
    for m in range(slots):
        keep = jnp.clip(filled - m, 0, 1).astype(f32)
        cotr[head * slots + m] = (pair[m].astype(f32) * keep).astype(bf16)

    def nb_wait(kind, idx, ref):
        arrived(ref, kind.at[idx])

    for k in near:
        zz = zat(k)
        arrived(normg.at[head, :, lanes(zz * n_x + x)], nb_z.at[zz])
    for k in (0,) + near:
        zz = zat(k)
        ii = zz * n_x + x
        send(normg.at[head, :, lanes(ii)], normg.at[head, :, lanes(ii)], sent.at[2], nb_x.at[zz], xdev)

    def at_forward_x():
        ii = z * n_x + xp
        arrived(slab.at[ii * n_head + head], at_x.at[0])
        put_line(ii)
        put_chip(ii)

    def at_forward_z(zz, xx, onward):
        ii = zz * n_x + xx
        uu = ii * n_head + head
        arrived(slab.at[uu], at_z.at[zz, xx])
        if onward:

            @pl.when(mid)
            def _():
                put_slab(uu, at_z.at[zz, xx], zdev(z1))

        put_chip(ii)

    def at_forward_y(ii):
        uu = ii * n_head + yp * 2 + c
        arrived(slab.at[uu], at_y.at[ii])
        put_slab(uu, at_c.at[ii, yp], cdev)

    def ff_unit(q, ii):
        return wide.at[q, ii]

    def ff_own_z(q):
        piece = ff_unit(q, img)
        send(piece, piece, sent.at[5], ff_z.at[z, q], zdev(z2))
        send(piece, piece, sent.at[5], ff_z.at[z, q], zdev(z1))

        @pl.when(mid)
        def _():
            send(piece, piece, sent.at[5], ff_z.at[z, q], zdev(z3))

    def ff_own_x(q):
        piece = ff_unit(q, img)
        send(piece, piece, sent.at[6], ff_x.at[z, q], xdev)

    def ff_forward(q):
        for zz in (z2, z1, z3):
            piece = ff_unit(q, zz * n_x + x)
            arrived(piece, ff_z.at[zz, q])
            if zz is z2:

                @pl.when(mid)
                def _():
                    send(piece, piece, sent.at[5], ff_z.at[zz, q], zdev(z1))

            send(piece, piece, sent.at[6], ff_x.at[zz, q], xdev)
        if q + 2 < 4:
            ff_own_z(q + 2)

    for q in range(4):
        ff_own_x(q)
    at_forward_x()
    for k in (0,) + near:
        zz = zat(k)
        arrived(normg.at[head, :, lanes(zz * n_x + xp)], nb_x.at[zz])
    send(normg.at[head], normg.at[head], sent.at[3], nb_y.at[0], ydev)
    send(normg.at[head], normg.at[head], sent.at[4], nb_c.at[y], cdev)
    at_forward_z(z2, x, True)
    at_forward_z(z1, x, False)
    at_forward_z(z3, x, False)
    arrived(normg.at[yp * 2 + c], nb_y.at[0])
    send(normg.at[yp * 2 + c], normg.at[yp * 2 + c], sent.at[4], nb_c.at[yp], cdev)
    at_forward_z(z2, xp, True)
    for q in range(2):
        ff_own_z(q)
    own_cot = cotr.at[pl.ds(head * slots, slots)]

    arrived(normg.at[y * 2 + cp], nb_c.at[y])
    arrived(normg.at[yp * 2 + cp], nb_c.at[yp])
    normv[...] = normg[0] + normg[1] + normg[2] + normg[3]

    def gain(j):
        return normv[j : j + 1, :]

    def shift(j):
        return normv[3 + j : 4 + j, :]

    def statistics(values):
        centered = values - jnp.mean(values, axis=-1, keepdims=True)
        inverse = lax.rsqrt(jnp.mean(centered * centered, axis=-1, keepdims=True) + 1e-05)
        return centered * inverse, inverse

    def norm_rows(values, j):
        return (statistics(values)[0] * gain(j) + shift(j)).astype(bf16)

    half = queries // 2

    def norm_latent(m, carry):
        for r in range(2):
            rows = slice(r * half, (r + 1) * half)
            latent_n[m, rows, :] = norm_rows(latent_v[m, rows, :].astype(f32), 1)
        return carry

    def norm_media(m, carry):
        for r in range(2):
            rows = slice(r * half, (r + 1) * half)
            media_n[m, rows, :] = norm_rows(media_v[m, rows, :].astype(f32), 0)
        return carry

    local[6].wait()
    lax.fori_loop(0, slots, norm_latent, 0)
    at_forward_z(z1, xp, False)
    at_forward_y(img)
    at_forward_y(z * n_x + xp)
    at_forward_z(z3, xp, False)
    send(own_cot, own_cot, sent.at[7], bg_y.at[0], ydev)
    send(own_cot, own_cot, sent.at[7], bg_c.at[y], cdev)
    local[7].wait()
    blocks = media_v.shape[0]
    step = blocks // 4
    order = [z2 * n_x + x, z1 * n_x + x, z3 * n_x + x, z2 * n_x + xp, z1 * n_x + xp, z3 * n_x + xp]
    for r in range(4):
        lax.fori_loop(r * step, (r + 1) * step, norm_media, 0)
        at_forward_y(order[r])

    def turn_media(r, carry):
        block = media_n[pl.ds(r * 2, 2)].reshape(128, width)
        for d in range(width // 128):
            media_t[d * 128 : (d + 1) * 128, pl.ds(pl.multiple_of(r * 128, 128), 128)] = tpose(
                block[:, d * 128 : (d + 1) * 128]
            )
        return carry

    rows_latent = slots * queries

    def turn_latent(source, target, columns):
        whole = source[...].reshape(rows_latent, columns)
        for r in range(0, rows_latent, 128):
            stop = min(r + 128, rows_latent)
            for d in range(columns // 128):
                target[d * 128 : (d + 1) * 128, r:stop] = tpose(
                    whole[r:stop, d * 128 : (d + 1) * 128]
                )

    turn_latent(latent_n, latent_t, width)
    at_forward_y(order[4])
    lax.fori_loop(0, blocks * queries // 128, turn_media, 0)
    at_forward_y(order[5])
    ff_forward(0)

    for ii in range(8):
        for yy in range(2):
            arrived(slab.at[ii * n_head + yy * 2 + cp], at_c.at[ii, yy])

    query_full[:, 0] = slab[:, 48:64, 0:inner]
    query_full[:, 1] = slab[:, 48:64, inner:width]

    def query_tile(cols):
        return query_full[:, :, :, cols].reshape(width, -1)

    def kv_tile(cols):
        return slab[:, 0:32, cols].reshape(width, -1)

    def out_tile(cols):
        return slab[:, 32:48, cols].reshape(inner, -1)

    latent_rows_n = latent_n[...].reshape(rows_latent, width)

    def tile(t):
        return pl.ds(pl.multiple_of(t * 256, 256), 256)

    query_v[...] = (
        (dot_nn(latent_rows_n, query_full[...].reshape(width, inner)) * scale)
        .astype(bf16)
        .reshape(slots, queries, inner)
    )
    groups = kv_media.shape[0]
    media_rows_n = media_n[...].reshape(groups * 256, width)

    def kv_step(t, carry):
        weight = kv_tile(tile(t))
        kv_latent[:, :, tile(t)] = dot_nn(latent_rows_n, weight).astype(bf16).reshape(slots, queries, 256)
        kv_media[:, :, tile(t)] = dot_nn(media_rows_n, weight).astype(bf16).reshape(groups, 256, 256)
        return carry

    lax.fori_loop(0, width // 256, kv_step, 0)
    ff_forward(1)

    def lane_mask(hh, dtype):
        lane = lax.broadcasted_iota(jnp.int32, (1, 256), 1)
        return (lane // queries == hh).astype(f32).astype(dtype)

    def spread(rows):
        return jnp.concatenate([rows * lane_mask(hh, bf16) for hh in range(4)], axis=0)

    def fold(rows):
        total = rows[0:queries] * lane_mask(0, f32)
        for hh in range(1, 4):
            total = total + rows[hh * queries : (hh + 1) * queries] * lane_mask(hh, f32)
        return total

    def probabilities(m, g):
        q_rows = spread(query_v[m, :, tile(g)])
        k_media = kv_media[m, :, tile(g)]
        k_latent = kv_latent[m, :, tile(g)]
        s_media = contract_cols(q_rows, k_media)
        s_latent = contract_cols(q_rows, k_latent)
        top = jnp.maximum(
            jnp.max(s_media, axis=-1, keepdims=True), jnp.max(s_latent, axis=-1, keepdims=True)
        )
        e_media = jnp.exp(s_media - top)
        e_latent = jnp.exp(s_latent - top)
        total = jnp.sum(e_media, axis=-1, keepdims=True) + jnp.sum(e_latent, axis=-1, keepdims=True)
        inverse = 1.0 / total
        return q_rows, k_media, k_latent, e_media * inverse, e_latent * inverse

    def attend(m, g):
        p_media, p_latent = probabilities(m, g)[3:]
        v_media = kv_media[m, :, tile(g + 2)]
        v_latent = kv_latent[m, :, tile(g + 2)]
        rows = dot_nn(p_media.astype(bf16), v_media) + dot_nn(p_latent.astype(bf16), v_latent)
        att_v[m, :, tile(g)] = fold(rows).astype(bf16)

    def forward_image(m, carry):
        attend(m, 0)
        attend(m, 1)
        mid_v[m] = latent_v[m].astype(f32) + dot_nn(att_v[m], out_tile(slice(0, width)))
        for r in range(2):
            rows = slice(r * half, (r + 1) * half)
            hid[head * slots + m, rows, :] = norm_rows(mid_v[m, rows, :], 2)
        piece = hid.at[head * slots + m]
        send(piece, piece, sent.at[8], hd_y.at[m], ydev)
        send(piece, piece, sent.at[8], hd_c.at[m], cdev)
        return carry

    lax.fori_loop(0, slots, forward_image, 0)
    ff_forward(2)

    other = yp * 2 + c
    cot_other = cotr.at[pl.ds(other * slots, slots)]
    arrived(cot_other, bg_y.at[0])
    send(cot_other, cot_other, sent.at[7], bg_c.at[yp], cdev)
    turn_latent(att_v, att_t, inner)
    for yy in (y, yp):
        arrived(cotr.at[pl.ds((yy * 2 + cp) * slots, slots)], bg_c.at[yy])

    all_rows = n_head * slots * queries

    def turn_rows(source, slot):
        def body(r, carry):
            block = source[pl.ds(r * 2, 2)].reshape(128, width)
            for d in range(width // 128):
                turned[slot, d * 128 : (d + 1) * 128, pl.ds(pl.multiple_of(r * 128, 128), 128)] = tpose(
                    block[:, d * 128 : (d + 1) * 128]
                )
            return carry

        lax.fori_loop(0, all_rows // 128, body, 0)

    turn_rows(cotr, 1)

    act_at = 4 * slots

    def ff_rows(q, start):
        rows = pl.ds(start, 2 * slots)
        pre = dot_nn(hid[rows].reshape(all_rows // 2, width), wide[q, :, :, 0:256].reshape(width, 256))
        grad = dot_nn(cotr[rows].reshape(all_rows // 2, width), wide[q, :, :, 256:512].reshape(width, 256))
        below = 0.5 * (1.0 + lax.erf(pre * 0.7071067811865476))
        slope = below + pre * (jnp.exp(-0.5 * pre * pre) * 0.3989422804014327)
        pair[rows, :, tile(q)] = (grad * slope).astype(bf16).reshape(2 * slots, queries, 256)
        pair[pl.ds(act_at + start, 2 * slots), :, tile(q)] = (
            (pre * below).astype(bf16).reshape(2 * slots, queries, 256)
        )

    def ff_near(q, carry):
        for zz in range(n_z):
            arrived(ff_unit(q, zz * n_x + xp), ff_x.at[zz, q])
        ff_rows(q, y * 2 * slots)
        return carry

    def ff_far(q, carry):
        ff_rows(q, yp * 2 * slots)
        return carry

    def hid_near(m, carry):
        arrived(hid.at[(y * 2 + cp) * slots + m], hd_c.at[m])
        return carry

    def hid_forward(m, carry):
        piece = hid.at[other * slots + m]
        arrived(piece, hd_y.at[m])
        send(piece, piece, sent.at[8], hd_f.at[m], cdev)
        return carry

    def hid_far(m, carry):
        arrived(hid.at[(yp * 2 + cp) * slots + m], hd_f.at[m])
        return carry

    def grad_tile(q, carry):
        def over_parts(part, carry2):
            right = pair[pl.ds(part * act_at, act_at), :, tile(q)].reshape(all_rows, 256)
            value = dot_nn(turned[part], right).astype(bf16).reshape(n_z, n_x, 128, 256)
            grads[q, part, 0] = value[:, 0]
            grads[q, part, 1] = value[:, 1]
            send(grads.at[q, part, xp], xrecv.at[q, part], sent.at[11], rf_x.at[q, part], xdev)
            return carry2

        return lax.fori_loop(0, 2, over_parts, carry)

    lax.fori_loop(0, slots, hid_near, 0)
    lax.fori_loop(0, 2, ff_near, 0)
    ff_forward(3)
    lax.fori_loop(2, 3, ff_near, 0)
    lax.fori_loop(0, slots, hid_forward, 0)
    lax.fori_loop(0, slots, hid_far, 0)
    turn_rows(hid, 0)
    ff_far(0, 0)
    grad_tile(0, 0)
    ff_near(3, 0)
    lax.fori_loop(1, 4, ff_far, 0)

    def wide_rows(part, q, t):
        return wide[q, pl.ds(t * 4, 4), :, part * 256 : (part + 1) * 256].reshape(512, 256)

    def broad(t):
        return pl.ds(pl.multiple_of(t * 512, 512), 512)

    def back_rows(left, part, t):
        total = contract_cols(left[:, 0:256], wide_rows(part, 0, t))
        for q in range(1, 4):
            total = total + contract_cols(left[:, q * 256 : (q + 1) * 256], wide_rows(part, q, t))
        return total

    def head_sum(part):
        def rows_of(hh):
            return pair[pl.ds(part * act_at + hh * slots, slots)].reshape(rows_latent, hidden)

        for slot, hh in enumerate((yp * 2 + cp, y * 2 + cp)):
            left = rows_of(hh)

            def to_core(t, carry, left=left, slot=slot):
                value = back_rows(left, part, t)
                hsend[slot, :, :, broad(t)] = value.astype(bf16).reshape(slots, queries, 512)
                return carry

            lax.fori_loop(0, width // 512, to_core, 0)
            send(hsend.at[slot], hrecv.at[part, slot], sent.at[9], hp_c.at[part, slot], cdev)
        left_y = rows_of(yp * 2 + c)
        arrived(hrecv.at[part, 0], hp_c.at[part, 0])

        def to_y(t, carry):
            value = back_rows(left_y, part, t).reshape(slots, queries, 512)
            hysend[part, :, :, broad(t)] = (value + hrecv[part, 0, :, :, broad(t)].astype(f32)).astype(bf16)
            return carry

        lax.fori_loop(0, width // 512, to_y, 0)
        send(hysend.at[part], hyrecv.at[part], sent.at[10], hp_y.at[part], ydev)
        left_own = rows_of(head)
        arrived(hrecv.at[part, 1], hp_c.at[part, 1])

        def to_own(t, carry):
            value = back_rows(left_own, part, t).reshape(slots, queries, 512)
            hown[part, :, :, broad(t)] = value + hrecv[part, 1, :, :, broad(t)].astype(f32)
            return carry

        lax.fori_loop(0, width // 512, to_own, 0)

    arrived(hid.at[0 : 3 * slots], sent.at[8])
    head_sum(0)

    def sum_tile(u):
        q, part = u // 2, u % 2
        arrived(xrecv.at[q, part], rf_x.at[q, part])
        for k, zz in enumerate((z1, z2, z3)):
            grads[q, part, x, zz] = (
                grads[q, part, x, zz].astype(f32) + xrecv[q, part, zz].astype(f32)
            ).astype(bf16)
            send(grads.at[q, part, x, zz], zrecv.at[k, part, q], sent.at[12], rf_z.at[k, part], zdev(zz))

    lax.fori_loop(1, 4, grad_tile, 0)
    sum_tile(0)
    sum_tile(1)
    arrived(hsend, sent.at[9])
    head_sum(1)
    sum_tile(2)

    gacc[...] = jnp.zeros_like(gacc)

    def tally(j, upper, xhat):
        gacc[j] += jnp.sum((upper * xhat).reshape(-1, 8, width), axis=0)
        gacc[3 + j] += jnp.sum(upper.reshape(-1, 8, width), axis=0)

    def norm_back(values, j, upper):
        xhat, inverse = statistics(values)
        tally(j, upper, xhat)
        g = upper * gain(j)
        return inverse * (
            g - jnp.mean(g, axis=-1, keepdims=True) - xhat * jnp.mean(g * xhat, axis=-1, keepdims=True)
        )

    sum_tile(3)
    arrived(hyrecv.at[0], hp_y.at[0])

    def mid_back(m, carry):
        upper = hown[0, m] + hyrecv[0, m].astype(f32)
        back = norm_back(mid_v[m], 2, upper)
        total = cotr[head * slots + m].astype(f32) + back
        hown[0, m] = total
        delta_v[m] = total.astype(bf16)
        return carry

    lax.fori_loop(0, slots, mid_back, 0)
    delta_rows = delta_v[...].reshape(rows_latent, width)

    attg_v[...] = (
        contract_cols(delta_rows, out_tile(slice(0, width))).astype(bf16).reshape(slots, queries, inner)
    )

    gslab = pair

    def gunit(ii, hh_y, hh_c):
        return ii * 4 + hh_c * 2 + hh_y

    def out_grad_step(t, carry):
        right = delta_v[:, :, broad(t)].reshape(rows_latent, 512)
        value = dot_nn(att_t[...], right).astype(bf16)
        for ii in range(8):
            for hh in range(4):
                at = (ii * 4 + hh) * 16
                gslab[gunit(ii, hh // 2, hh % 2), 32:48, broad(t)] = value[at : at + 16]
        return carry

    lax.fori_loop(0, width // 512, out_grad_step, 0)
    sum_tile(4)

    def back_pair(m, g):
        q_rows, k_media, k_latent, p_media, p_latent = probabilities(m, g)
        v_media = kv_media[m, :, tile(g + 2)]
        v_latent = kv_latent[m, :, tile(g + 2)]
        up_rows = spread(attg_v[m, :, tile(g)])
        g_media = contract_cols(up_rows, v_media)
        g_latent = contract_cols(up_rows, v_latent)
        dotted = jnp.sum(g_media * p_media, axis=-1, keepdims=True) + jnp.sum(
            g_latent * p_latent, axis=-1, keepdims=True
        )
        d_media = (p_media * (g_media - dotted)).astype(bf16)
        d_latent = (p_latent * (g_latent - dotted)).astype(bf16)
        qgrad_v[m, :, tile(g)] = fold(dot_nn(d_media, k_media) + dot_nn(d_latent, k_latent)).astype(bf16)
        kv_media[m, :, tile(g)] = contract_rows(d_media, q_rows).astype(bf16)
        kv_latent[m, :, tile(g)] = contract_rows(d_latent, q_rows).astype(bf16)
        kv_media[m, :, tile(g + 2)] = contract_rows(p_media.astype(bf16), up_rows).astype(bf16)
        kv_latent[m, :, tile(g + 2)] = contract_rows(p_latent.astype(bf16), up_rows).astype(bf16)

    def back_image(m, carry):
        back_pair(m, 0)
        back_pair(m, 1)
        return carry

    lax.fori_loop(0, slots, back_image, 0)

    sum_tile(5)

    gcr = hid
    gyr_v = media_n

    def kv_grad_chunk(zz):
        rows = pl.ds(pl.multiple_of(zz * 256, 256), 256)
        left_media = media_t[rows, :]
        left_latent = latent_t[rows, :]

        value = dot_nn(left_media, kv_media[...].reshape(groups * 256, width)) + dot_nn(
            left_latent, kv_latent[...].reshape(rows_latent, width)
        )
        value = value.astype(bf16)
        value_q = dot_nn(left_latent, qgrad_v[...].reshape(rows_latent, inner)) * scale
        value_q = value_q.astype(bf16)
        for xx in range(2):
            for hh in range(4):
                at = (xx * 4 + hh) * 32
                uu = gunit(zz * n_x + xx, hh // 2, hh % 2)
                gslab[uu, 0:32, :] = value[at : at + 32]
                gslab[uu, 48:64, 0:inner] = value_q[at : at + 16]
                gslab[uu, 48:64, inner:width] = value_q[at + 16 : at + 32]
        for xx in range(2):
            ii = zz * n_x + xx
            send(
                gslab.at[pl.ds(ii * 4 + cp * 2, 2)],
                gcr.at[pl.ds(ii * 2, 2)],
                sent.at[13],
                ra_c.at[ii],
                cdev,
            )

    def stage_y(zz):
        for xx in range(2):
            ii = zz * n_x + xx
            arrived(gcr.at[pl.ds(ii * 2, 2)], ra_c.at[ii])
            uu = gunit(ii, yp, c)
            gslab[uu] = (gslab[uu].astype(f32) + gcr[ii * 2 + yp].astype(f32)).astype(bf16)
            send(gslab.at[uu], gyr_v.at[ii], sent.at[14], ra_y.at[ii], ydev)

    def upto_y(ii):
        return (
            gslab[gunit(ii, y, c)].astype(f32) + gcr[ii * 2 + y].astype(f32) + gyr_v[ii].astype(f32)
        )

    def stage_x(zz):
        ii = zz * n_x + xp
        arrived(gyr_v.at[ii], ra_y.at[ii])
        uu = gunit(ii, y, c)
        gslab[uu] = upto_y(ii).astype(bf16)
        send(gslab.at[uu], gyr_v.at[8 + zz], sent.at[15], ra_x.at[zz], xdev)

    def stage_z(zz, last):
        ii = zz * n_x + x
        arrived(gyr_v.at[ii], ra_y.at[ii])
        arrived(gyr_v.at[8 + zz], ra_x.at[zz])
        if last:
            return upto_y(ii) + gyr_v[8 + zz].astype(f32)
        uu = gunit(ii, y, c)
        gslab[uu] = (upto_y(ii) + gyr_v[8 + zz].astype(f32)).astype(bf16)
        send(gslab.at[uu], gzr_v.at[z], sent.at[16], ra_z.at[z], zdev(zz))
        return None

    chunk = [zat(1), zat(3), zat(2), z]
    kv_grad_chunk(chunk[0])
    kv_grad_chunk(chunk[1])
    stage_y(chunk[0])
    kv_grad_chunk(chunk[2])
    stage_y(chunk[1])
    kv_grad_chunk(chunk[3])
    stage_y(chunk[2])
    sum_tile(6)

    arrived(hyrecv.at[1], hp_y.at[1])
    new_v = delta_v

    for m in range(slots):
        keep = jnp.clip(filled - m, 0, 1).astype(f32)
        for r in range(2):
            rows = slice(r * half, (r + 1) * half)
            branch = hown[1, m, rows, :] + hyrecv[1, m, rows, :].astype(f32)
            new_v[m, rows, :] = ((mid_v[m, rows, :] + branch) * keep).astype(bf16)
    new_copy = pltpu.make_async_copy(new_v, new_out, outs.at[0])
    new_copy.start()
    stage_y(chunk[3])

    def media_back(m, carry):
        hown[1, 0:4] = contract_cols(kv_media[m], kv_tile(slice(0, width))).reshape(4, 64, width)

        def over_rows(r, carry2):
            block = m * 4 + r
            back = norm_back(media_v[block].astype(f32), 0, hown[1, r])
            media_v[block] = back.astype(bf16)
            return carry2

        lax.fori_loop(0, 4, over_rows, 0)
        pltpu.make_async_copy(media_v.at[pl.ds(m * 4, 4)], media_out.at[pl.ds(m * 4, 4)], outs.at[1]).start()
        return carry

    def latent_back_tiles(t, carry):
        weight = slab[pl.ds(t * 16, 16), 0:32, :].reshape(512, width)
        query_weight = query_full[pl.ds(t * 16, 16)].reshape(512, inner)
        hown[1, :, :, broad(t)] = (
            contract_cols(kv_latent[...].reshape(rows_latent, width), weight)
            + contract_cols(qgrad_v[...].reshape(rows_latent, inner), query_weight) * scale
        ).reshape(slots, queries, 512)
        return carry

    def latent_back(m, carry):
        back = norm_back(latent_v[m].astype(f32), 1, hown[1, m])
        latent_v[m] = (hown[0, m] + back).astype(bf16)
        return carry

    lax.fori_loop(0, width // 512, latent_back_tiles, 0)
    lax.fori_loop(0, slots, latent_back, 0)
    latent_copy = pltpu.make_async_copy(latent_v, latent_out, outs.at[2])
    latent_copy.start()
    lax.fori_loop(0, 2, media_back, 0)
    sum_tile(7)
    stage_x(chunk[0])
    stage_x(chunk[1])
    lax.fori_loop(2, 4, media_back, 0)
    stage_x(chunk[2])
    stage_z(chunk[0], False)
    stage_z(chunk[1], False)
    lax.fori_loop(4, 5, media_back, 0)
    stage_x(chunk[3])
    stage_z(chunk[2], False)

    for j in range(6):
        gsend[0, j : j + 1, :] = jnp.sum(gacc[j], axis=0, keepdims=True)
    gsend[0, 6:8, :] = jnp.zeros((2, width), f32)
    send(gsend.at[0], gyr.at[0], sent.at[17], gr_c.at[0], cdev)
    arrived(gyr.at[0], gr_c.at[0])
    gsend[1] = gsend[0] + gyr[0]
    send(gsend.at[1], gyr.at[1], sent.at[17], gr_c.at[1], ydev)
    arrived(gyr.at[1], gr_c.at[1])
    gsend[2] = gsend[1] + gyr[1]
    send(gsend.at[2], gyr.at[2], sent.at[17], gr_c.at[2], xdev)
    arrived(gyr.at[2], gr_c.at[2])
    gsend[3] = gsend[2] + gyr[2]
    for k in near:
        zz = zat(k)
        send(gsend.at[3, :, lanes(zz * n_x + x)], gzr.at[z], sent.at[18], gr_z.at[z], zdev(zz))
    total = gsend[3, :, lanes(img)]
    for k in near:
        zz = zat(k)
        arrived(gzr.at[zz], gr_z.at[zz])
        total = total + gzr[zz]
    norm_out[...] = total

    for part in range(2):
        for k in range(3):
            arrived(zrecv.at[k, part], rf_z.at[k, part])

    def own_sum(part, q):
        value = grads[q, part, x, z].astype(f32) + xrecv[q, part, z].astype(f32)
        for k in range(3):
            value = value + zrecv[k, part, q].astype(f32)
        return value

    def last_sums(q, carry):
        up_out[:, tile(q)] = own_sum(0, q)
        value = own_sum(1, q)
        for j in range(2):
            rows = pl.ds(pl.multiple_of(q * 256 + j * 128, 128), 128)
            down_out[rows, :] = tpose(value[:, j * 128 : (j + 1) * 128])
        return carry

    lax.fori_loop(0, hidden // 256, last_sums, 0)

    final = stage_z(chunk[3], True)
    for k in near:
        zz = zat(k)
        arrived(gzr_v.at[zz], ra_z.at[zz])
        final = final + gzr_v[zz].astype(f32)
    key_value_out[...] = final[0:32]
    output_out[...] = final[32:48]
    query_out[0:16, :] = final[48:64, 0:inner]
    query_out[16:32, :] = final[48:64, inner:width]

    new_copy.wait()
    latent_copy.wait()
    arrived(media_v, outs.at[1])
    arrived(normg.at[0, :, 0:384], sent.at[0])
    arrived(slab.at[0:29], sent.at[1])

    @pl.when(mid)
    def _():
        arrived(slab.at[0:4], sent.at[1])
        arrived(wide.at[0], sent.at[5])

    arrived(normg.at[0, :, 0:512], sent.at[2])
    arrived(normg.at[0], sent.at[3])
    arrived(normg.at[0:2], sent.at[4])
    arrived(wide.at[0], sent.at[5])
    arrived(wide.at[0:2], sent.at[6])
    arrived(cotr.at[0 : 3 * slots], sent.at[7])
    arrived(hsend, sent.at[9])
    arrived(hysend, sent.at[10])
    arrived(xrecv, sent.at[11])
    arrived(zrecv, sent.at[12])
    arrived(gcr.at[0:16], sent.at[13])
    arrived(gyr_v.at[0:8], sent.at[14])
    arrived(gyr_v.at[0:4], sent.at[15])
    arrived(gyr_v.at[0:3], sent.at[16])
    arrived(gyr, sent.at[17])
    arrived(gzr.at[0:3], sent.at[18])


def finish_kernel(norms, *refs):
    gains_out, biases_out = refs[8:10]
    sources, targets, stage = refs[:8], refs[10:18], refs[18:26]
    sem_in, sem_out = refs[26:28]
    part = gains_out.shape[1]
    head = lax.axis_index("head")
    pieces = []
    for i in range(8):
        rows = sources[i].shape[0]
        count = 4 if rows % 4 == 0 and i == 1 else 1
        size = rows // count
        for j in range(count):
            at = slice(j * size, (j + 1) * size)
            pieces.append(
                (
                    pltpu.make_async_copy(sources[i].at[at], stage[i].at[at], sem_in.at[i, j]),
                    pltpu.make_async_copy(stage[i].at[at], targets[i].at[at], sem_out.at[i, j]),
                )
            )
    for read, write in pieces:
        read.start()
    rolled = pltpu.roll(norms[...], (128 - head * part) % 128, 1)
    gains_out[...] = rolled[0:3, 0:part]
    biases_out[...] = rolled[3:6, 0:part]
    for read, write in pieces:
        read.wait()
        write.start()
    for read, write in pieces:
        write.wait()


def block_plan(
    media_patches,
    latent_rows,
    media_counts,
    norm_gains,
    norm_biases,
    query_weight,
    key_value_weight,
    output_weight,
    up_weight,
    down_weight,
    cotangent,
):
    slots, patches, width = media_patches.shape[1:]
    queries = latent_rows.shape[2]
    inner = query_weight.shape[1]
    hidden = up_weight.shape[1]
    rows_up = up_weight.shape[0]
    part = norm_gains.shape[1]
    blocks = slots * patches // 64
    bf16, f32 = jnp.bfloat16, jnp.float32
    shape = jax.ShapeDtypeStruct
    hbm = pl.BlockSpec(memory_space=pl.ANY)
    vmem = pl.BlockSpec(memory_space=pltpu.VMEM)
    smem = pl.BlockSpec(memory_space=pltpu.SMEM)
    dma = pltpu.SemaphoreType.DMA
    all_rows = 4 * slots * queries
    rows_latent = slots * queries
    outs = pl.pallas_call(
        block_kernel,
        out_shape=(
            shape((slots, queries, width), bf16),
            shape((blocks, 64, width), bf16),
            shape((slots, queries, width), bf16),
            shape((8, 128), f32),
            shape(query_weight.shape, f32),
            shape(key_value_weight.shape, f32),
            shape(output_weight.shape, f32),
            shape(up_weight.shape, f32),
            shape(down_weight.shape, f32),
        ),
        in_specs=[smem] + [hbm] * 7 + [vmem] * 3,
        out_specs=(hbm, hbm, hbm, vmem, vmem, vmem, vmem, vmem, vmem),
        scratch_shapes=[
            pltpu.VMEM((32, 64, width), bf16),
            pltpu.VMEM((32, 2, 16, inner), bf16),
            pltpu.VMEM((4, 8, rows_up, 512), bf16),
            pltpu.VMEM((4 * slots, queries, width), bf16),
            pltpu.VMEM((4 * slots, queries, width), bf16),
            pltpu.VMEM((2, width, all_rows), bf16),
            pltpu.VMEM((blocks, 64, width), bf16),
            pltpu.VMEM((blocks, 64, width), bf16),
            pltpu.VMEM((slots, queries, width), bf16),
            pltpu.VMEM((slots, queries, width), bf16),
            pltpu.VMEM((width, slots * patches), bf16),
            pltpu.VMEM((width, rows_latent), bf16),
            pltpu.VMEM((slots, patches, 2 * inner), bf16),
            pltpu.VMEM((slots, queries, 2 * inner), bf16),
            pltpu.VMEM((slots, queries, inner), bf16),
            pltpu.VMEM((slots, queries, inner), bf16),
            pltpu.VMEM((inner, rows_latent), bf16),
            pltpu.VMEM((slots, queries, width), f32),
            pltpu.VMEM((8 * slots, queries, width), bf16),
            pltpu.VMEM((4, 2, 2, 4, rows_up, 256), bf16),
            pltpu.VMEM((4, 2, 4, rows_up, 256), bf16),
            pltpu.VMEM((3, 2, 4, rows_up, 256), bf16),
            pltpu.VMEM((2, slots, queries, width), bf16),
            pltpu.VMEM((2, 2, slots, queries, width), bf16),
            pltpu.VMEM((2, slots, queries, width), bf16),
            pltpu.VMEM((2, slots, queries, width), bf16),
            pltpu.VMEM((2, slots, queries, width), f32),
            pltpu.VMEM((slots, queries, width), bf16),
            pltpu.VMEM((slots, queries, inner), bf16),
            pltpu.VMEM((slots, queries, inner), bf16),
            pltpu.VMEM((4, 8, width), f32),
            pltpu.VMEM((8, width), f32),
            pltpu.VMEM((6, 8, width), f32),
            pltpu.VMEM((4, 8, width), f32),
            pltpu.VMEM((3, 8, width), f32),
            pltpu.VMEM((4, 8, 128), f32),
            pltpu.VMEM((4, 64, width), bf16),
            dma((11,)),
            dma((4, 2)),
            dma((1,)),
            dma((8,)),
            dma((8, 2)),
            dma((4, 4)),
            dma((4, 4)),
            dma((4,)),
            dma((4,)),
            dma((1,)),
            dma((2,)),
            dma((slots,)),
            dma((slots,)),
            dma((slots,)),
            dma((1,)),
            dma((2,)),
            dma((2, 2)),
            dma((2,)),
            dma((4, 2)),
            dma((4, 2)),
            dma((8,)),
            dma((8,)),
            dma((4,)),
            dma((4,)),
            dma((3,)),
            dma((4,)),
            dma((19,)),
            dma((3,)),
        ],
        compiler_params=pltpu.CompilerParams(
            collective_id=0, has_side_effects=True, vmem_limit_bytes=67043328
        ),
    )(
        media_counts,
        media_patches.reshape(blocks, 64, width),
        latent_rows.reshape(slots, queries, width),
        cotangent.reshape(slots, queries, width),
        query_weight,
        key_value_weight,
        output_weight,
        up_weight,
        down_weight,
        norm_gains,
        norm_biases,
    )
    norms = outs[3]
    rest = outs[:3] + outs[4:]
    done = pl.pallas_call(
        finish_kernel,
        out_shape=(shape((3, part), f32), shape((3, part), f32)) + tuple(shape(v.shape, v.dtype) for v in rest),
        in_specs=[vmem] + [hbm] * 8,
        out_specs=(vmem, vmem) + (hbm,) * 8,
        scratch_shapes=[pltpu.VMEM(v.shape, v.dtype) for v in rest] + [dma((8, 4)), dma((8, 4))],
        compiler_params=pltpu.CompilerParams(vmem_limit_bytes=67043328),
    )(norms, *rest)
    gains_grad, biases_grad, new, media_grad, latent_grad = done[:5]
    return (
        new.reshape(latent_rows.shape),
        media_grad.reshape(media_patches.shape),
        latent_grad.reshape(latent_rows.shape),
        gains_grad,
        biases_grad,
    ) + tuple(done[5:])


def block_fits(mesh):
    return mesh.shape["img"] == 8 and mesh.shape["head"] == 4


def solution(mesh):
    return jax.shard_map(
        block_plan if block_fits(mesh) else gathered_plan,
        mesh=mesh,
        in_specs=(
            P(("img", "head"), None, None, None),
            P(("img", "head"), None, None, None),
            P(("img", "head")),
            P(None, ("img", "head")),
            P(None, ("img", "head")),
            P(("img", "head"), None),
            P(("img", "head"), None),
            P(("img", "head"), None),
            P("img", "head"),
            P("head", "img"),
            P(("img", "head"), None, None, None),
        ),
        out_specs=(
            P(("img", "head"), None, None, None),
            P(("img", "head"), None, None, None),
            P(("img", "head"), None, None, None),
            P(None, ("img", "head")),
            P(None, ("img", "head")),
            P(("img", "head"), None),
            P(("img", "head"), None),
            P(("img", "head"), None),
            P("img", "head"),
            P("head", "img"),
        ),
        check_vma=False,
    )
```

```python
import jax
import jax.numpy as jnp
from jax import lax
from jax.experimental import pallas as pl
from jax.experimental.pallas import tpu as pltpu
from jax.sharding import PartitionSpec as P

HEADS = 8


def layer_norm(values, norm_gain, norm_shift):
    centered = values - jnp.mean(values, axis=-1, keepdims=True)
    variance = jnp.mean(centered * centered, axis=-1, keepdims=True)
    return centered * lax.rsqrt(variance + 1e-05) * norm_gain + norm_shift


def norm_backward(values, norm_gain, norm_shift, upstream):
    primal, pullback = jax.vjp(layer_norm, values, norm_gain, norm_shift)
    return pullback(upstream)


def exact_gelu(values):
    return jax.nn.gelu(values, approximate=False)


def gelu_backward(values, upstream):
    primal, pullback = jax.vjp(exact_gelu, values)
    return pullback(upstream)[0]


def contract_rows(left_side, right_side):
    return lax.dot_general(
        left_side, right_side, (((0,), (0,)), ((), ())), preferred_element_type=jnp.float32
    )


def contract_cols(left_side, right_side):
    return lax.dot_general(
        left_side, right_side, (((1,), (1,)), ((), ())), preferred_element_type=jnp.float32
    )


def gathered_plan(
    media_patches,
    latent_rows,
    media_counts,
    norm_gains,
    norm_biases,
    query_weight,
    key_value_weight,
    output_weight,
    up_weight,
    down_weight,
    cotangent,
):
    samp_local, media_slots, patches, model_width = media_patches.shape
    queries_per = latent_rows.shape[2]
    images = samp_local * media_slots
    keys_per = patches + queries_per
    rows_local = images * queries_per
    gathered = (
        lax.all_gather(query_weight, ("img", "head"), axis=0, tiled=True),
        lax.all_gather(key_value_weight, ("img", "head"), axis=0, tiled=True),
        lax.all_gather(output_weight, ("img", "head"), axis=0, tiled=True),
        lax.all_gather(norm_gains, ("img", "head"), axis=1, tiled=True),
        lax.all_gather(norm_biases, ("img", "head"), axis=1, tiled=True),
    )
    query_full, key_value_full, output_full, gains_low, biases_low = gathered
    norm_gain = gains_low.astype(jnp.float32)
    norm_shift = biases_low.astype(jnp.float32)
    inner_width = query_full.shape[1]
    head_size = inner_width // HEADS
    score_scale = head_size ** (-0.5)
    up_part, down_part = (
        lax.all_gather(up_weight, "img", axis=0, tiled=True),
        lax.all_gather(down_weight, "img", axis=1, tiled=True),
    )
    media_full = media_patches.reshape(images, patches, model_width).astype(jnp.float32)
    latent_full = latent_rows.reshape(images, queries_per, model_width).astype(jnp.float32)
    media_norm = layer_norm(media_full, norm_gain[0], norm_shift[0]).astype(jnp.bfloat16)
    latent_norm = layer_norm(latent_full, norm_gain[1], norm_shift[1]).astype(jnp.bfloat16)
    query_rows = (
        jnp.einsum("ild,de->ile", latent_norm, query_full, preferred_element_type=jnp.float32)
        * score_scale
    ).astype(jnp.bfloat16)
    key_input = jnp.concatenate([media_norm, latent_norm], axis=1)
    key_value_rows = jnp.einsum(
        "ikd,de->ike", key_input, key_value_full, preferred_element_type=jnp.float32
    ).astype(jnp.bfloat16)
    query_heads = (
        query_rows.reshape(images, queries_per, HEADS, head_size)
        .transpose(2, 0, 1, 3)
        .reshape(HEADS, images, queries_per * head_size)
    )
    key_value_heads = (
        key_value_rows.reshape(images, keys_per, 2, HEADS, head_size)
        .transpose(3, 0, 1, 2, 4)
        .reshape(HEADS, images, keys_per, 2 * head_size)
    )
    query_group, key_value_group = (
        lax.all_to_all(query_heads, "head", split_axis=0, concat_axis=1, tiled=True),
        lax.all_to_all(key_value_heads, "head", split_axis=0, concat_axis=1, tiled=True),
    )
    heads_dev = query_group.shape[0]
    group_images = query_group.shape[1]
    query_block = query_group.reshape(heads_dev, group_images, queries_per, head_size)
    key_block = key_value_group[:, :, :, :head_size]
    value_block = key_value_group[:, :, :, head_size:]
    scores = jnp.einsum(
        "hgqe,hgke->hgqk", query_block, key_block, preferred_element_type=jnp.float32
    )
    row_max = jnp.max(scores, axis=-1, keepdims=True)
    weights = jnp.exp(scores - row_max)
    totals = jnp.sum(weights, axis=-1, keepdims=True)
    log_total = row_max + jnp.log(totals)
    probabilities = (weights / totals).astype(jnp.bfloat16)
    attended = jnp.einsum(
        "hgqk,hgke->hgqe", probabilities, value_block, preferred_element_type=jnp.float32
    ).astype(jnp.bfloat16)
    attended_back = lax.all_to_all(
        attended.reshape(heads_dev, group_images, queries_per * head_size),
        "head",
        split_axis=1,
        concat_axis=0,
        tiled=True,
    )
    attended_local = (
        attended_back.reshape(HEADS, images, queries_per, head_size)
        .transpose(1, 2, 0, 3)
        .reshape(images, queries_per, inner_width)
    )
    attn_delta = jnp.einsum(
        "ile,ed->ild", attended_local, output_full, preferred_element_type=jnp.float32
    )
    mid_latent = latent_full + attn_delta
    hidden_in = (
        layer_norm(mid_latent, norm_gain[2], norm_shift[2])
        .astype(jnp.bfloat16)
        .reshape(rows_local, model_width)
    )
    slot_mask = (
        (jnp.arange(media_slots)[None, :] < media_counts[:, None])
        .astype(jnp.float32)
        .reshape(images, 1, 1)
    )
    up_full, down_full = (
        lax.all_gather(up_part, "head", axis=1, tiled=True),
        lax.all_gather(down_part, "head", axis=0, tiled=True),
    )
    pre_act = jnp.dot(hidden_in, up_full, preferred_element_type=jnp.float32)
    act_low = exact_gelu(pre_act).astype(jnp.bfloat16)
    branch_out = jnp.dot(act_low, down_full, preferred_element_type=jnp.float32)
    result = slot_mask * (mid_latent + branch_out.reshape(images, queries_per, model_width))
    new_latents = result.astype(jnp.bfloat16).reshape(latent_rows.shape)
    out_grad = slot_mask * cotangent.reshape(images, queries_per, model_width).astype(jnp.float32)
    branch_grad = out_grad.astype(jnp.bfloat16).reshape(rows_local, model_width)
    act_grad = contract_cols(branch_grad, down_full)
    pre_grad = gelu_backward(pre_act, act_grad).astype(jnp.bfloat16)
    down_grad_whole = contract_rows(act_low, branch_grad)
    up_grad_whole = contract_rows(hidden_in, pre_grad)
    hidden_grad = contract_cols(pre_grad, up_full)
    up_grad_part, down_grad_part = (
        lax.psum_scatter(
            up_grad_whole.astype(jnp.bfloat16), "head", scatter_dimension=1, tiled=True
        ).astype(jnp.float32),
        lax.psum_scatter(
            down_grad_whole.astype(jnp.bfloat16), "head", scatter_dimension=0, tiled=True
        ).astype(jnp.float32),
    )
    up_grad, down_grad = (
        lax.psum_scatter(
            up_grad_part.astype(jnp.bfloat16), "img", scatter_dimension=0, tiled=True
        ).astype(jnp.float32),
        lax.psum_scatter(
            down_grad_part.astype(jnp.bfloat16), "img", scatter_dimension=1, tiled=True
        ).astype(jnp.float32),
    )
    mid_from_norm, gain_ff, bias_ff = norm_backward(
        mid_latent,
        norm_gain[2],
        norm_shift[2],
        hidden_grad.reshape(images, queries_per, model_width),
    )
    mid_grad = out_grad + mid_from_norm
    delta_low = mid_grad.astype(jnp.bfloat16)
    output_weight_grad = jnp.einsum(
        "ile,ild->ed", attended_local, delta_low, preferred_element_type=jnp.float32
    )
    attended_grad = jnp.einsum(
        "ild,ed->ile", delta_low, output_full, preferred_element_type=jnp.float32
    ).astype(jnp.bfloat16)
    grad_heads = (
        attended_grad.reshape(images, queries_per, HEADS, head_size)
        .transpose(2, 0, 1, 3)
        .reshape(HEADS, images, queries_per * head_size)
    )
    grad_group = lax.all_to_all(
        grad_heads, "head", split_axis=0, concat_axis=1, tiled=True
    ).reshape(heads_dev, group_images, queries_per, head_size)
    scores_again = jnp.einsum(
        "hgqe,hgke->hgqk", query_block, key_block, preferred_element_type=jnp.float32
    )
    probs_again = jnp.exp(scores_again - log_total)
    probs_again_low = probs_again.astype(jnp.bfloat16)
    prob_grad = jnp.einsum(
        "hgqe,hgke->hgqk", grad_group, value_block, preferred_element_type=jnp.float32
    )
    value_grad = jnp.einsum(
        "hgqk,hgqe->hgke", probs_again_low, grad_group, preferred_element_type=jnp.float32
    )
    row_dot = jnp.sum(prob_grad * probs_again, axis=-1, keepdims=True)
    score_grad = (probs_again * (prob_grad - row_dot)).astype(jnp.bfloat16)
    query_grad_group = jnp.einsum(
        "hgqk,hgke->hgqe", score_grad, key_block, preferred_element_type=jnp.float32
    ).astype(jnp.bfloat16)
    key_grad = jnp.einsum(
        "hgqk,hgqe->hgke", score_grad, query_block, preferred_element_type=jnp.float32
    )
    key_value_grad_group = jnp.concatenate([key_grad, value_grad], axis=-1).astype(jnp.bfloat16)
    query_back, key_value_back = (
        lax.all_to_all(
            query_grad_group.reshape(heads_dev, group_images, queries_per * head_size),
            "head",
            split_axis=1,
            concat_axis=0,
            tiled=True,
        ),
        lax.all_to_all(key_value_grad_group, "head", split_axis=1, concat_axis=0, tiled=True),
    )
    query_local = (
        query_back.reshape(HEADS, images, queries_per, head_size)
        .transpose(1, 2, 0, 3)
        .reshape(images, queries_per, inner_width)
    )
    key_value_local = (
        key_value_back.reshape(HEADS, images, keys_per, 2, head_size)
        .transpose(1, 2, 3, 0, 4)
        .reshape(images, keys_per, 2 * inner_width)
    )
    query_weight_grad = (
        jnp.einsum("ild,ile->de", latent_norm, query_local, preferred_element_type=jnp.float32)
        * score_scale
    )
    key_value_weight_grad = jnp.einsum(
        "ikd,ike->de", key_input, key_value_local, preferred_element_type=jnp.float32
    )
    key_input_grad = jnp.einsum(
        "ike,de->ikd", key_value_local, key_value_full, preferred_element_type=jnp.float32
    )
    latent_norm_grad = (
        jnp.einsum("ile,de->ild", query_local, query_full, preferred_element_type=jnp.float32)
        * score_scale
        + key_input_grad[:, patches:]
    )
    media_grad_full, gain_media, bias_media = norm_backward(
        media_full, norm_gain[0], norm_shift[0], key_input_grad[:, :patches]
    )
    latent_from_norm, gain_latent, bias_latent = norm_backward(
        latent_full, norm_gain[1], norm_shift[1], latent_norm_grad
    )
    latent_grad_full = mid_grad + latent_from_norm
    gain_terms = jnp.stack([gain_media, gain_latent, gain_ff])
    bias_terms = jnp.stack([bias_media, bias_latent, bias_ff])
    summed = (
        lax.psum_scatter(query_weight_grad, ("img", "head"), scatter_dimension=0, tiled=True),
        lax.psum_scatter(key_value_weight_grad, ("img", "head"), scatter_dimension=0, tiled=True),
        lax.psum_scatter(output_weight_grad, ("img", "head"), scatter_dimension=0, tiled=True),
        lax.psum_scatter(gain_terms, ("img", "head"), scatter_dimension=1, tiled=True),
        lax.psum_scatter(bias_terms, ("img", "head"), scatter_dimension=1, tiled=True),
    )
    media_grad = media_grad_full.astype(jnp.bfloat16).reshape(media_patches.shape)
    latent_grad = latent_grad_full.astype(jnp.bfloat16).reshape(latent_rows.shape)
    return (
        new_latents,
        media_grad,
        latent_grad,
        summed[3],
        summed[4],
        summed[0],
        summed[1],
        summed[2],
        up_grad,
        down_grad,
    )


def tpose(values):
    return jnp.transpose(values, (1, 0))


def dot_nn(left_side, right_side):
    return jnp.dot(left_side, right_side, preferred_element_type=jnp.float32)


def block_kernel(
    counts,
    media_in,
    latent_in,
    cot_in,
    query_in,
    key_value_in,
    output_in,
    up_in,
    down_in,
    gain_in,
    bias_in,
    delta_v,
    media_v,
    latent_v,
    norm_out,
    query_out,
    key_value_out,
    output_out,
    up_out,
    down_out,
    slab,
    query_full,
    wide,
    hid,
    cotr,
    turned,
    media_n,
    latent_n,
    media_t,
    latent_t,
    kv_media,
    kv_latent,
    query_v,
    att_v,
    att_t,
    mid_v,
    pair,
    grads,
    xrecv,
    zrecv,
    hsend,
    hrecv,
    hysend,
    hyrecv,
    hown,
    attg_v,
    qgrad_v,
    normg,
    normv,
    gacc,
    gsend,
    gyr,
    gzr,
    gzr_v,
    loc,
    at_z,
    at_x,
    at_y,
    at_c,
    ff_z,
    ff_x,
    nb_z,
    nb_x,
    nb_y,
    nb_c,
    hd_y,
    hd_c,
    hd_f,
    bg_y,
    bg_c,
    hp_c,
    hp_y,
    rf_x,
    rf_z,
    ra_c,
    ra_y,
    ra_x,
    ra_z,
    gr_c,
    gr_z,
    sent,
):
    n_z, n_x, n_head = 4, 2, 4
    img = lax.axis_index("img")
    head = lax.axis_index("head")
    z = img // n_x
    x = img % n_x
    y = head // 2
    c = head % 2
    xp, yp, cp = 1 - x, 1 - y, 1 - c
    xdev = (z * n_x + xp, head)
    ydev = (img, yp * 2 + c)
    cdev = (img, y * 2 + cp)
    near = (1, 3, 2)
    z1 = z + 1 - 2 * (z % 2)
    z2 = (z + 2) % n_z
    z3 = n_z - 1 - z
    mid = jnp.logical_and(z >= 1, z <= 2)

    def zat(k):
        return (z + k) % n_z

    def zdev(zz):
        return (zz * n_x + x, head)

    width = media_v.shape[2]
    slots = latent_v.shape[0]
    queries = latent_v.shape[1]
    hidden = up_in.shape[1]
    inner = query_full.shape[3]
    f32 = jnp.float32
    bf16 = jnp.bfloat16
    scale = (inner // HEADS) ** (-0.5)

    def rcopy(src, dst, sem_s, sem_r, dev):
        return pltpu.make_async_remote_copy(
            src_ref=src,
            dst_ref=dst,
            send_sem=sem_s,
            recv_sem=sem_r,
            device_id=dev,
            device_id_type=pl.DeviceIdType.MESH,
        )

    def send(src, dst, sem_s, sem_r, dev):
        rcopy(src, dst, sem_s, sem_r, dev).start()

    def arrived(ref, sem):
        pltpu.make_async_copy(ref, ref, sem).wait()

    unit = img * n_head + head
    local = [
        pltpu.make_async_copy(key_value_in, slab.at[unit, 0:32], loc.at[0]),
        pltpu.make_async_copy(output_in, slab.at[unit, 32:48], loc.at[1]),
        pltpu.make_async_copy(query_in.at[0:16], slab.at[unit, 48:64, 0:inner], loc.at[2]),
        pltpu.make_async_copy(query_in.at[16:32], slab.at[unit, 48:64, inner:width], loc.at[3]),
        pltpu.make_async_copy(up_in.at[:, 0:256], wide.at[0, img, :, 0:256], loc.at[4]),
        pltpu.make_async_copy(cot_in, pair.at[0:slots], loc.at[5]),
        pltpu.make_async_copy(latent_in, latent_v, loc.at[6]),
        pltpu.make_async_copy(media_in, media_v, loc.at[7]),
    ] + [
        pltpu.make_async_copy(
            up_in.at[:, q * 256 : (q + 1) * 256], wide.at[q, img, :, 0:256], loc.at[7 + q]
        )
        for q in range(1, 4)
    ]
    for copy in local:
        copy.start()

    barrier = pltpu.get_barrier_semaphore()
    peers = [zdev(zat(k)) for k in near] + [xdev, ydev, cdev]
    for dev in peers:
        pl.semaphore_signal(barrier, inc=1, device_id=dev, device_id_type=pl.DeviceIdType.MESH)
    pl.semaphore_wait(barrier, len(peers))

    def lanes(ii):
        return pl.ds(pl.multiple_of(ii * 128, 128), 128)

    part = gain_in.shape[1]
    norm_own = normg.at[head, :, lanes(img)]
    normv[:, 0:128] = jnp.zeros((8, 128), f32)
    normv[0:3, 0:part] = gain_in[...].astype(f32)
    normv[3:6, 0:part] = bias_in[...].astype(f32)
    norm_own[...] = pltpu.roll(normv[:, 0:128], head * part, 1)
    for k in near:
        send(norm_own, norm_own, sent.at[0], nb_z.at[z], zdev(zat(k)))
    for copy in local[0:4]:
        copy.wait()

    def put_slab(uu, sem, dev):
        send(slab.at[uu], slab.at[uu], sent.at[1], sem, dev)

    def put_line(ii):
        uu = ii * n_head + head
        put_slab(uu, at_z.at[z, ii % n_x], zdev(z2))
        put_slab(uu, at_z.at[z, ii % n_x], zdev(z1))

        @pl.when(mid)
        def _():
            put_slab(uu, at_z.at[z, ii % n_x], zdev(z3))

    def put_chip(ii):
        uu = ii * n_head + head
        put_slab(uu, at_y.at[ii], ydev)
        put_slab(uu, at_c.at[ii, y], cdev)

    put_slab(unit, at_x.at[0], xdev)
    put_line(img)
    put_chip(img)

    for copy in [local[4]] + local[8:11]:
        copy.wait()
    down = down_in[...]
    for j in range(hidden // 128):
        at = 256 + (j % 2) * 128
        wide[j // 2, img, :, at : at + 128] = tpose(down[j * 128 : (j + 1) * 128, :])

    local[5].wait()
    filled = counts[0]
    for m in range(slots):
        keep = jnp.clip(filled - m, 0, 1).astype(f32)
        cotr[head * slots + m] = (pair[m].astype(f32) * keep).astype(bf16)

    def nb_wait(kind, idx, ref):
        arrived(ref, kind.at[idx])

    for k in near:
        zz = zat(k)
        arrived(normg.at[head, :, lanes(zz * n_x + x)], nb_z.at[zz])
    for k in (0,) + near:
        zz = zat(k)
        ii = zz * n_x + x
        send(normg.at[head, :, lanes(ii)], normg.at[head, :, lanes(ii)], sent.at[2], nb_x.at[zz], xdev)

    def at_forward_x():
        ii = z * n_x + xp
        arrived(slab.at[ii * n_head + head], at_x.at[0])
        put_line(ii)
        put_chip(ii)

    def at_forward_z(zz, xx, onward):
        ii = zz * n_x + xx
        uu = ii * n_head + head
        arrived(slab.at[uu], at_z.at[zz, xx])
        if onward:

            @pl.when(mid)
            def _():
                put_slab(uu, at_z.at[zz, xx], zdev(z1))

        put_chip(ii)

    def at_forward_y(ii):
        uu = ii * n_head + yp * 2 + c
        arrived(slab.at[uu], at_y.at[ii])
        put_slab(uu, at_c.at[ii, yp], cdev)

    def ff_unit(q, ii):
        return wide.at[q, ii]

    def ff_own_z(q):
        piece = ff_unit(q, img)
        send(piece, piece, sent.at[5], ff_z.at[z, q], zdev(z2))
        send(piece, piece, sent.at[5], ff_z.at[z, q], zdev(z1))

        @pl.when(mid)
        def _():
            send(piece, piece, sent.at[5], ff_z.at[z, q], zdev(z3))

    def ff_own_x(q):
        piece = ff_unit(q, img)
        send(piece, piece, sent.at[6], ff_x.at[z, q], xdev)

    def ff_forward(e):
        q, k = e // 3, e % 3
        zz = (z2 * (2 - k) * (1 - k) + z1 * 2 * k * (2 - k) + z3 * k * (k - 1)) // 2
        piece = ff_unit(q, zz * n_x + x)
        arrived(piece, ff_z.at[zz, q])

        @pl.when(jnp.logical_and(mid, k == 0))
        def _():
            send(piece, piece, sent.at[5], ff_z.at[zz, q], zdev(z1))

        send(piece, piece, sent.at[6], ff_x.at[zz, q], xdev)

    for q in range(4):
        ff_own_x(q)
    at_forward_x()
    for k in (0,) + near:
        zz = zat(k)
        arrived(normg.at[head, :, lanes(zz * n_x + xp)], nb_x.at[zz])
    send(normg.at[head], normg.at[head], sent.at[3], nb_y.at[0], ydev)
    send(normg.at[head], normg.at[head], sent.at[4], nb_c.at[y], cdev)
    at_forward_z(z2, x, True)
    at_forward_z(z1, x, False)
    at_forward_z(z3, x, False)
    arrived(normg.at[yp * 2 + c], nb_y.at[0])
    send(normg.at[yp * 2 + c], normg.at[yp * 2 + c], sent.at[4], nb_c.at[yp], cdev)
    at_forward_z(z2, xp, True)
    for q in range(2):
        ff_own_z(q)
    own_cot = cotr.at[pl.ds(head * slots, slots)]

    arrived(normg.at[y * 2 + cp], nb_c.at[y])
    arrived(normg.at[yp * 2 + cp], nb_c.at[yp])
    normv[...] = normg[0] + normg[1] + normg[2] + normg[3]

    def gain(j):
        return normv[j : j + 1, :]

    def shift(j):
        return normv[3 + j : 4 + j, :]

    def statistics(values):
        centered = values - jnp.mean(values, axis=-1, keepdims=True)
        inverse = lax.rsqrt(jnp.mean(centered * centered, axis=-1, keepdims=True) + 1e-05)
        return centered * inverse, inverse

    def norm_rows(values, j):
        return (statistics(values)[0] * gain(j) + shift(j)).astype(bf16)

    half = queries // 2

    def norm_latent(m, carry):
        for r in range(2):
            rows = slice(r * half, (r + 1) * half)
            latent_n[m, rows, :] = norm_rows(latent_v[m, rows, :].astype(f32), 1)
        return carry

    def norm_media(m, carry):
        for r in range(2):
            rows = slice(r * half, (r + 1) * half)
            media_n[m, rows, :] = norm_rows(media_v[m, rows, :].astype(f32), 0)
        return carry

    local[6].wait()
    lax.fori_loop(0, slots, norm_latent, 0)
    at_forward_z(z1, xp, False)
    at_forward_y(img)
    at_forward_y(z * n_x + xp)
    at_forward_z(z3, xp, False)
    send(own_cot, own_cot, sent.at[7], bg_y.at[0], ydev)
    send(own_cot, own_cot, sent.at[7], bg_c.at[y], cdev)
    local[7].wait()
    blocks = media_v.shape[0]
    step = blocks // 4
    order = [z2 * n_x + x, z1 * n_x + x, z3 * n_x + x, z2 * n_x + xp, z1 * n_x + xp, z3 * n_x + xp]
    for r in range(4):
        lax.fori_loop(r * step, (r + 1) * step, norm_media, 0)
        at_forward_y(order[r])

    def turn_media(r, carry):
        block = media_n[pl.ds(r * 2, 2)].reshape(128, width)
        for d in range(width // 128):
            media_t[d * 128 : (d + 1) * 128, pl.ds(pl.multiple_of(r * 128, 128), 128)] = tpose(
                block[:, d * 128 : (d + 1) * 128]
            )
        return carry

    rows_latent = slots * queries

    def turn_latent(source, target, columns):
        whole = source[...].reshape(rows_latent, columns)
        for r in range(0, rows_latent, 128):
            stop = min(r + 128, rows_latent)
            for d in range(columns // 128):
                target[d * 128 : (d + 1) * 128, r:stop] = tpose(
                    whole[r:stop, d * 128 : (d + 1) * 128]
                )

    turn_latent(latent_n, latent_t, width)
    lax.fori_loop(0, blocks * queries // 128, turn_media, 0)
    ff_forward(0)
    at_forward_y(order[4])
    ff_forward(1)
    at_forward_y(order[5])

    for ii in range(8):
        for yy in range(2):
            arrived(slab.at[ii * n_head + yy * 2 + cp], at_c.at[ii, yy])
    ff_forward(2)
    ff_own_z(2)

    query_full[:, 0] = slab[:, 48:64, 0:inner]
    query_full[:, 1] = slab[:, 48:64, inner:width]

    def query_tile(cols):
        return query_full[:, :, :, cols].reshape(width, -1)

    def kv_tile(cols):
        return slab[:, 0:32, cols].reshape(width, -1)

    def out_tile(cols):
        return slab[:, 32:48, cols].reshape(inner, -1)

    latent_rows_n = latent_n[...].reshape(rows_latent, width)

    def tile(t):
        return pl.ds(pl.multiple_of(t * 256, 256), 256)

    query_v[...] = (
        (dot_nn(latent_rows_n, query_full[...].reshape(width, inner)) * scale)
        .astype(bf16)
        .reshape(slots, queries, inner)
    )
    groups = kv_media.shape[0]
    media_rows_n = media_n[...].reshape(groups * 256, width)

    def kv_step(t, carry):
        weight = kv_tile(tile(t))
        kv_latent[:, :, tile(t)] = dot_nn(latent_rows_n, weight).astype(bf16).reshape(slots, queries, 256)
        kv_media[:, :, tile(t)] = dot_nn(media_rows_n, weight).astype(bf16).reshape(groups, 256, 256)
        return carry

    def kv_two(i, carry):
        ff_forward(3 + i)
        return lax.fori_loop(2 * i, 2 * i + 2, kv_step, carry)

    lax.fori_loop(0, width // 512, kv_two, 0)
    ff_forward(5)
    ff_own_z(3)

    def lane_mask(hh, dtype):
        lane = lax.broadcasted_iota(jnp.int32, (1, 256), 1)
        return (lane // queries == hh).astype(f32).astype(dtype)

    def spread(rows):
        return jnp.concatenate([rows * lane_mask(hh, bf16) for hh in range(4)], axis=0)

    def fold(rows):
        total = rows[0:queries] * lane_mask(0, f32)
        for hh in range(1, 4):
            total = total + rows[hh * queries : (hh + 1) * queries] * lane_mask(hh, f32)
        return total

    def probabilities(m, g):
        q_rows = spread(query_v[m, :, tile(g)])
        k_media = kv_media[m, :, tile(g)]
        k_latent = kv_latent[m, :, tile(g)]
        s_media = contract_cols(q_rows, k_media)
        s_latent = contract_cols(q_rows, k_latent)
        top = jnp.maximum(
            jnp.max(s_media, axis=-1, keepdims=True), jnp.max(s_latent, axis=-1, keepdims=True)
        )
        e_media = jnp.exp(s_media - top)
        e_latent = jnp.exp(s_latent - top)
        total = jnp.sum(e_media, axis=-1, keepdims=True) + jnp.sum(e_latent, axis=-1, keepdims=True)
        inverse = 1.0 / total
        return q_rows, k_media, k_latent, e_media * inverse, e_latent * inverse

    def attend(m, g):
        p_media, p_latent = probabilities(m, g)[3:]
        v_media = kv_media[m, :, tile(g + 2)]
        v_latent = kv_latent[m, :, tile(g + 2)]
        rows = dot_nn(p_media.astype(bf16), v_media) + dot_nn(p_latent.astype(bf16), v_latent)
        att_v[m, :, tile(g)] = fold(rows).astype(bf16)

    def forward_image(m, carry):
        attend(m, 0)
        attend(m, 1)
        mid_v[m] = latent_v[m].astype(f32) + dot_nn(att_v[m], out_tile(slice(0, width)))
        for r in range(2):
            rows = slice(r * half, (r + 1) * half)
            hid[head * slots + m, rows, :] = norm_rows(mid_v[m, rows, :], 2)
        piece = hid.at[head * slots + m]
        send(piece, piece, sent.at[8], hd_y.at[m], ydev)
        send(piece, piece, sent.at[8], hd_c.at[m], cdev)

        @pl.when(jnp.logical_and(m >= 1, m <= 3))
        def _():
            ff_forward(5 + m)

        return carry

    lax.fori_loop(0, slots, forward_image, 0)

    other = yp * 2 + c
    cot_other = cotr.at[pl.ds(other * slots, slots)]
    arrived(cot_other, bg_y.at[0])
    send(cot_other, cot_other, sent.at[7], bg_c.at[yp], cdev)
    turn_latent(att_v, att_t, inner)
    for yy in (y, yp):
        arrived(cotr.at[pl.ds((yy * 2 + cp) * slots, slots)], bg_c.at[yy])

    all_rows = n_head * slots * queries

    def turn_rows(source, slot):
        def body(r, carry):
            block = source[pl.ds(r * 2, 2)].reshape(128, width)
            for d in range(width // 128):
                turned[slot, d * 128 : (d + 1) * 128, pl.ds(pl.multiple_of(r * 128, 128), 128)] = tpose(
                    block[:, d * 128 : (d + 1) * 128]
                )
            return carry

        lax.fori_loop(0, all_rows // 128, body, 0)

    turn_rows(cotr, 1)

    act_at = 4 * slots

    def ff_rows(q, start):
        rows = pl.ds(start, 2 * slots)
        pre = dot_nn(hid[rows].reshape(all_rows // 2, width), wide[q, :, :, 0:256].reshape(width, 256))
        grad = dot_nn(cotr[rows].reshape(all_rows // 2, width), wide[q, :, :, 256:512].reshape(width, 256))
        below = 0.5 * (1.0 + lax.erf(pre * 0.7071067811865476))
        slope = below + pre * (jnp.exp(-0.5 * pre * pre) * 0.3989422804014327)
        pair[rows, :, tile(q)] = (grad * slope).astype(bf16).reshape(2 * slots, queries, 256)
        pair[pl.ds(act_at + start, 2 * slots), :, tile(q)] = (
            (pre * below).astype(bf16).reshape(2 * slots, queries, 256)
        )

    def ff_near(q, carry):
        for zz in range(n_z):
            arrived(ff_unit(q, zz * n_x + xp), ff_x.at[zz, q])
        ff_rows(q, y * 2 * slots)
        return carry

    def ff_far(q, carry):
        ff_rows(q, yp * 2 * slots)
        return carry

    def hid_near(m, carry):
        arrived(hid.at[(y * 2 + cp) * slots + m], hd_c.at[m])
        return carry

    def hid_forward(m, carry):
        piece = hid.at[other * slots + m]
        arrived(piece, hd_y.at[m])
        send(piece, piece, sent.at[8], hd_f.at[m], cdev)
        return carry

    def hid_far(m, carry):
        arrived(hid.at[(yp * 2 + cp) * slots + m], hd_f.at[m])
        return carry

    def grad_tile(q, carry):
        def over_parts(part, carry2):
            right = pair[pl.ds(part * act_at, act_at), :, tile(q)].reshape(all_rows, 256)
            value = dot_nn(turned[part], right).astype(bf16).reshape(n_z, n_x, 128, 256)
            grads[q, part, 0] = value[:, 0]
            grads[q, part, 1] = value[:, 1]
            send(grads.at[q, part, xp], xrecv.at[q, part], sent.at[11], rf_x.at[q, part], xdev)
            return carry2

        return lax.fori_loop(0, 2, over_parts, carry)

    def ff_near_and_forward(q, carry):
        ff_near(q, 0)
        ff_forward(9 + q)
        return carry

    lax.fori_loop(0, slots, hid_near, 0)
    lax.fori_loop(0, 3, ff_near_and_forward, 0)
    lax.fori_loop(0, slots, hid_forward, 0)
    lax.fori_loop(0, slots, hid_far, 0)
    lax.fori_loop(0, 3, ff_far, 0)
    turn_rows(hid, 0)
    grad_tile(0, 0)
    ff_near(3, 0)
    ff_far(3, 0)

    def wide_rows(part, q, t):
        return wide[q, pl.ds(t * 4, 4), :, part * 256 : (part + 1) * 256].reshape(512, 256)

    def broad(t):
        return pl.ds(pl.multiple_of(t * 512, 512), 512)

    def back_rows(left, part, t):
        total = contract_cols(left[:, 0:256], wide_rows(part, 0, t))
        for q in range(1, 4):
            total = total + contract_cols(left[:, q * 256 : (q + 1) * 256], wide_rows(part, q, t))
        return total

    def head_sum(part):
        def rows_of(hh):
            return pair[pl.ds(part * act_at + hh * slots, slots)].reshape(rows_latent, hidden)

        for slot, hh in enumerate((yp * 2 + cp, y * 2 + cp)):
            left = rows_of(hh)

            def to_core(t, carry, left=left, slot=slot):
                value = back_rows(left, part, t)
                hsend[slot, :, :, broad(t)] = value.astype(bf16).reshape(slots, queries, 512)
                return carry

            lax.fori_loop(0, width // 512, to_core, 0)
            send(hsend.at[slot], hrecv.at[part, slot], sent.at[9], hp_c.at[part, slot], cdev)
        left_y = rows_of(yp * 2 + c)
        arrived(hrecv.at[part, 0], hp_c.at[part, 0])

        def to_y(t, carry):
            value = back_rows(left_y, part, t).reshape(slots, queries, 512)
            hysend[part, :, :, broad(t)] = (value + hrecv[part, 0, :, :, broad(t)].astype(f32)).astype(bf16)
            return carry

        lax.fori_loop(0, width // 512, to_y, 0)
        send(hysend.at[part], hyrecv.at[part], sent.at[10], hp_y.at[part], ydev)
        left_own = rows_of(head)
        arrived(hrecv.at[part, 1], hp_c.at[part, 1])

        def to_own(t, carry):
            value = back_rows(left_own, part, t).reshape(slots, queries, 512)
            hown[part, :, :, broad(t)] = value + hrecv[part, 1, :, :, broad(t)].astype(f32)
            return carry

        lax.fori_loop(0, width // 512, to_own, 0)

    arrived(hid.at[0 : 3 * slots], sent.at[8])
    head_sum(0)

    def sum_tile(u):
        q, part = u // 2, u % 2
        arrived(xrecv.at[q, part], rf_x.at[q, part])
        for k, zz in enumerate((z1, z2, z3)):
            grads[q, part, x, zz] = (
                grads[q, part, x, zz].astype(f32) + xrecv[q, part, zz].astype(f32)
            ).astype(bf16)
            send(grads.at[q, part, x, zz], zrecv.at[k, part, q], sent.at[12], rf_z.at[k, part], zdev(zz))

    lax.fori_loop(1, 4, grad_tile, 0)
    sum_tile(0)
    sum_tile(1)
    arrived(hsend, sent.at[9])
    head_sum(1)
    sum_tile(2)

    gacc[...] = jnp.zeros_like(gacc)

    def tally(j, upper, xhat):
        gacc[j] += jnp.sum((upper * xhat).reshape(-1, 8, width), axis=0)
        gacc[3 + j] += jnp.sum(upper.reshape(-1, 8, width), axis=0)

    def norm_back(values, j, upper):
        xhat, inverse = statistics(values)
        tally(j, upper, xhat)
        g = upper * gain(j)
        return inverse * (
            g - jnp.mean(g, axis=-1, keepdims=True) - xhat * jnp.mean(g * xhat, axis=-1, keepdims=True)
        )

    sum_tile(3)
    arrived(hyrecv.at[0], hp_y.at[0])

    def mid_back(m, carry):
        upper = hown[0, m] + hyrecv[0, m].astype(f32)
        back = norm_back(mid_v[m], 2, upper)
        total = cotr[head * slots + m].astype(f32) + back
        hown[0, m] = total
        delta_v[m] = total.astype(bf16)
        return carry

    lax.fori_loop(0, slots, mid_back, 0)
    delta_rows = delta_v[...].reshape(rows_latent, width)

    attg_v[...] = (
        contract_cols(delta_rows, out_tile(slice(0, width))).astype(bf16).reshape(slots, queries, inner)
    )

    gslab = pair

    def gunit(ii, hh_y, hh_c):
        return ii * 4 + hh_c * 2 + hh_y

    def out_grad_step(t, carry):
        right = delta_v[:, :, broad(t)].reshape(rows_latent, 512)
        value = dot_nn(att_t[...], right).astype(bf16)
        for ii in range(8):
            for hh in range(4):
                at = (ii * 4 + hh) * 16
                gslab[gunit(ii, hh // 2, hh % 2), 32:48, broad(t)] = value[at : at + 16]
        return carry

    lax.fori_loop(0, width // 512, out_grad_step, 0)
    sum_tile(4)

    def back_pair(m, g):
        q_rows, k_media, k_latent, p_media, p_latent = probabilities(m, g)
        v_media = kv_media[m, :, tile(g + 2)]
        v_latent = kv_latent[m, :, tile(g + 2)]
        up_rows = spread(attg_v[m, :, tile(g)])
        g_media = contract_cols(up_rows, v_media)
        g_latent = contract_cols(up_rows, v_latent)
        dotted = jnp.sum(g_media * p_media, axis=-1, keepdims=True) + jnp.sum(
            g_latent * p_latent, axis=-1, keepdims=True
        )
        d_media = (p_media * (g_media - dotted)).astype(bf16)
        d_latent = (p_latent * (g_latent - dotted)).astype(bf16)
        qgrad_v[m, :, tile(g)] = fold(dot_nn(d_media, k_media) + dot_nn(d_latent, k_latent)).astype(bf16)
        kv_media[m, :, tile(g)] = contract_rows(d_media, q_rows).astype(bf16)
        kv_latent[m, :, tile(g)] = contract_rows(d_latent, q_rows).astype(bf16)
        kv_media[m, :, tile(g + 2)] = contract_rows(p_media.astype(bf16), up_rows).astype(bf16)
        kv_latent[m, :, tile(g + 2)] = contract_rows(p_latent.astype(bf16), up_rows).astype(bf16)

    def back_image(m, carry):
        back_pair(m, 0)
        back_pair(m, 1)
        return carry

    lax.fori_loop(0, slots, back_image, 0)

    sum_tile(5)

    gcr = hid
    gyr_v = media_n

    def kv_grad_chunk(zz):
        rows = pl.ds(pl.multiple_of(zz * 256, 256), 256)
        left_media = media_t[rows, :]
        left_latent = latent_t[rows, :]

        value = dot_nn(left_media, kv_media[...].reshape(groups * 256, width)) + dot_nn(
            left_latent, kv_latent[...].reshape(rows_latent, width)
        )
        value = value.astype(bf16)
        value_q = dot_nn(left_latent, qgrad_v[...].reshape(rows_latent, inner)) * scale
        value_q = value_q.astype(bf16)
        for xx in range(2):
            for hh in range(4):
                at = (xx * 4 + hh) * 32
                uu = gunit(zz * n_x + xx, hh // 2, hh % 2)
                gslab[uu, 0:32, :] = value[at : at + 32]
                gslab[uu, 48:64, 0:inner] = value_q[at : at + 16]
                gslab[uu, 48:64, inner:width] = value_q[at + 16 : at + 32]
        for xx in range(2):
            ii = zz * n_x + xx
            send(
                gslab.at[pl.ds(ii * 4 + cp * 2, 2)],
                gcr.at[pl.ds(ii * 2, 2)],
                sent.at[13],
                ra_c.at[ii],
                cdev,
            )

    def stage_y(zz):
        for xx in range(2):
            ii = zz * n_x + xx
            arrived(gcr.at[pl.ds(ii * 2, 2)], ra_c.at[ii])
            uu = gunit(ii, yp, c)
            gslab[uu] = (gslab[uu].astype(f32) + gcr[ii * 2 + yp].astype(f32)).astype(bf16)
            send(gslab.at[uu], gyr_v.at[ii], sent.at[14], ra_y.at[ii], ydev)

    def upto_y(ii):
        return (
            gslab[gunit(ii, y, c)].astype(f32) + gcr[ii * 2 + y].astype(f32) + gyr_v[ii].astype(f32)
        )

    def stage_x(zz):
        ii = zz * n_x + xp
        arrived(gyr_v.at[ii], ra_y.at[ii])
        uu = gunit(ii, y, c)
        gslab[uu] = upto_y(ii).astype(bf16)
        send(gslab.at[uu], gyr_v.at[8 + zz], sent.at[15], ra_x.at[zz], xdev)

    def stage_z(zz, last):
        ii = zz * n_x + x
        arrived(gyr_v.at[ii], ra_y.at[ii])
        arrived(gyr_v.at[8 + zz], ra_x.at[zz])
        if last:
            return upto_y(ii) + gyr_v[8 + zz].astype(f32)
        uu = gunit(ii, y, c)
        gslab[uu] = (upto_y(ii) + gyr_v[8 + zz].astype(f32)).astype(bf16)
        send(gslab.at[uu], gzr_v.at[z], sent.at[16], ra_z.at[z], zdev(zz))
        return None

    chunk = [zat(1), zat(3), zat(2), z]
    kv_grad_chunk(chunk[0])
    kv_grad_chunk(chunk[1])
    stage_y(chunk[0])
    kv_grad_chunk(chunk[2])
    stage_y(chunk[1])
    kv_grad_chunk(chunk[3])
    stage_y(chunk[2])
    sum_tile(6)

    arrived(hyrecv.at[1], hp_y.at[1])
    new_v = delta_v

    for m in range(slots):
        keep = jnp.clip(filled - m, 0, 1).astype(f32)
        for r in range(2):
            rows = slice(r * half, (r + 1) * half)
            branch = hown[1, m, rows, :] + hyrecv[1, m, rows, :].astype(f32)
            new_v[m, rows, :] = ((mid_v[m, rows, :] + branch) * keep).astype(bf16)
    stage_y(chunk[3])

    def media_back(m, carry):
        hown[1, 0:4] = contract_cols(kv_media[m], kv_tile(slice(0, width))).reshape(4, 64, width)

        def over_rows(r, carry2):
            block = m * 4 + r
            back = norm_back(media_v[block].astype(f32), 0, hown[1, r])
            media_v[block] = back.astype(bf16)
            return carry2

        lax.fori_loop(0, 4, over_rows, 0)
        return carry

    def latent_back_tiles(t, carry):
        weight = slab[pl.ds(t * 16, 16), 0:32, :].reshape(512, width)
        query_weight = query_full[pl.ds(t * 16, 16)].reshape(512, inner)
        hown[1, :, :, broad(t)] = (
            contract_cols(kv_latent[...].reshape(rows_latent, width), weight)
            + contract_cols(qgrad_v[...].reshape(rows_latent, inner), query_weight) * scale
        ).reshape(slots, queries, 512)
        return carry

    def latent_back(m, carry):
        back = norm_back(latent_v[m].astype(f32), 1, hown[1, m])
        latent_v[m] = (hown[0, m] + back).astype(bf16)
        return carry

    lax.fori_loop(0, width // 512, latent_back_tiles, 0)
    lax.fori_loop(0, slots, latent_back, 0)
    lax.fori_loop(0, 2, media_back, 0)
    sum_tile(7)
    stage_x(chunk[0])
    lax.fori_loop(2, 4, media_back, 0)
    stage_x(chunk[1])
    stage_z(chunk[0], False)
    lax.fori_loop(4, 5, media_back, 0)

    for j in range(6):
        gsend[0, j : j + 1, :] = jnp.sum(gacc[j], axis=0, keepdims=True)
    gsend[0, 6:8, :] = jnp.zeros((2, width), f32)
    send(gsend.at[0], gyr.at[0], sent.at[17], gr_c.at[0], cdev)
    arrived(gyr.at[0], gr_c.at[0])
    gsend[1] = gsend[0] + gyr[0]
    send(gsend.at[1], gyr.at[1], sent.at[17], gr_c.at[1], xdev)
    stage_z(chunk[1], False)
    arrived(gyr.at[1], gr_c.at[1])
    gsend[2] = gsend[1] + gyr[1]
    for k in near:
        zz = zat(k)
        send(gsend.at[2, :, lanes(zz * n_x + x)], gzr.at[z], sent.at[18], gr_z.at[z], zdev(zz))
    stage_x(chunk[2])
    total = gsend[2, :, lanes(img)]
    for k in near:
        zz = zat(k)
        arrived(gzr.at[zz], gr_z.at[zz])
        total = total + gzr[zz]
    gsend[3, :, 0:128] = total
    send(gsend.at[3, :, 0:128], gyr.at[2, :, 0:128], sent.at[17], gr_c.at[2], ydev)

    for part in range(2):
        for k in range(3):
            arrived(zrecv.at[k, part], rf_z.at[k, part])

    def own_sum(part, q):
        value = grads[q, part, x, z].astype(f32) + xrecv[q, part, z].astype(f32)
        for k in range(3):
            value = value + zrecv[k, part, q].astype(f32)
        return value

    def last_sums(q, carry):
        up_out[:, tile(q)] = own_sum(0, q)
        value = own_sum(1, q)
        for j in range(2):
            rows = pl.ds(pl.multiple_of(q * 256 + j * 128, 128), 128)
            down_out[rows, :] = tpose(value[:, j * 128 : (j + 1) * 128])
        return carry

    lax.fori_loop(0, hidden // 256, last_sums, 0)

    stage_x(chunk[3])
    stage_z(chunk[2], False)
    arrived(gyr.at[2, :, 0:128], gr_c.at[2])
    norm_out[...] = gsend[3, :, 0:128] + gyr[2, :, 0:128]
    final = stage_z(chunk[3], True)
    for k in near:
        zz = zat(k)
        arrived(gzr_v.at[zz], ra_z.at[zz])
        final = final + gzr_v[zz].astype(f32)
    key_value_out[...] = final[0:32]
    output_out[...] = final[32:48]
    query_out[0:16, :] = final[48:64, 0:inner]
    query_out[16:32, :] = final[48:64, inner:width]

    arrived(normg.at[0, :, 0:384], sent.at[0])
    arrived(slab.at[0:29], sent.at[1])

    @pl.when(mid)
    def _():
        arrived(slab.at[0:4], sent.at[1])
        arrived(wide.at[0], sent.at[5])

    arrived(normg.at[0, :, 0:512], sent.at[2])
    arrived(normg.at[0], sent.at[3])
    arrived(normg.at[0:2], sent.at[4])
    arrived(wide.at[0], sent.at[5])
    arrived(wide.at[0:2], sent.at[6])
    arrived(cotr.at[0 : 3 * slots], sent.at[7])
    arrived(hsend, sent.at[9])
    arrived(hysend, sent.at[10])
    arrived(xrecv, sent.at[11])
    arrived(zrecv, sent.at[12])
    arrived(gcr.at[0:16], sent.at[13])
    arrived(gyr_v.at[0:8], sent.at[14])
    arrived(gyr_v.at[0:4], sent.at[15])
    arrived(gyr_v.at[0:3], sent.at[16])
    arrived(gyr.at[0:2], sent.at[17])
    arrived(gyr.at[2, :, 0:128], sent.at[17])
    arrived(gzr.at[0:3], sent.at[18])


def finish_kernel(norms, *refs):
    sources, gains_out, biases_out, targets, sems = refs[:8], refs[8], refs[9], refs[10:18], refs[18]
    copies = [pltpu.make_async_copy(sources[i], targets[i], sems.at[i]) for i in range(8)]
    for copy in copies:
        copy.start()
    part = gains_out.shape[1]
    head = lax.axis_index("head")
    rolled = pltpu.roll(norms[...], (128 - head * part) % 128, 1)
    gains_out[...] = rolled[0:3, 0:part]
    biases_out[...] = rolled[3:6, 0:part]
    for copy in copies:
        copy.wait()


def block_plan(
    media_patches,
    latent_rows,
    media_counts,
    norm_gains,
    norm_biases,
    query_weight,
    key_value_weight,
    output_weight,
    up_weight,
    down_weight,
    cotangent,
):
    slots, patches, width = media_patches.shape[1:]
    queries = latent_rows.shape[2]
    inner = query_weight.shape[1]
    hidden = up_weight.shape[1]
    rows_up = up_weight.shape[0]
    part = norm_gains.shape[1]
    blocks = slots * patches // 64
    bf16, f32 = jnp.bfloat16, jnp.float32
    shape = jax.ShapeDtypeStruct
    hbm = pl.BlockSpec(memory_space=pl.ANY)
    vmem = pl.BlockSpec(memory_space=pltpu.VMEM)
    smem = pl.BlockSpec(memory_space=pltpu.SMEM)
    dma = pltpu.SemaphoreType.DMA
    all_rows = 4 * slots * queries
    rows_latent = slots * queries
    outs = pl.pallas_call(
        block_kernel,
        out_shape=(
            pltpu.VMEM((slots, queries, width), bf16),
            pltpu.VMEM((blocks, 64, width), bf16),
            pltpu.VMEM((slots, queries, width), bf16),
            pltpu.VMEM((8, 128), f32),
            pltpu.VMEM(query_weight.shape, f32),
            pltpu.VMEM(key_value_weight.shape, f32),
            pltpu.VMEM(output_weight.shape, f32),
            pltpu.VMEM(up_weight.shape, f32),
            pltpu.VMEM(down_weight.shape, f32),
        ),
        in_specs=[smem] + [hbm] * 7 + [vmem] * 3,
        out_specs=(vmem,) * 9,
        scratch_shapes=[
            pltpu.VMEM((32, 64, width), bf16),
            pltpu.VMEM((32, 2, 16, inner), bf16),
            pltpu.VMEM((4, 8, rows_up, 512), bf16),
            pltpu.VMEM((4 * slots, queries, width), bf16),
            pltpu.VMEM((4 * slots, queries, width), bf16),
            pltpu.VMEM((2, width, all_rows), bf16),
            pltpu.VMEM((blocks, 64, width), bf16),
            pltpu.VMEM((slots, queries, width), bf16),
            pltpu.VMEM((width, slots * patches), bf16),
            pltpu.VMEM((width, rows_latent), bf16),
            pltpu.VMEM((slots, patches, 2 * inner), bf16),
            pltpu.VMEM((slots, queries, 2 * inner), bf16),
            pltpu.VMEM((slots, queries, inner), bf16),
            pltpu.VMEM((slots, queries, inner), bf16),
            pltpu.VMEM((inner, rows_latent), bf16),
            pltpu.VMEM((slots, queries, width), f32),
            pltpu.VMEM((8 * slots, queries, width), bf16),
            pltpu.VMEM((4, 2, 2, 4, rows_up, 256), bf16),
            pltpu.VMEM((4, 2, 4, rows_up, 256), bf16),
            pltpu.VMEM((3, 2, 4, rows_up, 256), bf16),
            pltpu.VMEM((2, slots, queries, width), bf16),
            pltpu.VMEM((2, 2, slots, queries, width), bf16),
            pltpu.VMEM((2, slots, queries, width), bf16),
            pltpu.VMEM((2, slots, queries, width), bf16),
            pltpu.VMEM((2, slots, queries, width), f32),
            pltpu.VMEM((slots, queries, inner), bf16),
            pltpu.VMEM((slots, queries, inner), bf16),
            pltpu.VMEM((4, 8, width), f32),
            pltpu.VMEM((8, width), f32),
            pltpu.VMEM((6, 8, width), f32),
            pltpu.VMEM((4, 8, width), f32),
            pltpu.VMEM((3, 8, width), f32),
            pltpu.VMEM((4, 8, 128), f32),
            pltpu.VMEM((4, 64, width), bf16),
            dma((11,)),
            dma((4, 2)),
            dma((1,)),
            dma((8,)),
            dma((8, 2)),
            dma((4, 4)),
            dma((4, 4)),
            dma((4,)),
            dma((4,)),
            dma((1,)),
            dma((2,)),
            dma((slots,)),
            dma((slots,)),
            dma((slots,)),
            dma((1,)),
            dma((2,)),
            dma((2, 2)),
            dma((2,)),
            dma((4, 2)),
            dma((4, 2)),
            dma((8,)),
            dma((8,)),
            dma((4,)),
            dma((4,)),
            dma((3,)),
            dma((4,)),
            dma((19,)),
        ],
        compiler_params=pltpu.CompilerParams(
            collective_id=0, has_side_effects=True, vmem_limit_bytes=61796352
        ),
    )(
        media_counts,
        media_patches.reshape(blocks, 64, width),
        latent_rows.reshape(slots, queries, width),
        cotangent.reshape(slots, queries, width),
        query_weight,
        key_value_weight,
        output_weight,
        up_weight,
        down_weight,
        norm_gains,
        norm_biases,
    )
    norms = outs[3]
    rest = outs[:3] + outs[4:]
    done = pl.pallas_call(
        finish_kernel,
        out_shape=(shape((3, part), f32), shape((3, part), f32)) + tuple(shape(v.shape, v.dtype) for v in rest),
        in_specs=[vmem] * 9,
        out_specs=(vmem, vmem) + (hbm,) * 8,
        scratch_shapes=[dma((8,))],
        compiler_params=pltpu.CompilerParams(vmem_limit_bytes=4194304),
    )(norms, *rest)
    gains_grad, biases_grad, new, media_grad, latent_grad = done[:5]
    return (
        new.reshape(latent_rows.shape),
        media_grad.reshape(media_patches.shape),
        latent_grad.reshape(latent_rows.shape),
        gains_grad,
        biases_grad,
    ) + tuple(done[5:])


def block_fits(mesh):
    return mesh.shape["img"] == 8 and mesh.shape["head"] == 4


def solution(mesh):
    return jax.shard_map(
        block_plan if block_fits(mesh) else gathered_plan,
        mesh=mesh,
        in_specs=(
            P(("img", "head"), None, None, None),
            P(("img", "head"), None, None, None),
            P(("img", "head")),
            P(None, ("img", "head")),
            P(None, ("img", "head")),
            P(("img", "head"), None),
            P(("img", "head"), None),
            P(("img", "head"), None),
            P("img", "head"),
            P("head", "img"),
            P(("img", "head"), None, None, None),
        ),
        out_specs=(
            P(("img", "head"), None, None, None),
            P(("img", "head"), None, None, None),
            P(("img", "head"), None, None, None),
            P(None, ("img", "head")),
            P(None, ("img", "head")),
            P(("img", "head"), None),
            P(("img", "head"), None),
            P(("img", "head"), None),
            P("img", "head"),
            P("head", "img"),
        ),
        check_vma=False,
    )
```

```python
import jax
import jax.numpy as jnp
from jax import lax
from jax.experimental import pallas as pl
from jax.experimental.pallas import tpu as pltpu
from jax.sharding import PartitionSpec as P

HEADS = 8


def layer_norm(values, norm_gain, norm_shift):
    centered = values - jnp.mean(values, axis=-1, keepdims=True)
    variance = jnp.mean(centered * centered, axis=-1, keepdims=True)
    return centered * lax.rsqrt(variance + 1e-05) * norm_gain + norm_shift


def norm_backward(values, norm_gain, norm_shift, upstream):
    primal, pullback = jax.vjp(layer_norm, values, norm_gain, norm_shift)
    return pullback(upstream)


def exact_gelu(values):
    return jax.nn.gelu(values, approximate=False)


def gelu_backward(values, upstream):
    primal, pullback = jax.vjp(exact_gelu, values)
    return pullback(upstream)[0]


def contract_rows(left_side, right_side):
    return lax.dot_general(
        left_side, right_side, (((0,), (0,)), ((), ())), preferred_element_type=jnp.float32
    )


def contract_cols(left_side, right_side):
    return lax.dot_general(
        left_side, right_side, (((1,), (1,)), ((), ())), preferred_element_type=jnp.float32
    )


def gathered_plan(
    media_patches,
    latent_rows,
    media_counts,
    norm_gains,
    norm_biases,
    query_weight,
    key_value_weight,
    output_weight,
    up_weight,
    down_weight,
    cotangent,
):
    samp_local, media_slots, patches, model_width = media_patches.shape
    queries_per = latent_rows.shape[2]
    images = samp_local * media_slots
    keys_per = patches + queries_per
    rows_local = images * queries_per
    gathered = (
        lax.all_gather(query_weight, ("img", "head"), axis=0, tiled=True),
        lax.all_gather(key_value_weight, ("img", "head"), axis=0, tiled=True),
        lax.all_gather(output_weight, ("img", "head"), axis=0, tiled=True),
        lax.all_gather(norm_gains, ("img", "head"), axis=1, tiled=True),
        lax.all_gather(norm_biases, ("img", "head"), axis=1, tiled=True),
    )
    query_full, key_value_full, output_full, gains_low, biases_low = gathered
    norm_gain = gains_low.astype(jnp.float32)
    norm_shift = biases_low.astype(jnp.float32)
    inner_width = query_full.shape[1]
    head_size = inner_width // HEADS
    score_scale = head_size ** (-0.5)
    up_part, down_part = (
        lax.all_gather(up_weight, "img", axis=0, tiled=True),
        lax.all_gather(down_weight, "img", axis=1, tiled=True),
    )
    media_full = media_patches.reshape(images, patches, model_width).astype(jnp.float32)
    latent_full = latent_rows.reshape(images, queries_per, model_width).astype(jnp.float32)
    media_norm = layer_norm(media_full, norm_gain[0], norm_shift[0]).astype(jnp.bfloat16)
    latent_norm = layer_norm(latent_full, norm_gain[1], norm_shift[1]).astype(jnp.bfloat16)
    query_rows = (
        jnp.einsum("ild,de->ile", latent_norm, query_full, preferred_element_type=jnp.float32)
        * score_scale
    ).astype(jnp.bfloat16)
    key_input = jnp.concatenate([media_norm, latent_norm], axis=1)
    key_value_rows = jnp.einsum(
        "ikd,de->ike", key_input, key_value_full, preferred_element_type=jnp.float32
    ).astype(jnp.bfloat16)
    query_heads = (
        query_rows.reshape(images, queries_per, HEADS, head_size)
        .transpose(2, 0, 1, 3)
        .reshape(HEADS, images, queries_per * head_size)
    )
    key_value_heads = (
        key_value_rows.reshape(images, keys_per, 2, HEADS, head_size)
        .transpose(3, 0, 1, 2, 4)
        .reshape(HEADS, images, keys_per, 2 * head_size)
    )
    query_group, key_value_group = (
        lax.all_to_all(query_heads, "head", split_axis=0, concat_axis=1, tiled=True),
        lax.all_to_all(key_value_heads, "head", split_axis=0, concat_axis=1, tiled=True),
    )
    heads_dev = query_group.shape[0]
    group_images = query_group.shape[1]
    query_block = query_group.reshape(heads_dev, group_images, queries_per, head_size)
    key_block = key_value_group[:, :, :, :head_size]
    value_block = key_value_group[:, :, :, head_size:]
    scores = jnp.einsum(
        "hgqe,hgke->hgqk", query_block, key_block, preferred_element_type=jnp.float32
    )
    row_max = jnp.max(scores, axis=-1, keepdims=True)
    weights = jnp.exp(scores - row_max)
    totals = jnp.sum(weights, axis=-1, keepdims=True)
    log_total = row_max + jnp.log(totals)
    probabilities = (weights / totals).astype(jnp.bfloat16)
    attended = jnp.einsum(
        "hgqk,hgke->hgqe", probabilities, value_block, preferred_element_type=jnp.float32
    ).astype(jnp.bfloat16)
    attended_back = lax.all_to_all(
        attended.reshape(heads_dev, group_images, queries_per * head_size),
        "head",
        split_axis=1,
        concat_axis=0,
        tiled=True,
    )
    attended_local = (
        attended_back.reshape(HEADS, images, queries_per, head_size)
        .transpose(1, 2, 0, 3)
        .reshape(images, queries_per, inner_width)
    )
    attn_delta = jnp.einsum(
        "ile,ed->ild", attended_local, output_full, preferred_element_type=jnp.float32
    )
    mid_latent = latent_full + attn_delta
    hidden_in = (
        layer_norm(mid_latent, norm_gain[2], norm_shift[2])
        .astype(jnp.bfloat16)
        .reshape(rows_local, model_width)
    )
    slot_mask = (
        (jnp.arange(media_slots)[None, :] < media_counts[:, None])
        .astype(jnp.float32)
        .reshape(images, 1, 1)
    )
    up_full, down_full = (
        lax.all_gather(up_part, "head", axis=1, tiled=True),
        lax.all_gather(down_part, "head", axis=0, tiled=True),
    )
    pre_act = jnp.dot(hidden_in, up_full, preferred_element_type=jnp.float32)
    act_low = exact_gelu(pre_act).astype(jnp.bfloat16)
    branch_out = jnp.dot(act_low, down_full, preferred_element_type=jnp.float32)
    result = slot_mask * (mid_latent + branch_out.reshape(images, queries_per, model_width))
    new_latents = result.astype(jnp.bfloat16).reshape(latent_rows.shape)
    out_grad = slot_mask * cotangent.reshape(images, queries_per, model_width).astype(jnp.float32)
    branch_grad = out_grad.astype(jnp.bfloat16).reshape(rows_local, model_width)
    act_grad = contract_cols(branch_grad, down_full)
    pre_grad = gelu_backward(pre_act, act_grad).astype(jnp.bfloat16)
    down_grad_whole = contract_rows(act_low, branch_grad)
    up_grad_whole = contract_rows(hidden_in, pre_grad)
    hidden_grad = contract_cols(pre_grad, up_full)
    up_grad_part, down_grad_part = (
        lax.psum_scatter(
            up_grad_whole.astype(jnp.bfloat16), "head", scatter_dimension=1, tiled=True
        ).astype(jnp.float32),
        lax.psum_scatter(
            down_grad_whole.astype(jnp.bfloat16), "head", scatter_dimension=0, tiled=True
        ).astype(jnp.float32),
    )
    up_grad, down_grad = (
        lax.psum_scatter(
            up_grad_part.astype(jnp.bfloat16), "img", scatter_dimension=0, tiled=True
        ).astype(jnp.float32),
        lax.psum_scatter(
            down_grad_part.astype(jnp.bfloat16), "img", scatter_dimension=1, tiled=True
        ).astype(jnp.float32),
    )
    mid_from_norm, gain_ff, bias_ff = norm_backward(
        mid_latent,
        norm_gain[2],
        norm_shift[2],
        hidden_grad.reshape(images, queries_per, model_width),
    )
    mid_grad = out_grad + mid_from_norm
    delta_low = mid_grad.astype(jnp.bfloat16)
    output_weight_grad = jnp.einsum(
        "ile,ild->ed", attended_local, delta_low, preferred_element_type=jnp.float32
    )
    attended_grad = jnp.einsum(
        "ild,ed->ile", delta_low, output_full, preferred_element_type=jnp.float32
    ).astype(jnp.bfloat16)
    grad_heads = (
        attended_grad.reshape(images, queries_per, HEADS, head_size)
        .transpose(2, 0, 1, 3)
        .reshape(HEADS, images, queries_per * head_size)
    )
    grad_group = lax.all_to_all(
        grad_heads, "head", split_axis=0, concat_axis=1, tiled=True
    ).reshape(heads_dev, group_images, queries_per, head_size)
    scores_again = jnp.einsum(
        "hgqe,hgke->hgqk", query_block, key_block, preferred_element_type=jnp.float32
    )
    probs_again = jnp.exp(scores_again - log_total)
    probs_again_low = probs_again.astype(jnp.bfloat16)
    prob_grad = jnp.einsum(
        "hgqe,hgke->hgqk", grad_group, value_block, preferred_element_type=jnp.float32
    )
    value_grad = jnp.einsum(
        "hgqk,hgqe->hgke", probs_again_low, grad_group, preferred_element_type=jnp.float32
    )
    row_dot = jnp.sum(prob_grad * probs_again, axis=-1, keepdims=True)
    score_grad = (probs_again * (prob_grad - row_dot)).astype(jnp.bfloat16)
    query_grad_group = jnp.einsum(
        "hgqk,hgke->hgqe", score_grad, key_block, preferred_element_type=jnp.float32
    ).astype(jnp.bfloat16)
    key_grad = jnp.einsum(
        "hgqk,hgqe->hgke", score_grad, query_block, preferred_element_type=jnp.float32
    )
    key_value_grad_group = jnp.concatenate([key_grad, value_grad], axis=-1).astype(jnp.bfloat16)
    query_back, key_value_back = (
        lax.all_to_all(
            query_grad_group.reshape(heads_dev, group_images, queries_per * head_size),
            "head",
            split_axis=1,
            concat_axis=0,
            tiled=True,
        ),
        lax.all_to_all(key_value_grad_group, "head", split_axis=1, concat_axis=0, tiled=True),
    )
    query_local = (
        query_back.reshape(HEADS, images, queries_per, head_size)
        .transpose(1, 2, 0, 3)
        .reshape(images, queries_per, inner_width)
    )
    key_value_local = (
        key_value_back.reshape(HEADS, images, keys_per, 2, head_size)
        .transpose(1, 2, 3, 0, 4)
        .reshape(images, keys_per, 2 * inner_width)
    )
    query_weight_grad = (
        jnp.einsum("ild,ile->de", latent_norm, query_local, preferred_element_type=jnp.float32)
        * score_scale
    )
    key_value_weight_grad = jnp.einsum(
        "ikd,ike->de", key_input, key_value_local, preferred_element_type=jnp.float32
    )
    key_input_grad = jnp.einsum(
        "ike,de->ikd", key_value_local, key_value_full, preferred_element_type=jnp.float32
    )
    latent_norm_grad = (
        jnp.einsum("ile,de->ild", query_local, query_full, preferred_element_type=jnp.float32)
        * score_scale
        + key_input_grad[:, patches:]
    )
    media_grad_full, gain_media, bias_media = norm_backward(
        media_full, norm_gain[0], norm_shift[0], key_input_grad[:, :patches]
    )
    latent_from_norm, gain_latent, bias_latent = norm_backward(
        latent_full, norm_gain[1], norm_shift[1], latent_norm_grad
    )
    latent_grad_full = mid_grad + latent_from_norm
    gain_terms = jnp.stack([gain_media, gain_latent, gain_ff])
    bias_terms = jnp.stack([bias_media, bias_latent, bias_ff])
    summed = (
        lax.psum_scatter(query_weight_grad, ("img", "head"), scatter_dimension=0, tiled=True),
        lax.psum_scatter(key_value_weight_grad, ("img", "head"), scatter_dimension=0, tiled=True),
        lax.psum_scatter(output_weight_grad, ("img", "head"), scatter_dimension=0, tiled=True),
        lax.psum_scatter(gain_terms, ("img", "head"), scatter_dimension=1, tiled=True),
        lax.psum_scatter(bias_terms, ("img", "head"), scatter_dimension=1, tiled=True),
    )
    media_grad = media_grad_full.astype(jnp.bfloat16).reshape(media_patches.shape)
    latent_grad = latent_grad_full.astype(jnp.bfloat16).reshape(latent_rows.shape)
    return (
        new_latents,
        media_grad,
        latent_grad,
        summed[3],
        summed[4],
        summed[0],
        summed[1],
        summed[2],
        up_grad,
        down_grad,
    )


def tpose(values):
    return jnp.transpose(values, (1, 0))


def dot_nn(left_side, right_side):
    return jnp.dot(left_side, right_side, preferred_element_type=jnp.float32)


def block_kernel(
    counts,
    media_in,
    latent_in,
    cot_in,
    query_in,
    key_value_in,
    output_in,
    up_in,
    down_in,
    gain_in,
    bias_in,
    delta_v,
    media_v,
    latent_v,
    norm_out,
    query_out,
    key_value_out,
    output_out,
    up_out,
    down_out,
    slab,
    query_full,
    wide,
    hid,
    cotr,
    turned,
    media_n,
    latent_n,
    media_t,
    latent_t,
    kv_media,
    kv_latent,
    query_v,
    att_v,
    att_t,
    mid_v,
    pair,
    grads,
    xrecv,
    zrecv,
    hsend,
    hrecv,
    hysend,
    hyrecv,
    hown,
    attg_v,
    qgrad_v,
    normg,
    normv,
    gacc,
    gsend,
    gyr,
    gzr,
    gzr_v,
    loc,
    at_z,
    at_x,
    at_y,
    at_c,
    ff_z,
    ff_x,
    nb_z,
    nb_x,
    nb_y,
    nb_c,
    hd_y,
    hd_c,
    hd_f,
    bg_y,
    bg_c,
    hp_c,
    hp_y,
    rf_x,
    rf_z,
    ra_c,
    ra_y,
    ra_x,
    ra_z,
    gr_c,
    gr_z,
    sent,
):
    n_z, n_x, n_head = 4, 2, 4
    img = lax.axis_index("img")
    head = lax.axis_index("head")
    z = img // n_x
    x = img % n_x
    y = head // 2
    c = head % 2
    xp, yp, cp = 1 - x, 1 - y, 1 - c
    xdev = (z * n_x + xp, head)
    ydev = (img, yp * 2 + c)
    cdev = (img, y * 2 + cp)
    near = (1, 3, 2)
    z1 = z + 1 - 2 * (z % 2)
    z2 = (z + 2) % n_z
    z3 = n_z - 1 - z
    mid = jnp.logical_and(z >= 1, z <= 2)

    def zat(k):
        return (z + k) % n_z

    def zdev(zz):
        return (zz * n_x + x, head)

    width = media_v.shape[2]
    slots = latent_v.shape[0]
    queries = latent_v.shape[1]
    hidden = up_in.shape[1]
    inner = query_full.shape[3]
    f32 = jnp.float32
    bf16 = jnp.bfloat16
    scale = (inner // HEADS) ** (-0.5)

    def rcopy(src, dst, sem_s, sem_r, dev):
        return pltpu.make_async_remote_copy(
            src_ref=src,
            dst_ref=dst,
            send_sem=sem_s,
            recv_sem=sem_r,
            device_id=dev,
            device_id_type=pl.DeviceIdType.MESH,
        )

    def send(src, dst, sem_s, sem_r, dev):
        rcopy(src, dst, sem_s, sem_r, dev).start()

    def arrived(ref, sem):
        pltpu.make_async_copy(ref, ref, sem).wait()

    unit = img * n_head + head
    local = [
        pltpu.make_async_copy(key_value_in, slab.at[unit, 0:32], loc.at[0]),
        pltpu.make_async_copy(output_in, slab.at[unit, 32:48], loc.at[1]),
        pltpu.make_async_copy(query_in.at[0:16], slab.at[unit, 48:64, 0:inner], loc.at[2]),
        pltpu.make_async_copy(query_in.at[16:32], slab.at[unit, 48:64, inner:width], loc.at[3]),
        pltpu.make_async_copy(up_in.at[:, 0:256], wide.at[0, img, :, 0:256], loc.at[4]),
        pltpu.make_async_copy(cot_in, pair.at[0:slots], loc.at[5]),
        pltpu.make_async_copy(latent_in, latent_v, loc.at[6]),
        pltpu.make_async_copy(media_in, media_v, loc.at[7]),
    ] + [
        pltpu.make_async_copy(
            up_in.at[:, q * 256 : (q + 1) * 256], wide.at[q, img, :, 0:256], loc.at[7 + q]
        )
        for q in range(1, 4)
    ]
    for copy in local:
        copy.start()

    barrier = pltpu.get_barrier_semaphore()
    peers = [zdev(zat(k)) for k in near] + [xdev, ydev, cdev]
    for dev in peers:
        pl.semaphore_signal(barrier, inc=1, device_id=dev, device_id_type=pl.DeviceIdType.MESH)
    pl.semaphore_wait(barrier, len(peers))

    def lanes(ii):
        return pl.ds(pl.multiple_of(ii * 128, 128), 128)

    part = gain_in.shape[1]
    norm_own = normg.at[head, :, lanes(img)]
    normv[:, 0:128] = jnp.zeros((8, 128), f32)
    normv[0:3, 0:part] = gain_in[...].astype(f32)
    normv[3:6, 0:part] = bias_in[...].astype(f32)
    norm_own[...] = pltpu.roll(normv[:, 0:128], head * part, 1)
    for k in near:
        send(norm_own, norm_own, sent.at[0], nb_z.at[z], zdev(zat(k)))
    for copy in local[0:4]:
        copy.wait()

    def put_slab(uu, sem, dev):
        send(slab.at[uu], slab.at[uu], sent.at[1], sem, dev)

    def put_line(ii):
        uu = ii * n_head + head
        put_slab(uu, at_z.at[z, ii % n_x], zdev(z2))
        put_slab(uu, at_z.at[z, ii % n_x], zdev(z1))

        @pl.when(mid)
        def _():
            put_slab(uu, at_z.at[z, ii % n_x], zdev(z3))

    def put_chip(ii):
        uu = ii * n_head + head
        put_slab(uu, at_y.at[ii], ydev)
        put_slab(uu, at_c.at[ii, y], cdev)

    put_slab(unit, at_x.at[0], xdev)
    put_line(img)
    put_chip(img)

    for copy in [local[4]] + local[8:11]:
        copy.wait()
    down = down_in[...]
    for j in range(hidden // 128):
        at = 256 + (j % 2) * 128
        wide[j // 2, img, :, at : at + 128] = tpose(down[j * 128 : (j + 1) * 128, :])

    local[5].wait()
    filled = counts[0]
    for m in range(slots):
        keep = jnp.clip(filled - m, 0, 1).astype(f32)
        cotr[head * slots + m] = (pair[m].astype(f32) * keep).astype(bf16)

    def nb_wait(kind, idx, ref):
        arrived(ref, kind.at[idx])

    for k in near:
        zz = zat(k)
        arrived(normg.at[head, :, lanes(zz * n_x + x)], nb_z.at[zz])
    for k in (0,) + near:
        zz = zat(k)
        ii = zz * n_x + x
        send(normg.at[head, :, lanes(ii)], normg.at[head, :, lanes(ii)], sent.at[2], nb_x.at[zz], xdev)

    def at_forward_x():
        ii = z * n_x + xp
        arrived(slab.at[ii * n_head + head], at_x.at[0])
        put_line(ii)
        put_chip(ii)

    def at_forward_z(zz, xx, onward):
        ii = zz * n_x + xx
        uu = ii * n_head + head
        arrived(slab.at[uu], at_z.at[zz, xx])
        if onward:

            @pl.when(mid)
            def _():
                put_slab(uu, at_z.at[zz, xx], zdev(z1))

        put_chip(ii)

    def at_forward_y(ii):
        uu = ii * n_head + yp * 2 + c
        arrived(slab.at[uu], at_y.at[ii])
        put_slab(uu, at_c.at[ii, yp], cdev)

    def ff_unit(q, ii):
        return wide.at[q, ii]

    def ff_own_z(q):
        piece = ff_unit(q, img)
        send(piece, piece, sent.at[5], ff_z.at[z, q], zdev(z2))
        send(piece, piece, sent.at[5], ff_z.at[z, q], zdev(z1))

        @pl.when(mid)
        def _():
            send(piece, piece, sent.at[5], ff_z.at[z, q], zdev(z3))

    def ff_own_x(q):
        piece = ff_unit(q, img)
        send(piece, piece, sent.at[6], ff_x.at[z, q], xdev)

    def ff_forward(e):
        q, k = e // 3, e % 3
        zz = (z2 * (2 - k) * (1 - k) + z1 * 2 * k * (2 - k) + z3 * k * (k - 1)) // 2
        piece = ff_unit(q, zz * n_x + x)
        arrived(piece, ff_z.at[zz, q])

        @pl.when(jnp.logical_and(mid, k == 0))
        def _():
            send(piece, piece, sent.at[5], ff_z.at[zz, q], zdev(z1))

        send(piece, piece, sent.at[6], ff_x.at[zz, q], xdev)

    for q in range(4):
        ff_own_x(q)
    at_forward_x()
    for k in (0,) + near:
        zz = zat(k)
        arrived(normg.at[head, :, lanes(zz * n_x + xp)], nb_x.at[zz])
    send(normg.at[head], normg.at[head], sent.at[3], nb_y.at[0], ydev)
    send(normg.at[head], normg.at[head], sent.at[4], nb_c.at[y], cdev)
    at_forward_z(z2, x, True)
    at_forward_z(z1, x, False)
    at_forward_z(z3, x, False)
    arrived(normg.at[yp * 2 + c], nb_y.at[0])
    send(normg.at[yp * 2 + c], normg.at[yp * 2 + c], sent.at[4], nb_c.at[yp], cdev)
    at_forward_z(z2, xp, True)
    for q in range(2):
        ff_own_z(q)
    own_cot = cotr.at[pl.ds(head * slots, slots)]

    arrived(normg.at[y * 2 + cp], nb_c.at[y])
    arrived(normg.at[yp * 2 + cp], nb_c.at[yp])
    normv[...] = normg[0] + normg[1] + normg[2] + normg[3]

    def gain(j):
        return normv[j : j + 1, :]

    def shift(j):
        return normv[3 + j : 4 + j, :]

    def statistics(values):
        centered = values - jnp.mean(values, axis=-1, keepdims=True)
        inverse = lax.rsqrt(jnp.mean(centered * centered, axis=-1, keepdims=True) + 1e-05)
        return centered * inverse, inverse

    def norm_rows(values, j):
        return (statistics(values)[0] * gain(j) + shift(j)).astype(bf16)

    half = queries // 2

    def norm_latent(m, carry):
        for r in range(2):
            rows = slice(r * half, (r + 1) * half)
            latent_n[m, rows, :] = norm_rows(latent_v[m, rows, :].astype(f32), 1)
        return carry

    def norm_media(m, carry):
        for r in range(2):
            rows = slice(r * half, (r + 1) * half)
            media_n[m, rows, :] = norm_rows(media_v[m, rows, :].astype(f32), 0)
        return carry

    local[6].wait()
    lax.fori_loop(0, slots, norm_latent, 0)
    at_forward_z(z1, xp, False)
    at_forward_y(img)
    at_forward_y(z * n_x + xp)
    at_forward_z(z3, xp, False)
    send(own_cot, own_cot, sent.at[7], bg_y.at[0], ydev)
    send(own_cot, own_cot, sent.at[7], bg_c.at[y], cdev)
    local[7].wait()
    blocks = media_v.shape[0]
    step = blocks // 4
    order = [z2 * n_x + x, z1 * n_x + x, z3 * n_x + x, z2 * n_x + xp, z1 * n_x + xp, z3 * n_x + xp]
    for r in range(4):
        lax.fori_loop(r * step, (r + 1) * step, norm_media, 0)
        at_forward_y(order[r])

    def turn_media(r, carry):
        block = media_n[pl.ds(r * 2, 2)].reshape(128, width)
        for d in range(width // 128):
            media_t[d * 128 : (d + 1) * 128, pl.ds(pl.multiple_of(r * 128, 128), 128)] = tpose(
                block[:, d * 128 : (d + 1) * 128]
            )
        return carry

    rows_latent = slots * queries

    def turn_latent(source, target, columns):
        whole = source[...].reshape(rows_latent, columns)
        for r in range(0, rows_latent, 128):
            stop = min(r + 128, rows_latent)
            for d in range(columns // 128):
                target[d * 128 : (d + 1) * 128, r:stop] = tpose(
                    whole[r:stop, d * 128 : (d + 1) * 128]
                )

    turn_latent(latent_n, latent_t, width)
    lax.fori_loop(0, blocks * queries // 128, turn_media, 0)
    ff_forward(0)
    at_forward_y(order[4])
    ff_forward(1)
    at_forward_y(order[5])

    for ii in range(8):
        for yy in range(2):
            arrived(slab.at[ii * n_head + yy * 2 + cp], at_c.at[ii, yy])
    ff_forward(2)
    ff_own_z(2)

    query_full[:, 0] = slab[:, 48:64, 0:inner]
    query_full[:, 1] = slab[:, 48:64, inner:width]

    def query_tile(cols):
        return query_full[:, :, :, cols].reshape(width, -1)

    def kv_tile(cols):
        return slab[:, 0:32, cols].reshape(width, -1)

    def out_tile(cols):
        return slab[:, 32:48, cols].reshape(inner, -1)

    latent_rows_n = latent_n[...].reshape(rows_latent, width)

    def tile(t):
        return pl.ds(pl.multiple_of(t * 256, 256), 256)

    query_v[...] = (
        (dot_nn(latent_rows_n, query_full[...].reshape(width, inner)) * scale)
        .astype(bf16)
        .reshape(slots, queries, inner)
    )
    groups = kv_media.shape[0]
    media_rows_n = media_n[...].reshape(groups * 256, width)

    def kv_step(t, carry):
        weight = kv_tile(tile(t))
        kv_latent[:, :, tile(t)] = dot_nn(latent_rows_n, weight).astype(bf16).reshape(slots, queries, 256)
        kv_media[:, :, tile(t)] = dot_nn(media_rows_n, weight).astype(bf16).reshape(groups, 256, 256)
        return carry

    def kv_two(i, carry):
        ff_forward(3 + i)
        return lax.fori_loop(2 * i, 2 * i + 2, kv_step, carry)

    lax.fori_loop(0, width // 512, kv_two, 0)
    ff_forward(5)
    ff_own_z(3)

    def lane_mask(hh, dtype):
        lane = lax.broadcasted_iota(jnp.int32, (1, 256), 1)
        return (lane // queries == hh).astype(f32).astype(dtype)

    def spread(rows):
        return jnp.concatenate([rows * lane_mask(hh, bf16) for hh in range(4)], axis=0)

    def fold(rows):
        total = rows[0:queries] * lane_mask(0, f32)
        for hh in range(1, 4):
            total = total + rows[hh * queries : (hh + 1) * queries] * lane_mask(hh, f32)
        return total

    def probabilities(m, g):
        q_rows = spread(query_v[m, :, tile(g)])
        k_media = kv_media[m, :, tile(g)]
        k_latent = kv_latent[m, :, tile(g)]
        s_media = contract_cols(q_rows, k_media)
        s_latent = contract_cols(q_rows, k_latent)
        top = jnp.maximum(
            jnp.max(s_media, axis=-1, keepdims=True), jnp.max(s_latent, axis=-1, keepdims=True)
        )
        e_media = jnp.exp(s_media - top)
        e_latent = jnp.exp(s_latent - top)
        total = jnp.sum(e_media, axis=-1, keepdims=True) + jnp.sum(e_latent, axis=-1, keepdims=True)
        inverse = 1.0 / total
        return q_rows, k_media, k_latent, e_media * inverse, e_latent * inverse

    def attend(m, g):
        p_media, p_latent = probabilities(m, g)[3:]
        v_media = kv_media[m, :, tile(g + 2)]
        v_latent = kv_latent[m, :, tile(g + 2)]
        rows = dot_nn(p_media.astype(bf16), v_media) + dot_nn(p_latent.astype(bf16), v_latent)
        att_v[m, :, tile(g)] = fold(rows).astype(bf16)

    def forward_image(m, carry):
        attend(m, 0)
        attend(m, 1)
        mid_v[m] = latent_v[m].astype(f32) + dot_nn(att_v[m], out_tile(slice(0, width)))
        for r in range(2):
            rows = slice(r * half, (r + 1) * half)
            hid[head * slots + m, rows, :] = norm_rows(mid_v[m, rows, :], 2)
        piece = hid.at[head * slots + m]
        send(piece, piece, sent.at[8], hd_y.at[m], ydev)
        send(piece, piece, sent.at[8], hd_c.at[m], cdev)

        @pl.when(jnp.logical_and(m >= 1, m <= 3))
        def _():
            ff_forward(5 + m)

        return carry

    lax.fori_loop(0, slots, forward_image, 0)

    other = yp * 2 + c
    cot_other = cotr.at[pl.ds(other * slots, slots)]
    arrived(cot_other, bg_y.at[0])
    send(cot_other, cot_other, sent.at[7], bg_c.at[yp], cdev)
    turn_latent(att_v, att_t, inner)
    for yy in (y, yp):
        arrived(cotr.at[pl.ds((yy * 2 + cp) * slots, slots)], bg_c.at[yy])

    all_rows = n_head * slots * queries

    def turn_rows(source, slot):
        def body(r, carry):
            block = source[pl.ds(r * 2, 2)].reshape(128, width)
            for d in range(width // 128):
                turned[slot, d * 128 : (d + 1) * 128, pl.ds(pl.multiple_of(r * 128, 128), 128)] = tpose(
                    block[:, d * 128 : (d + 1) * 128]
                )
            return carry

        lax.fori_loop(0, all_rows // 128, body, 0)

    turn_rows(cotr, 1)

    act_at = 4 * slots

    def ff_rows(q, start):
        rows = pl.ds(start, 2 * slots)
        pre = dot_nn(hid[rows].reshape(all_rows // 2, width), wide[q, :, :, 0:256].reshape(width, 256))
        grad = dot_nn(cotr[rows].reshape(all_rows // 2, width), wide[q, :, :, 256:512].reshape(width, 256))
        below = 0.5 * (1.0 + lax.erf(pre * 0.7071067811865476))
        slope = below + pre * (jnp.exp(-0.5 * pre * pre) * 0.3989422804014327)
        pair[rows, :, tile(q)] = (grad * slope).astype(bf16).reshape(2 * slots, queries, 256)
        pair[pl.ds(act_at + start, 2 * slots), :, tile(q)] = (
            (pre * below).astype(bf16).reshape(2 * slots, queries, 256)
        )

    def ff_near(q, carry):
        for zz in range(n_z):
            arrived(ff_unit(q, zz * n_x + xp), ff_x.at[zz, q])
        ff_rows(q, y * 2 * slots)
        return carry

    def ff_far(q, carry):
        ff_rows(q, yp * 2 * slots)
        return carry

    def hid_near(m, carry):
        arrived(hid.at[(y * 2 + cp) * slots + m], hd_c.at[m])
        return carry

    def hid_forward(m, carry):
        piece = hid.at[other * slots + m]
        arrived(piece, hd_y.at[m])
        send(piece, piece, sent.at[8], hd_f.at[m], cdev)
        return carry

    def hid_far(m, carry):
        arrived(hid.at[(yp * 2 + cp) * slots + m], hd_f.at[m])
        return carry

    def grad_tile(q, carry):
        def over_parts(part, carry2):
            right = pair[pl.ds(part * act_at, act_at), :, tile(q)].reshape(all_rows, 256)
            value = dot_nn(turned[part], right).astype(bf16).reshape(n_z, n_x, 128, 256)
            grads[q, part, 0] = value[:, 0]
            grads[q, part, 1] = value[:, 1]
            send(grads.at[q, part, xp], xrecv.at[q, part], sent.at[11], rf_x.at[q, part], xdev)
            return carry2

        return lax.fori_loop(0, 2, over_parts, carry)

    def ff_near_and_forward(q, carry):
        ff_near(q, 0)
        ff_forward(9 + q)
        return carry

    lax.fori_loop(0, slots, hid_near, 0)
    lax.fori_loop(0, 3, ff_near_and_forward, 0)
    lax.fori_loop(0, slots, hid_forward, 0)
    lax.fori_loop(0, slots, hid_far, 0)
    lax.fori_loop(0, 3, ff_far, 0)
    turn_rows(hid, 0)
    grad_tile(0, 0)
    ff_near(3, 0)
    ff_far(3, 0)

    def wide_rows(part, q, t):
        return wide[q, pl.ds(t * 4, 4), :, part * 256 : (part + 1) * 256].reshape(512, 256)

    def broad(t):
        return pl.ds(pl.multiple_of(t * 512, 512), 512)

    def back_rows(left, part, t):
        total = contract_cols(left[:, 0:256], wide_rows(part, 0, t))
        for q in range(1, 4):
            total = total + contract_cols(left[:, q * 256 : (q + 1) * 256], wide_rows(part, q, t))
        return total

    def head_sum(part):
        def rows_of(hh):
            return pair[pl.ds(part * act_at + hh * slots, slots)].reshape(rows_latent, hidden)

        for slot, hh in enumerate((yp * 2 + cp, y * 2 + cp)):
            left = rows_of(hh)

            def to_core(t, carry, left=left, slot=slot):
                value = back_rows(left, part, t)
                hsend[slot, :, :, broad(t)] = value.astype(bf16).reshape(slots, queries, 512)
                return carry

            lax.fori_loop(0, width // 512, to_core, 0)
            send(hsend.at[slot], hrecv.at[part, slot], sent.at[9], hp_c.at[part, slot], cdev)
        left_y = rows_of(yp * 2 + c)
        arrived(hrecv.at[part, 0], hp_c.at[part, 0])

        def to_y(t, carry):
            value = back_rows(left_y, part, t).reshape(slots, queries, 512)
            hysend[part, t] = (value + hrecv[part, 0, :, :, broad(t)].astype(f32)).astype(bf16)
            send(hysend.at[part, t], hyrecv.at[part, t], sent.at[10], hp_y.at[part], ydev)
            return carry

        lax.fori_loop(0, width // 512, to_y, 0)
        left_own = rows_of(head)
        arrived(hrecv.at[part, 1], hp_c.at[part, 1])

        def to_own(t, carry):
            value = back_rows(left_own, part, t).reshape(slots, queries, 512)
            hown[part, :, :, broad(t)] = value + hrecv[part, 1, :, :, broad(t)].astype(f32)
            return carry

        lax.fori_loop(0, width // 512, to_own, 0)

    arrived(hid.at[0 : 3 * slots], sent.at[8])
    head_sum(0)

    def sum_tile(u):
        q, part = u // 2, u % 2
        arrived(xrecv.at[q, part], rf_x.at[q, part])
        for k, zz in enumerate((z1, z2, z3)):
            grads[q, part, x, zz] = (
                grads[q, part, x, zz].astype(f32) + xrecv[q, part, zz].astype(f32)
            ).astype(bf16)
            send(grads.at[q, part, x, zz], zrecv.at[k, part, q], sent.at[12], rf_z.at[k, part], zdev(zz))

    grad_tile(1, 0)
    sum_tile(0)
    arrived(hsend, sent.at[9])
    head_sum(1)
    lax.fori_loop(2, 4, grad_tile, 0)
    sum_tile(1)

    gacc[...] = jnp.zeros_like(gacc)

    def tally(j, upper, xhat):
        gacc[j] += jnp.sum((upper * xhat).reshape(-1, 8, width), axis=0)
        gacc[3 + j] += jnp.sum(upper.reshape(-1, 8, width), axis=0)

    def norm_back(values, j, upper):
        xhat, inverse = statistics(values)
        tally(j, upper, xhat)
        g = upper * gain(j)
        return inverse * (
            g - jnp.mean(g, axis=-1, keepdims=True) - xhat * jnp.mean(g * xhat, axis=-1, keepdims=True)
        )

    sum_tile(2)
    arrived(hyrecv.at[0], hp_y.at[0])

    def mid_back(m, carry):
        upper = hown[0, m] + jnp.concatenate([hyrecv[0, 0, m], hyrecv[0, 1, m]], axis=-1).astype(f32)
        back = norm_back(mid_v[m], 2, upper)
        total = cotr[head * slots + m].astype(f32) + back
        hown[0, m] = total
        delta_v[m] = total.astype(bf16)
        return carry

    lax.fori_loop(0, slots, mid_back, 0)
    delta_rows = delta_v[...].reshape(rows_latent, width)

    attg_v[...] = (
        contract_cols(delta_rows, out_tile(slice(0, width))).astype(bf16).reshape(slots, queries, inner)
    )

    gslab = pair

    def gunit(ii, hh_y, hh_c):
        return ii * 4 + hh_c * 2 + hh_y

    def out_grad_step(t, carry):
        right = delta_v[:, :, broad(t)].reshape(rows_latent, 512)
        value = dot_nn(att_t[...], right).astype(bf16)
        for ii in range(8):
            for hh in range(4):
                at = (ii * 4 + hh) * 16
                gslab[gunit(ii, hh // 2, hh % 2), 32:48, broad(t)] = value[at : at + 16]
        return carry

    lax.fori_loop(0, width // 512, out_grad_step, 0)
    sum_tile(3)

    def back_pair(m, g):
        q_rows, k_media, k_latent, p_media, p_latent = probabilities(m, g)
        v_media = kv_media[m, :, tile(g + 2)]
        v_latent = kv_latent[m, :, tile(g + 2)]
        up_rows = spread(attg_v[m, :, tile(g)])
        g_media = contract_cols(up_rows, v_media)
        g_latent = contract_cols(up_rows, v_latent)
        dotted = jnp.sum(g_media * p_media, axis=-1, keepdims=True) + jnp.sum(
            g_latent * p_latent, axis=-1, keepdims=True
        )
        d_media = (p_media * (g_media - dotted)).astype(bf16)
        d_latent = (p_latent * (g_latent - dotted)).astype(bf16)
        qgrad_v[m, :, tile(g)] = fold(dot_nn(d_media, k_media) + dot_nn(d_latent, k_latent)).astype(bf16)
        kv_media[m, :, tile(g)] = contract_rows(d_media, q_rows).astype(bf16)
        kv_latent[m, :, tile(g)] = contract_rows(d_latent, q_rows).astype(bf16)
        kv_media[m, :, tile(g + 2)] = contract_rows(p_media.astype(bf16), up_rows).astype(bf16)
        kv_latent[m, :, tile(g + 2)] = contract_rows(p_latent.astype(bf16), up_rows).astype(bf16)

    def back_image(m, carry):
        back_pair(m, 0)
        back_pair(m, 1)
        return carry

    lax.fori_loop(0, slots, back_image, 0)

    sum_tile(4)

    gcr = hid
    gyr_v = media_n

    def kv_grad_chunk(zz):
        rows = pl.ds(pl.multiple_of(zz * 256, 256), 256)
        left_media = media_t[rows, :]
        left_latent = latent_t[rows, :]

        value = dot_nn(left_media, kv_media[...].reshape(groups * 256, width)) + dot_nn(
            left_latent, kv_latent[...].reshape(rows_latent, width)
        )
        value = value.astype(bf16)
        value_q = dot_nn(left_latent, qgrad_v[...].reshape(rows_latent, inner)) * scale
        value_q = value_q.astype(bf16)
        for xx in range(2):
            for hh in range(4):
                at = (xx * 4 + hh) * 32
                uu = gunit(zz * n_x + xx, hh // 2, hh % 2)
                gslab[uu, 0:32, :] = value[at : at + 32]
                gslab[uu, 48:64, 0:inner] = value_q[at : at + 16]
                gslab[uu, 48:64, inner:width] = value_q[at + 16 : at + 32]
        for xx in range(2):
            ii = zz * n_x + xx
            send(
                gslab.at[pl.ds(ii * 4 + cp * 2, 2)],
                gcr.at[pl.ds(ii * 2, 2)],
                sent.at[13],
                ra_c.at[ii],
                cdev,
            )

    def stage_y(zz):
        for xx in (xp, x):
            ii = zz * n_x + xx
            arrived(gcr.at[pl.ds(ii * 2, 2)], ra_c.at[ii])
            uu = gunit(ii, yp, c)
            gslab[uu] = (gslab[uu].astype(f32) + gcr[ii * 2 + yp].astype(f32)).astype(bf16)
            send(gslab.at[uu], gyr_v.at[ii], sent.at[14], ra_y.at[ii], ydev)

    def upto_y(ii):
        return (
            gslab[gunit(ii, y, c)].astype(f32) + gcr[ii * 2 + y].astype(f32) + gyr_v[ii].astype(f32)
        )

    def stage_x(zz):
        ii = zz * n_x + xp
        arrived(gyr_v.at[ii], ra_y.at[ii])
        uu = gunit(ii, y, c)
        gslab[uu] = upto_y(ii).astype(bf16)
        send(gslab.at[uu], gyr_v.at[8 + zz], sent.at[15], ra_x.at[zz], xdev)

    def stage_z(zz, last):
        ii = zz * n_x + x
        arrived(gyr_v.at[ii], ra_y.at[ii])
        arrived(gyr_v.at[8 + zz], ra_x.at[zz])
        if last:
            return upto_y(ii) + gyr_v[8 + zz].astype(f32)
        uu = gunit(ii, y, c)
        gslab[uu] = (upto_y(ii) + gyr_v[8 + zz].astype(f32)).astype(bf16)
        send(gslab.at[uu], gzr_v.at[z], sent.at[16], ra_z.at[z], zdev(zz))
        return None

    chunk = [zat(1), zat(3), zat(2), z]
    kv_grad_chunk(chunk[0])
    kv_grad_chunk(chunk[1])
    stage_y(chunk[0])
    kv_grad_chunk(chunk[2])
    stage_y(chunk[1])
    kv_grad_chunk(chunk[3])
    stage_y(chunk[2])
    sum_tile(5)

    arrived(hyrecv.at[1], hp_y.at[1])
    new_v = delta_v

    for m in range(slots):
        keep = jnp.clip(filled - m, 0, 1).astype(f32)
        for r in range(2):
            rows = slice(r * half, (r + 1) * half)
            branch = hown[1, m, rows, :] + jnp.concatenate(
                [hyrecv[1, 0, m, rows, :], hyrecv[1, 1, m, rows, :]], axis=-1
            ).astype(f32)
            new_v[m, rows, :] = ((mid_v[m, rows, :] + branch) * keep).astype(bf16)
    stage_y(chunk[3])

    def media_back(m, carry):
        hown[1, 0:4] = contract_cols(kv_media[m], kv_tile(slice(0, width))).reshape(4, 64, width)

        def over_rows(r, carry2):
            block = m * 4 + r
            back = norm_back(media_v[block].astype(f32), 0, hown[1, r])
            media_v[block] = back.astype(bf16)
            return carry2

        lax.fori_loop(0, 4, over_rows, 0)
        return carry

    def latent_back_tiles(t, carry):
        weight = slab[pl.ds(t * 16, 16), 0:32, :].reshape(512, width)
        query_weight = query_full[pl.ds(t * 16, 16)].reshape(512, inner)
        hown[1, :, :, broad(t)] = (
            contract_cols(kv_latent[...].reshape(rows_latent, width), weight)
            + contract_cols(qgrad_v[...].reshape(rows_latent, inner), query_weight) * scale
        ).reshape(slots, queries, 512)
        return carry

    def latent_back(m, carry):
        back = norm_back(latent_v[m].astype(f32), 1, hown[1, m])
        latent_v[m] = (hown[0, m] + back).astype(bf16)
        return carry

    lax.fori_loop(0, width // 512, latent_back_tiles, 0)
    lax.fori_loop(0, slots, latent_back, 0)
    sum_tile(6)
    lax.fori_loop(0, 2, media_back, 0)
    sum_tile(7)
    stage_x(chunk[0])
    lax.fori_loop(2, 4, media_back, 0)
    stage_x(chunk[1])
    stage_z(chunk[0], False)
    lax.fori_loop(4, 5, media_back, 0)

    for j in range(6):
        gsend[0, j : j + 1, :] = jnp.sum(gacc[j], axis=0, keepdims=True)
    gsend[0, 6:8, :] = jnp.zeros((2, width), f32)
    send(gsend.at[0], gyr.at[0], sent.at[17], gr_c.at[0], cdev)
    arrived(gyr.at[0], gr_c.at[0])
    gsend[1] = gsend[0] + gyr[0]
    send(gsend.at[1], gyr.at[1], sent.at[17], gr_c.at[1], xdev)
    stage_z(chunk[1], False)
    arrived(gyr.at[1], gr_c.at[1])
    gsend[2] = gsend[1] + gyr[1]
    for k in near:
        zz = zat(k)
        send(gsend.at[2, :, lanes(zz * n_x + x)], gzr.at[z], sent.at[18], gr_z.at[z], zdev(zz))
    stage_x(chunk[2])
    total = gsend[2, :, lanes(img)]
    for k in near:
        zz = zat(k)
        arrived(gzr.at[zz], gr_z.at[zz])
        total = total + gzr[zz]
    gsend[3, :, 0:128] = total
    send(gsend.at[3, :, 0:128], gyr.at[2, :, 0:128], sent.at[17], gr_c.at[2], ydev)

    for part in range(2):
        for k in range(3):
            arrived(zrecv.at[k, part], rf_z.at[k, part])

    def own_sum(part, q):
        value = grads[q, part, x, z].astype(f32) + xrecv[q, part, z].astype(f32)
        for k in range(3):
            value = value + zrecv[k, part, q].astype(f32)
        return value

    def last_sums(q, carry):
        up_out[:, tile(q)] = own_sum(0, q)
        value = own_sum(1, q)
        for j in range(2):
            rows = pl.ds(pl.multiple_of(q * 256 + j * 128, 128), 128)
            down_out[rows, :] = tpose(value[:, j * 128 : (j + 1) * 128])
        return carry

    lax.fori_loop(0, hidden // 256, last_sums, 0)

    stage_x(chunk[3])
    stage_z(chunk[2], False)
    arrived(gyr.at[2, :, 0:128], gr_c.at[2])
    norm_out[...] = gsend[3, :, 0:128] + gyr[2, :, 0:128]
    final = stage_z(chunk[3], True)
    for k in near:
        zz = zat(k)
        arrived(gzr_v.at[zz], ra_z.at[zz])
        final = final + gzr_v[zz].astype(f32)
    key_value_out[...] = final[0:32]
    output_out[...] = final[32:48]
    query_out[0:16, :] = final[48:64, 0:inner]
    query_out[16:32, :] = final[48:64, inner:width]

    arrived(normg.at[0, :, 0:384], sent.at[0])
    arrived(slab.at[0:29], sent.at[1])

    @pl.when(mid)
    def _():
        arrived(slab.at[0:4], sent.at[1])
        arrived(wide.at[0], sent.at[5])

    arrived(normg.at[0, :, 0:512], sent.at[2])
    arrived(normg.at[0], sent.at[3])
    arrived(normg.at[0:2], sent.at[4])
    arrived(wide.at[0], sent.at[5])
    arrived(wide.at[0:2], sent.at[6])
    arrived(cotr.at[0 : 3 * slots], sent.at[7])
    arrived(hsend, sent.at[9])
    arrived(hysend, sent.at[10])
    arrived(xrecv, sent.at[11])
    arrived(zrecv, sent.at[12])
    arrived(gcr.at[0:16], sent.at[13])
    arrived(gyr_v.at[0:8], sent.at[14])
    arrived(gyr_v.at[0:4], sent.at[15])
    arrived(gyr_v.at[0:3], sent.at[16])
    arrived(gyr.at[0:2], sent.at[17])
    arrived(gyr.at[2, :, 0:128], sent.at[17])
    arrived(gzr.at[0:3], sent.at[18])


def finish_kernel(norms, *refs):
    sources, gains_out, biases_out, targets, sems = refs[:8], refs[8], refs[9], refs[10:18], refs[18]
    copies = [pltpu.make_async_copy(sources[i], targets[i], sems.at[i]) for i in range(8)]
    for copy in copies:
        copy.start()
    part = gains_out.shape[1]
    head = lax.axis_index("head")
    rolled = pltpu.roll(norms[...], (128 - head * part) % 128, 1)
    gains_out[...] = rolled[0:3, 0:part]
    biases_out[...] = rolled[3:6, 0:part]
    for copy in copies:
        copy.wait()


def block_plan(
    media_patches,
    latent_rows,
    media_counts,
    norm_gains,
    norm_biases,
    query_weight,
    key_value_weight,
    output_weight,
    up_weight,
    down_weight,
    cotangent,
):
    slots, patches, width = media_patches.shape[1:]
    queries = latent_rows.shape[2]
    inner = query_weight.shape[1]
    hidden = up_weight.shape[1]
    rows_up = up_weight.shape[0]
    part = norm_gains.shape[1]
    blocks = slots * patches // 64
    bf16, f32 = jnp.bfloat16, jnp.float32
    shape = jax.ShapeDtypeStruct
    hbm = pl.BlockSpec(memory_space=pl.ANY)
    vmem = pl.BlockSpec(memory_space=pltpu.VMEM)
    smem = pl.BlockSpec(memory_space=pltpu.SMEM)
    dma = pltpu.SemaphoreType.DMA
    all_rows = 4 * slots * queries
    rows_latent = slots * queries
    outs = pl.pallas_call(
        block_kernel,
        out_shape=(
            pltpu.VMEM((slots, queries, width), bf16),
            pltpu.VMEM((blocks, 64, width), bf16),
            pltpu.VMEM((slots, queries, width), bf16),
            pltpu.VMEM((8, 128), f32),
            pltpu.VMEM(query_weight.shape, f32),
            pltpu.VMEM(key_value_weight.shape, f32),
            pltpu.VMEM(output_weight.shape, f32),
            pltpu.VMEM(up_weight.shape, f32),
            pltpu.VMEM(down_weight.shape, f32),
        ),
        in_specs=[smem] + [hbm] * 7 + [vmem] * 3,
        out_specs=(vmem,) * 9,
        scratch_shapes=[
            pltpu.VMEM((32, 64, width), bf16),
            pltpu.VMEM((32, 2, 16, inner), bf16),
            pltpu.VMEM((4, 8, rows_up, 512), bf16),
            pltpu.VMEM((4 * slots, queries, width), bf16),
            pltpu.VMEM((4 * slots, queries, width), bf16),
            pltpu.VMEM((2, width, all_rows), bf16),
            pltpu.VMEM((blocks, 64, width), bf16),
            pltpu.VMEM((slots, queries, width), bf16),
            pltpu.VMEM((width, slots * patches), bf16),
            pltpu.VMEM((width, rows_latent), bf16),
            pltpu.VMEM((slots, patches, 2 * inner), bf16),
            pltpu.VMEM((slots, queries, 2 * inner), bf16),
            pltpu.VMEM((slots, queries, inner), bf16),
            pltpu.VMEM((slots, queries, inner), bf16),
            pltpu.VMEM((inner, rows_latent), bf16),
            pltpu.VMEM((slots, queries, width), f32),
            pltpu.VMEM((8 * slots, queries, width), bf16),
            pltpu.VMEM((4, 2, 2, 4, rows_up, 256), bf16),
            pltpu.VMEM((4, 2, 4, rows_up, 256), bf16),
            pltpu.VMEM((3, 2, 4, rows_up, 256), bf16),
            pltpu.VMEM((2, slots, queries, width), bf16),
            pltpu.VMEM((2, 2, slots, queries, width), bf16),
            pltpu.VMEM((2, 2, slots, queries, width // 2), bf16),
            pltpu.VMEM((2, 2, slots, queries, width // 2), bf16),
            pltpu.VMEM((2, slots, queries, width), f32),
            pltpu.VMEM((slots, queries, inner), bf16),
            pltpu.VMEM((slots, queries, inner), bf16),
            pltpu.VMEM((4, 8, width), f32),
            pltpu.VMEM((8, width), f32),
            pltpu.VMEM((6, 8, width), f32),
            pltpu.VMEM((4, 8, width), f32),
            pltpu.VMEM((3, 8, width), f32),
            pltpu.VMEM((4, 8, 128), f32),
            pltpu.VMEM((4, 64, width), bf16),
            dma((11,)),
            dma((4, 2)),
            dma((1,)),
            dma((8,)),
            dma((8, 2)),
            dma((4, 4)),
            dma((4, 4)),
            dma((4,)),
            dma((4,)),
            dma((1,)),
            dma((2,)),
            dma((slots,)),
            dma((slots,)),
            dma((slots,)),
            dma((1,)),
            dma((2,)),
            dma((2, 2)),
            dma((2,)),
            dma((4, 2)),
            dma((4, 2)),
            dma((8,)),
            dma((8,)),
            dma((4,)),
            dma((4,)),
            dma((3,)),
            dma((4,)),
            dma((19,)),
        ],
        compiler_params=pltpu.CompilerParams(
            collective_id=0, has_side_effects=True, vmem_limit_bytes=61796352
        ),
    )(
        media_counts,
        media_patches.reshape(blocks, 64, width),
        latent_rows.reshape(slots, queries, width),
        cotangent.reshape(slots, queries, width),
        query_weight,
        key_value_weight,
        output_weight,
        up_weight,
        down_weight,
        norm_gains,
        norm_biases,
    )
    norms = outs[3]
    rest = outs[:3] + outs[4:]
    done = pl.pallas_call(
        finish_kernel,
        out_shape=(shape((3, part), f32), shape((3, part), f32)) + tuple(shape(v.shape, v.dtype) for v in rest),
        in_specs=[vmem] * 9,
        out_specs=(vmem, vmem) + (hbm,) * 8,
        scratch_shapes=[dma((8,))],
        compiler_params=pltpu.CompilerParams(vmem_limit_bytes=4194304),
    )(norms, *rest)
    gains_grad, biases_grad, new, media_grad, latent_grad = done[:5]
    return (
        new.reshape(latent_rows.shape),
        media_grad.reshape(media_patches.shape),
        latent_grad.reshape(latent_rows.shape),
        gains_grad,
        biases_grad,
    ) + tuple(done[5:])


def block_fits(mesh):
    return mesh.shape["img"] == 8 and mesh.shape["head"] == 4


def solution(mesh):
    return jax.shard_map(
        block_plan if block_fits(mesh) else gathered_plan,
        mesh=mesh,
        in_specs=(
            P(("img", "head"), None, None, None),
            P(("img", "head"), None, None, None),
            P(("img", "head")),
            P(None, ("img", "head")),
            P(None, ("img", "head")),
            P(("img", "head"), None),
            P(("img", "head"), None),
            P(("img", "head"), None),
            P("img", "head"),
            P("head", "img"),
            P(("img", "head"), None, None, None),
        ),
        out_specs=(
            P(("img", "head"), None, None, None),
            P(("img", "head"), None, None, None),
            P(("img", "head"), None, None, None),
            P(None, ("img", "head")),
            P(None, ("img", "head")),
            P(("img", "head"), None),
            P(("img", "head"), None),
            P(("img", "head"), None),
            P("img", "head"),
            P("head", "img"),
        ),
        check_vma=False,
    )
```

```python
import jax
import jax.numpy as jnp
from jax import lax
from jax.experimental import pallas as pl
from jax.experimental.pallas import tpu as pltpu
from jax.sharding import PartitionSpec as P

HEADS = 8


def layer_norm(values, norm_gain, norm_shift):
    centered = values - jnp.mean(values, axis=-1, keepdims=True)
    variance = jnp.mean(centered * centered, axis=-1, keepdims=True)
    return centered * lax.rsqrt(variance + 1e-05) * norm_gain + norm_shift


def norm_backward(values, norm_gain, norm_shift, upstream):
    primal, pullback = jax.vjp(layer_norm, values, norm_gain, norm_shift)
    return pullback(upstream)


def exact_gelu(values):
    return jax.nn.gelu(values, approximate=False)


def gelu_backward(values, upstream):
    primal, pullback = jax.vjp(exact_gelu, values)
    return pullback(upstream)[0]


def contract_rows(left_side, right_side):
    return lax.dot_general(
        left_side, right_side, (((0,), (0,)), ((), ())), preferred_element_type=jnp.float32
    )


def contract_cols(left_side, right_side):
    return lax.dot_general(
        left_side, right_side, (((1,), (1,)), ((), ())), preferred_element_type=jnp.float32
    )


def gathered_plan(
    media_patches,
    latent_rows,
    media_counts,
    norm_gains,
    norm_biases,
    query_weight,
    key_value_weight,
    output_weight,
    up_weight,
    down_weight,
    cotangent,
):
    samp_local, media_slots, patches, model_width = media_patches.shape
    queries_per = latent_rows.shape[2]
    images = samp_local * media_slots
    keys_per = patches + queries_per
    rows_local = images * queries_per
    gathered = (
        lax.all_gather(query_weight, ("img", "head"), axis=0, tiled=True),
        lax.all_gather(key_value_weight, ("img", "head"), axis=0, tiled=True),
        lax.all_gather(output_weight, ("img", "head"), axis=0, tiled=True),
        lax.all_gather(norm_gains, ("img", "head"), axis=1, tiled=True),
        lax.all_gather(norm_biases, ("img", "head"), axis=1, tiled=True),
    )
    query_full, key_value_full, output_full, gains_low, biases_low = gathered
    norm_gain = gains_low.astype(jnp.float32)
    norm_shift = biases_low.astype(jnp.float32)
    inner_width = query_full.shape[1]
    head_size = inner_width // HEADS
    score_scale = head_size ** (-0.5)
    up_part, down_part = (
        lax.all_gather(up_weight, "img", axis=0, tiled=True),
        lax.all_gather(down_weight, "img", axis=1, tiled=True),
    )
    media_full = media_patches.reshape(images, patches, model_width).astype(jnp.float32)
    latent_full = latent_rows.reshape(images, queries_per, model_width).astype(jnp.float32)
    media_norm = layer_norm(media_full, norm_gain[0], norm_shift[0]).astype(jnp.bfloat16)
    latent_norm = layer_norm(latent_full, norm_gain[1], norm_shift[1]).astype(jnp.bfloat16)
    query_rows = (
        jnp.einsum("ild,de->ile", latent_norm, query_full, preferred_element_type=jnp.float32)
        * score_scale
    ).astype(jnp.bfloat16)
    key_input = jnp.concatenate([media_norm, latent_norm], axis=1)
    key_value_rows = jnp.einsum(
        "ikd,de->ike", key_input, key_value_full, preferred_element_type=jnp.float32
    ).astype(jnp.bfloat16)
    query_heads = (
        query_rows.reshape(images, queries_per, HEADS, head_size)
        .transpose(2, 0, 1, 3)
        .reshape(HEADS, images, queries_per * head_size)
    )
    key_value_heads = (
        key_value_rows.reshape(images, keys_per, 2, HEADS, head_size)
        .transpose(3, 0, 1, 2, 4)
        .reshape(HEADS, images, keys_per, 2 * head_size)
    )
    query_group, key_value_group = (
        lax.all_to_all(query_heads, "head", split_axis=0, concat_axis=1, tiled=True),
        lax.all_to_all(key_value_heads, "head", split_axis=0, concat_axis=1, tiled=True),
    )
    heads_dev = query_group.shape[0]
    group_images = query_group.shape[1]
    query_block = query_group.reshape(heads_dev, group_images, queries_per, head_size)
    key_block = key_value_group[:, :, :, :head_size]
    value_block = key_value_group[:, :, :, head_size:]
    scores = jnp.einsum(
        "hgqe,hgke->hgqk", query_block, key_block, preferred_element_type=jnp.float32
    )
    row_max = jnp.max(scores, axis=-1, keepdims=True)
    weights = jnp.exp(scores - row_max)
    totals = jnp.sum(weights, axis=-1, keepdims=True)
    log_total = row_max + jnp.log(totals)
    probabilities = (weights / totals).astype(jnp.bfloat16)
    attended = jnp.einsum(
        "hgqk,hgke->hgqe", probabilities, value_block, preferred_element_type=jnp.float32
    ).astype(jnp.bfloat16)
    attended_back = lax.all_to_all(
        attended.reshape(heads_dev, group_images, queries_per * head_size),
        "head",
        split_axis=1,
        concat_axis=0,
        tiled=True,
    )
    attended_local = (
        attended_back.reshape(HEADS, images, queries_per, head_size)
        .transpose(1, 2, 0, 3)
        .reshape(images, queries_per, inner_width)
    )
    attn_delta = jnp.einsum(
        "ile,ed->ild", attended_local, output_full, preferred_element_type=jnp.float32
    )
    mid_latent = latent_full + attn_delta
    hidden_in = (
        layer_norm(mid_latent, norm_gain[2], norm_shift[2])
        .astype(jnp.bfloat16)
        .reshape(rows_local, model_width)
    )
    slot_mask = (
        (jnp.arange(media_slots)[None, :] < media_counts[:, None])
        .astype(jnp.float32)
        .reshape(images, 1, 1)
    )
    up_full, down_full = (
        lax.all_gather(up_part, "head", axis=1, tiled=True),
        lax.all_gather(down_part, "head", axis=0, tiled=True),
    )
    pre_act = jnp.dot(hidden_in, up_full, preferred_element_type=jnp.float32)
    act_low = exact_gelu(pre_act).astype(jnp.bfloat16)
    branch_out = jnp.dot(act_low, down_full, preferred_element_type=jnp.float32)
    result = slot_mask * (mid_latent + branch_out.reshape(images, queries_per, model_width))
    new_latents = result.astype(jnp.bfloat16).reshape(latent_rows.shape)
    out_grad = slot_mask * cotangent.reshape(images, queries_per, model_width).astype(jnp.float32)
    branch_grad = out_grad.astype(jnp.bfloat16).reshape(rows_local, model_width)
    act_grad = contract_cols(branch_grad, down_full)
    pre_grad = gelu_backward(pre_act, act_grad).astype(jnp.bfloat16)
    down_grad_whole = contract_rows(act_low, branch_grad)
    up_grad_whole = contract_rows(hidden_in, pre_grad)
    hidden_grad = contract_cols(pre_grad, up_full)
    up_grad_part, down_grad_part = (
        lax.psum_scatter(
            up_grad_whole.astype(jnp.bfloat16), "head", scatter_dimension=1, tiled=True
        ).astype(jnp.float32),
        lax.psum_scatter(
            down_grad_whole.astype(jnp.bfloat16), "head", scatter_dimension=0, tiled=True
        ).astype(jnp.float32),
    )
    up_grad, down_grad = (
        lax.psum_scatter(
            up_grad_part.astype(jnp.bfloat16), "img", scatter_dimension=0, tiled=True
        ).astype(jnp.float32),
        lax.psum_scatter(
            down_grad_part.astype(jnp.bfloat16), "img", scatter_dimension=1, tiled=True
        ).astype(jnp.float32),
    )
    mid_from_norm, gain_ff, bias_ff = norm_backward(
        mid_latent,
        norm_gain[2],
        norm_shift[2],
        hidden_grad.reshape(images, queries_per, model_width),
    )
    mid_grad = out_grad + mid_from_norm
    delta_low = mid_grad.astype(jnp.bfloat16)
    output_weight_grad = jnp.einsum(
        "ile,ild->ed", attended_local, delta_low, preferred_element_type=jnp.float32
    )
    attended_grad = jnp.einsum(
        "ild,ed->ile", delta_low, output_full, preferred_element_type=jnp.float32
    ).astype(jnp.bfloat16)
    grad_heads = (
        attended_grad.reshape(images, queries_per, HEADS, head_size)
        .transpose(2, 0, 1, 3)
        .reshape(HEADS, images, queries_per * head_size)
    )
    grad_group = lax.all_to_all(
        grad_heads, "head", split_axis=0, concat_axis=1, tiled=True
    ).reshape(heads_dev, group_images, queries_per, head_size)
    scores_again = jnp.einsum(
        "hgqe,hgke->hgqk", query_block, key_block, preferred_element_type=jnp.float32
    )
    probs_again = jnp.exp(scores_again - log_total)
    probs_again_low = probs_again.astype(jnp.bfloat16)
    prob_grad = jnp.einsum(
        "hgqe,hgke->hgqk", grad_group, value_block, preferred_element_type=jnp.float32
    )
    value_grad = jnp.einsum(
        "hgqk,hgqe->hgke", probs_again_low, grad_group, preferred_element_type=jnp.float32
    )
    row_dot = jnp.sum(prob_grad * probs_again, axis=-1, keepdims=True)
    score_grad = (probs_again * (prob_grad - row_dot)).astype(jnp.bfloat16)
    query_grad_group = jnp.einsum(
        "hgqk,hgke->hgqe", score_grad, key_block, preferred_element_type=jnp.float32
    ).astype(jnp.bfloat16)
    key_grad = jnp.einsum(
        "hgqk,hgqe->hgke", score_grad, query_block, preferred_element_type=jnp.float32
    )
    key_value_grad_group = jnp.concatenate([key_grad, value_grad], axis=-1).astype(jnp.bfloat16)
    query_back, key_value_back = (
        lax.all_to_all(
            query_grad_group.reshape(heads_dev, group_images, queries_per * head_size),
            "head",
            split_axis=1,
            concat_axis=0,
            tiled=True,
        ),
        lax.all_to_all(key_value_grad_group, "head", split_axis=1, concat_axis=0, tiled=True),
    )
    query_local = (
        query_back.reshape(HEADS, images, queries_per, head_size)
        .transpose(1, 2, 0, 3)
        .reshape(images, queries_per, inner_width)
    )
    key_value_local = (
        key_value_back.reshape(HEADS, images, keys_per, 2, head_size)
        .transpose(1, 2, 3, 0, 4)
        .reshape(images, keys_per, 2 * inner_width)
    )
    query_weight_grad = (
        jnp.einsum("ild,ile->de", latent_norm, query_local, preferred_element_type=jnp.float32)
        * score_scale
    )
    key_value_weight_grad = jnp.einsum(
        "ikd,ike->de", key_input, key_value_local, preferred_element_type=jnp.float32
    )
    key_input_grad = jnp.einsum(
        "ike,de->ikd", key_value_local, key_value_full, preferred_element_type=jnp.float32
    )
    latent_norm_grad = (
        jnp.einsum("ile,de->ild", query_local, query_full, preferred_element_type=jnp.float32)
        * score_scale
        + key_input_grad[:, patches:]
    )
    media_grad_full, gain_media, bias_media = norm_backward(
        media_full, norm_gain[0], norm_shift[0], key_input_grad[:, :patches]
    )
    latent_from_norm, gain_latent, bias_latent = norm_backward(
        latent_full, norm_gain[1], norm_shift[1], latent_norm_grad
    )
    latent_grad_full = mid_grad + latent_from_norm
    gain_terms = jnp.stack([gain_media, gain_latent, gain_ff])
    bias_terms = jnp.stack([bias_media, bias_latent, bias_ff])
    summed = (
        lax.psum_scatter(query_weight_grad, ("img", "head"), scatter_dimension=0, tiled=True),
        lax.psum_scatter(key_value_weight_grad, ("img", "head"), scatter_dimension=0, tiled=True),
        lax.psum_scatter(output_weight_grad, ("img", "head"), scatter_dimension=0, tiled=True),
        lax.psum_scatter(gain_terms, ("img", "head"), scatter_dimension=1, tiled=True),
        lax.psum_scatter(bias_terms, ("img", "head"), scatter_dimension=1, tiled=True),
    )
    media_grad = media_grad_full.astype(jnp.bfloat16).reshape(media_patches.shape)
    latent_grad = latent_grad_full.astype(jnp.bfloat16).reshape(latent_rows.shape)
    return (
        new_latents,
        media_grad,
        latent_grad,
        summed[3],
        summed[4],
        summed[0],
        summed[1],
        summed[2],
        up_grad,
        down_grad,
    )


def tpose(values):
    return jnp.transpose(values, (1, 0))


def dot_nn(left_side, right_side):
    return jnp.dot(left_side, right_side, preferred_element_type=jnp.float32)


def block_kernel(
    counts,
    media_in,
    latent_in,
    cot_in,
    query_in,
    key_value_in,
    output_in,
    up_in,
    down_in,
    gain_in,
    bias_in,
    delta_v,
    media_v,
    latent_v,
    norm_out,
    query_out,
    key_value_out,
    output_out,
    up_out,
    down_out,
    slab,
    query_full,
    wide,
    hid,
    cotr,
    turned,
    media_n,
    latent_n,
    media_t,
    latent_t,
    kv_media,
    kv_latent,
    query_v,
    att_v,
    att_t,
    mid_v,
    pair,
    grads,
    xrecv,
    zrecv,
    hsend,
    hrecv,
    hysend,
    hyrecv,
    hown,
    attg_v,
    qgrad_v,
    normg,
    normv,
    gacc,
    gsend,
    gyr,
    gzr,
    gzr_v,
    loc,
    at_z,
    at_x,
    at_y,
    at_c,
    ff_z,
    ff_x,
    nb_z,
    nb_x,
    nb_y,
    nb_c,
    hd_y,
    hd_c,
    hd_f,
    bg_y,
    bg_c,
    hp_c,
    hp_y,
    rf_x,
    rf_z,
    ra_c,
    ra_y,
    ra_x,
    ra_z,
    gr_c,
    gr_z,
    sent,
):
    n_z, n_x, n_head = 4, 2, 4
    img = lax.axis_index("img")
    head = lax.axis_index("head")
    z = img // n_x
    x = img % n_x
    y = head // 2
    c = head % 2
    xp, yp, cp = 1 - x, 1 - y, 1 - c
    xdev = (z * n_x + xp, head)
    ydev = (img, yp * 2 + c)
    cdev = (img, y * 2 + cp)
    near = (1, 3, 2)
    z1 = z + 1 - 2 * (z % 2)
    z2 = (z + 2) % n_z
    z3 = n_z - 1 - z
    mid = jnp.logical_and(z >= 1, z <= 2)

    def zat(k):
        return (z + k) % n_z

    def zdev(zz):
        return (zz * n_x + x, head)

    width = media_v.shape[2]
    slots = latent_v.shape[0]
    queries = latent_v.shape[1]
    hidden = up_in.shape[1]
    inner = query_full.shape[3]
    f32 = jnp.float32
    bf16 = jnp.bfloat16
    scale = (inner // HEADS) ** (-0.5)

    def rcopy(src, dst, sem_s, sem_r, dev):
        return pltpu.make_async_remote_copy(
            src_ref=src,
            dst_ref=dst,
            send_sem=sem_s,
            recv_sem=sem_r,
            device_id=dev,
            device_id_type=pl.DeviceIdType.MESH,
        )

    def send(src, dst, sem_s, sem_r, dev):
        rcopy(src, dst, sem_s, sem_r, dev).start()

    def arrived(ref, sem):
        pltpu.make_async_copy(ref, ref, sem).wait()

    unit = img * n_head + head
    local = [
        pltpu.make_async_copy(key_value_in, slab.at[unit, 0:32], loc.at[0]),
        pltpu.make_async_copy(output_in, slab.at[unit, 32:48], loc.at[1]),
        pltpu.make_async_copy(query_in.at[0:16], slab.at[unit, 48:64, 0:inner], loc.at[2]),
        pltpu.make_async_copy(query_in.at[16:32], slab.at[unit, 48:64, inner:width], loc.at[3]),
        pltpu.make_async_copy(up_in.at[:, 0:256], wide.at[0, img, :, 0:256], loc.at[4]),
        pltpu.make_async_copy(cot_in, pair.at[0:slots], loc.at[5]),
        pltpu.make_async_copy(latent_in, latent_v, loc.at[6]),
        pltpu.make_async_copy(media_in, media_v, loc.at[7]),
    ] + [
        pltpu.make_async_copy(
            up_in.at[:, q * 256 : (q + 1) * 256], wide.at[q, img, :, 0:256], loc.at[7 + q]
        )
        for q in range(1, 4)
    ]
    for copy in local:
        copy.start()

    barrier = pltpu.get_barrier_semaphore()
    peers = [zdev(zat(k)) for k in near] + [xdev, ydev, cdev]
    for dev in peers:
        pl.semaphore_signal(barrier, inc=1, device_id=dev, device_id_type=pl.DeviceIdType.MESH)
    pl.semaphore_wait(barrier, len(peers))

    def lanes(ii):
        return pl.ds(pl.multiple_of(ii * 128, 128), 128)

    part = gain_in.shape[1]
    norm_own = normg.at[head, :, lanes(img)]
    normv[:, 0:128] = jnp.zeros((8, 128), f32)
    normv[0:3, 0:part] = gain_in[...].astype(f32)
    normv[3:6, 0:part] = bias_in[...].astype(f32)
    norm_own[...] = pltpu.roll(normv[:, 0:128], head * part, 1)
    for k in near:
        send(norm_own, norm_own, sent.at[0], nb_z.at[z], zdev(zat(k)))
    for copy in local[0:4]:
        copy.wait()

    def put_slab(uu, sem, dev):
        send(slab.at[uu], slab.at[uu], sent.at[1], sem, dev)

    def put_line(ii):
        uu = ii * n_head + head
        put_slab(uu, at_z.at[z, ii % n_x], zdev(z2))
        put_slab(uu, at_z.at[z, ii % n_x], zdev(z1))

        @pl.when(mid)
        def _():
            put_slab(uu, at_z.at[z, ii % n_x], zdev(z3))

    def put_chip(ii):
        uu = ii * n_head + head
        put_slab(uu, at_y.at[ii], ydev)
        put_slab(uu, at_c.at[ii, y], cdev)

    put_slab(unit, at_x.at[0], xdev)
    put_line(img)
    put_chip(img)

    for copy in [local[4]] + local[8:11]:
        copy.wait()
    down = down_in[...]
    for j in range(hidden // 128):
        at = 256 + (j % 2) * 128
        wide[j // 2, img, :, at : at + 128] = tpose(down[j * 128 : (j + 1) * 128, :])

    local[5].wait()
    filled = counts[0]
    for m in range(slots):
        keep = jnp.clip(filled - m, 0, 1).astype(f32)
        cotr[head * slots + m] = (pair[m].astype(f32) * keep).astype(bf16)

    def nb_wait(kind, idx, ref):
        arrived(ref, kind.at[idx])

    for k in near:
        zz = zat(k)
        arrived(normg.at[head, :, lanes(zz * n_x + x)], nb_z.at[zz])
    for k in (0,) + near:
        zz = zat(k)
        ii = zz * n_x + x
        send(normg.at[head, :, lanes(ii)], normg.at[head, :, lanes(ii)], sent.at[2], nb_x.at[zz], xdev)

    def at_forward_x():
        ii = z * n_x + xp
        arrived(slab.at[ii * n_head + head], at_x.at[0])
        put_line(ii)
        put_chip(ii)

    def at_forward_z(zz, xx, onward):
        ii = zz * n_x + xx
        uu = ii * n_head + head
        arrived(slab.at[uu], at_z.at[zz, xx])
        if onward:

            @pl.when(mid)
            def _():
                put_slab(uu, at_z.at[zz, xx], zdev(z1))

        put_chip(ii)

    def at_forward_y(ii):
        uu = ii * n_head + yp * 2 + c
        arrived(slab.at[uu], at_y.at[ii])
        put_slab(uu, at_c.at[ii, yp], cdev)

    def ff_unit(q, ii):
        return wide.at[q, ii]

    def ff_own_z(q):
        piece = ff_unit(q, img)
        send(piece, piece, sent.at[5], ff_z.at[z, q], zdev(z2))
        send(piece, piece, sent.at[5], ff_z.at[z, q], zdev(z1))

        @pl.when(mid)
        def _():
            send(piece, piece, sent.at[5], ff_z.at[z, q], zdev(z3))

    def ff_own_x(q):
        piece = ff_unit(q, img)
        send(piece, piece, sent.at[6], ff_x.at[z, q], xdev)

    def ff_forward(e):
        q, k = e // 3, e % 3
        zz = (z2 * (2 - k) * (1 - k) + z1 * 2 * k * (2 - k) + z3 * k * (k - 1)) // 2
        piece = ff_unit(q, zz * n_x + x)
        arrived(piece, ff_z.at[zz, q])

        @pl.when(jnp.logical_and(mid, k == 0))
        def _():
            send(piece, piece, sent.at[5], ff_z.at[zz, q], zdev(z1))

        send(piece, piece, sent.at[6], ff_x.at[zz, q], xdev)

    for q in range(4):
        ff_own_x(q)
    at_forward_x()
    for k in (0,) + near:
        zz = zat(k)
        arrived(normg.at[head, :, lanes(zz * n_x + xp)], nb_x.at[zz])
    send(normg.at[head], normg.at[head], sent.at[3], nb_y.at[0], ydev)
    send(normg.at[head], normg.at[head], sent.at[4], nb_c.at[y], cdev)
    at_forward_z(z2, x, True)
    at_forward_z(z1, x, False)
    at_forward_z(z3, x, False)
    arrived(normg.at[yp * 2 + c], nb_y.at[0])
    send(normg.at[yp * 2 + c], normg.at[yp * 2 + c], sent.at[4], nb_c.at[yp], cdev)
    at_forward_z(z2, xp, True)
    for q in range(2):
        ff_own_z(q)
    own_cot = cotr.at[pl.ds(head * slots, slots)]

    arrived(normg.at[y * 2 + cp], nb_c.at[y])
    arrived(normg.at[yp * 2 + cp], nb_c.at[yp])
    normv[...] = normg[0] + normg[1] + normg[2] + normg[3]

    def gain(j):
        return normv[j : j + 1, :]

    def shift(j):
        return normv[3 + j : 4 + j, :]

    def statistics(values):
        centered = values - jnp.mean(values, axis=-1, keepdims=True)
        inverse = lax.rsqrt(jnp.mean(centered * centered, axis=-1, keepdims=True) + 1e-05)
        return centered * inverse, inverse

    def norm_rows(values, j):
        return (statistics(values)[0] * gain(j) + shift(j)).astype(bf16)

    half = queries // 2

    def norm_latent(m, carry):
        for r in range(2):
            rows = slice(r * half, (r + 1) * half)
            latent_n[m, rows, :] = norm_rows(latent_v[m, rows, :].astype(f32), 1)
        return carry

    def norm_media(m, carry):
        for r in range(2):
            rows = slice(r * half, (r + 1) * half)
            media_n[m, rows, :] = norm_rows(media_v[m, rows, :].astype(f32), 0)
        return carry

    local[6].wait()
    lax.fori_loop(0, slots, norm_latent, 0)
    at_forward_z(z1, xp, False)
    at_forward_y(img)
    at_forward_y(z * n_x + xp)
    at_forward_z(z3, xp, False)
    send(own_cot, own_cot, sent.at[7], bg_y.at[0], ydev)
    send(own_cot, own_cot, sent.at[7], bg_c.at[y], cdev)
    local[7].wait()
    blocks = media_v.shape[0]
    step = blocks // 4
    order = [z2 * n_x + x, z1 * n_x + x, z3 * n_x + x, z2 * n_x + xp, z1 * n_x + xp, z3 * n_x + xp]
    for r in range(4):
        lax.fori_loop(r * step, (r + 1) * step, norm_media, 0)
        at_forward_y(order[r])

    def turn_media(r, carry):
        block = media_n[pl.ds(r * 2, 2)].reshape(128, width)
        for d in range(width // 128):
            media_t[d * 128 : (d + 1) * 128, pl.ds(pl.multiple_of(r * 128, 128), 128)] = tpose(
                block[:, d * 128 : (d + 1) * 128]
            )
        return carry

    rows_latent = slots * queries

    def turn_latent(source, target, columns):
        whole = source[...].reshape(rows_latent, columns)
        for r in range(0, rows_latent, 128):
            stop = min(r + 128, rows_latent)
            for d in range(columns // 128):
                target[d * 128 : (d + 1) * 128, r:stop] = tpose(
                    whole[r:stop, d * 128 : (d + 1) * 128]
                )

    turn_latent(latent_n, latent_t, width)
    lax.fori_loop(0, blocks * queries // 128, turn_media, 0)
    ff_forward(0)
    at_forward_y(order[4])
    ff_forward(1)
    at_forward_y(order[5])

    for ii in range(8):
        for yy in range(2):
            arrived(slab.at[ii * n_head + yy * 2 + cp], at_c.at[ii, yy])
    ff_forward(2)
    ff_own_z(2)

    query_full[:, 0] = slab[:, 48:64, 0:inner]
    query_full[:, 1] = slab[:, 48:64, inner:width]

    def query_tile(cols):
        return query_full[:, :, :, cols].reshape(width, -1)

    def kv_tile(cols):
        return slab[:, 0:32, cols].reshape(width, -1)

    def out_tile(cols):
        return slab[:, 32:48, cols].reshape(inner, -1)

    latent_rows_n = latent_n[...].reshape(rows_latent, width)

    def tile(t):
        return pl.ds(pl.multiple_of(t * 256, 256), 256)

    query_v[...] = (
        (dot_nn(latent_rows_n, query_full[...].reshape(width, inner)) * scale)
        .astype(bf16)
        .reshape(slots, queries, inner)
    )
    groups = kv_media.shape[0]
    media_rows_n = media_n[...].reshape(groups * 256, width)

    def kv_step(t, carry):
        weight = kv_tile(tile(t))
        kv_latent[:, :, tile(t)] = dot_nn(latent_rows_n, weight).astype(bf16).reshape(slots, queries, 256)
        kv_media[:, :, tile(t)] = dot_nn(media_rows_n, weight).astype(bf16).reshape(groups, 256, 256)
        return carry

    def kv_two(i, carry):
        ff_forward(3 + i)
        return lax.fori_loop(2 * i, 2 * i + 2, kv_step, carry)

    lax.fori_loop(0, width // 512, kv_two, 0)
    ff_forward(5)
    ff_own_z(3)

    def lane_mask(hh, dtype):
        lane = lax.broadcasted_iota(jnp.int32, (1, 256), 1)
        return (lane // queries == hh).astype(f32).astype(dtype)

    def spread(rows):
        return jnp.concatenate([rows * lane_mask(hh, bf16) for hh in range(4)], axis=0)

    def fold(rows):
        total = rows[0:queries] * lane_mask(0, f32)
        for hh in range(1, 4):
            total = total + rows[hh * queries : (hh + 1) * queries] * lane_mask(hh, f32)
        return total

    def probabilities(m, g):
        q_rows = spread(query_v[m, :, tile(g)])
        k_media = kv_media[m, :, tile(g)]
        k_latent = kv_latent[m, :, tile(g)]
        s_media = contract_cols(q_rows, k_media)
        s_latent = contract_cols(q_rows, k_latent)
        top = jnp.maximum(
            jnp.max(s_media, axis=-1, keepdims=True), jnp.max(s_latent, axis=-1, keepdims=True)
        )
        e_media = jnp.exp(s_media - top)
        e_latent = jnp.exp(s_latent - top)
        total = jnp.sum(e_media, axis=-1, keepdims=True) + jnp.sum(e_latent, axis=-1, keepdims=True)
        inverse = 1.0 / total
        return q_rows, k_media, k_latent, e_media * inverse, e_latent * inverse

    def attend(m, g):
        p_media, p_latent = probabilities(m, g)[3:]
        v_media = kv_media[m, :, tile(g + 2)]
        v_latent = kv_latent[m, :, tile(g + 2)]
        rows = dot_nn(p_media.astype(bf16), v_media) + dot_nn(p_latent.astype(bf16), v_latent)
        att_v[m, :, tile(g)] = fold(rows).astype(bf16)

    def forward_image(m, carry):
        attend(m, 0)
        attend(m, 1)
        mid_v[m] = latent_v[m].astype(f32) + dot_nn(att_v[m], out_tile(slice(0, width)))
        for r in range(2):
            rows = slice(r * half, (r + 1) * half)
            hid[head * slots + m, rows, :] = norm_rows(mid_v[m, rows, :], 2)
        piece = hid.at[head * slots + m]
        send(piece, piece, sent.at[8], hd_y.at[m], ydev)
        send(piece, piece, sent.at[8], hd_c.at[m], cdev)

        @pl.when(jnp.logical_and(m >= 1, m <= 3))
        def _():
            ff_forward(5 + m)

        return carry

    lax.fori_loop(0, slots, forward_image, 0)

    other = yp * 2 + c
    cot_other = cotr.at[pl.ds(other * slots, slots)]
    arrived(cot_other, bg_y.at[0])
    send(cot_other, cot_other, sent.at[7], bg_c.at[yp], cdev)
    turn_latent(att_v, att_t, inner)
    for yy in (y, yp):
        arrived(cotr.at[pl.ds((yy * 2 + cp) * slots, slots)], bg_c.at[yy])

    all_rows = n_head * slots * queries

    def turn_rows(source, slot):
        def body(r, carry):
            block = source[pl.ds(r * 2, 2)].reshape(128, width)
            for d in range(width // 128):
                turned[slot, d * 128 : (d + 1) * 128, pl.ds(pl.multiple_of(r * 128, 128), 128)] = tpose(
                    block[:, d * 128 : (d + 1) * 128]
                )
            return carry

        lax.fori_loop(0, all_rows // 128, body, 0)

    turn_rows(cotr, 1)

    act_at = 4 * slots

    def ff_rows(q, start):
        rows = pl.ds(start, 2 * slots)
        pre = dot_nn(hid[rows].reshape(all_rows // 2, width), wide[q, :, :, 0:256].reshape(width, 256))
        grad = dot_nn(cotr[rows].reshape(all_rows // 2, width), wide[q, :, :, 256:512].reshape(width, 256))
        below = 0.5 * (1.0 + lax.erf(pre * 0.7071067811865476))
        slope = below + pre * (jnp.exp(-0.5 * pre * pre) * 0.3989422804014327)
        pair[rows, :, tile(q)] = (grad * slope).astype(bf16).reshape(2 * slots, queries, 256)
        pair[pl.ds(act_at + start, 2 * slots), :, tile(q)] = (
            (pre * below).astype(bf16).reshape(2 * slots, queries, 256)
        )

    def ff_near(q, carry):
        for zz in range(n_z):
            arrived(ff_unit(q, zz * n_x + xp), ff_x.at[zz, q])
        ff_rows(q, y * 2 * slots)
        return carry

    def ff_far(q, carry):
        ff_rows(q, yp * 2 * slots)
        return carry

    def hid_near(m, carry):
        arrived(hid.at[(y * 2 + cp) * slots + m], hd_c.at[m])
        return carry

    def hid_forward(m, carry):
        piece = hid.at[other * slots + m]
        arrived(piece, hd_y.at[m])
        send(piece, piece, sent.at[8], hd_f.at[m], cdev)
        return carry

    def hid_far(m, carry):
        arrived(hid.at[(yp * 2 + cp) * slots + m], hd_f.at[m])
        return carry

    def grad_tile(q, carry):
        def over_parts(part, carry2):
            right = pair[pl.ds(part * act_at, act_at), :, tile(q)].reshape(all_rows, 256)
            value = dot_nn(turned[part], right).astype(bf16).reshape(n_z, n_x, 128, 256)
            grads[q, part, 0] = value[:, 0]
            grads[q, part, 1] = value[:, 1]
            send(grads.at[q, part, xp], xrecv.at[q, part], sent.at[11], rf_x.at[q, part], xdev)
            return carry2

        return lax.fori_loop(0, 2, over_parts, carry)

    def ff_near_and_forward(q, carry):
        ff_near(q, 0)
        ff_forward(9 + q)
        return carry

    lax.fori_loop(0, slots, hid_near, 0)
    lax.fori_loop(0, 3, ff_near_and_forward, 0)
    lax.fori_loop(0, slots, hid_forward, 0)
    lax.fori_loop(0, slots, hid_far, 0)
    lax.fori_loop(0, 3, ff_far, 0)
    turn_rows(hid, 0)
    grad_tile(0, 0)
    ff_near(3, 0)
    ff_far(3, 0)

    def wide_rows(part, q, t):
        return wide[q, pl.ds(t * 4, 4), :, part * 256 : (part + 1) * 256].reshape(512, 256)

    def broad(t):
        return pl.ds(pl.multiple_of(t * 512, 512), 512)

    def back_rows(left, part, t):
        total = contract_cols(left[:, 0:256], wide_rows(part, 0, t))
        for q in range(1, 4):
            total = total + contract_cols(left[:, q * 256 : (q + 1) * 256], wide_rows(part, q, t))
        return total

    def head_sum(part):
        def rows_of(hh):
            return pair[pl.ds(part * act_at + hh * slots, slots)].reshape(rows_latent, hidden)

        for slot, hh in enumerate((yp * 2 + cp, y * 2 + cp)):
            left = rows_of(hh)

            def to_core(t, carry, left=left, slot=slot):
                value = back_rows(left, part, t)
                hsend[slot, :, :, broad(t)] = value.astype(bf16).reshape(slots, queries, 512)
                return carry

            lax.fori_loop(0, width // 512, to_core, 0)
            send(hsend.at[slot], hrecv.at[part, slot], sent.at[9], hp_c.at[part, slot], cdev)
        left_y = rows_of(yp * 2 + c)
        arrived(hrecv.at[part, 0], hp_c.at[part, 0])

        def to_y(t, carry):
            value = back_rows(left_y, part, t).reshape(slots, queries, 512)
            hysend[part, t] = (value + hrecv[part, 0, :, :, broad(t)].astype(f32)).astype(bf16)
            send(hysend.at[part, t], hyrecv.at[part, t], sent.at[10], hp_y.at[part], ydev)
            return carry

        lax.fori_loop(0, width // 512, to_y, 0)
        left_own = rows_of(head)
        arrived(hrecv.at[part, 1], hp_c.at[part, 1])

        def to_own(t, carry):
            value = back_rows(left_own, part, t).reshape(slots, queries, 512)
            hown[part, :, :, broad(t)] = value + hrecv[part, 1, :, :, broad(t)].astype(f32)
            return carry

        lax.fori_loop(0, width // 512, to_own, 0)

    arrived(hid.at[0 : 3 * slots], sent.at[8])
    head_sum(0)

    def sum_tile(u):
        q, part = u // 2, u % 2
        arrived(xrecv.at[q, part], rf_x.at[q, part])
        for k, zz in enumerate((z1, z2, z3)):
            grads[q, part, x, zz] = (
                grads[q, part, x, zz].astype(f32) + xrecv[q, part, zz].astype(f32)
            ).astype(bf16)
            send(grads.at[q, part, x, zz], zrecv.at[k, part, q], sent.at[12], rf_z.at[k, part], zdev(zz))

    grad_tile(1, 0)
    arrived(hsend, sent.at[9])
    head_sum(1)
    lax.fori_loop(2, 4, grad_tile, 0)
    sum_tile(0)
    sum_tile(1)

    gacc[...] = jnp.zeros_like(gacc)

    def tally(j, upper, xhat):
        gacc[j] += jnp.sum((upper * xhat).reshape(-1, 8, width), axis=0)
        gacc[3 + j] += jnp.sum(upper.reshape(-1, 8, width), axis=0)

    def norm_back(values, j, upper):
        xhat, inverse = statistics(values)
        tally(j, upper, xhat)
        g = upper * gain(j)
        return inverse * (
            g - jnp.mean(g, axis=-1, keepdims=True) - xhat * jnp.mean(g * xhat, axis=-1, keepdims=True)
        )

    sum_tile(2)
    arrived(hyrecv.at[0], hp_y.at[0])

    def mid_back(m, carry):
        upper = hown[0, m] + jnp.concatenate([hyrecv[0, 0, m], hyrecv[0, 1, m]], axis=-1).astype(f32)
        back = norm_back(mid_v[m], 2, upper)
        total = cotr[head * slots + m].astype(f32) + back
        hown[0, m] = total
        delta_v[m] = total.astype(bf16)
        return carry

    lax.fori_loop(0, slots, mid_back, 0)
    delta_rows = delta_v[...].reshape(rows_latent, width)

    attg_v[...] = (
        contract_cols(delta_rows, out_tile(slice(0, width))).astype(bf16).reshape(slots, queries, inner)
    )

    gslab = pair

    def gunit(ii, hh_y, hh_c):
        return ii * 4 + hh_c * 2 + hh_y

    def out_grad_step(t, carry):
        right = delta_v[:, :, broad(t)].reshape(rows_latent, 512)
        value = dot_nn(att_t[...], right).astype(bf16)
        for ii in range(8):
            for hh in range(4):
                at = (ii * 4 + hh) * 16
                gslab[gunit(ii, hh // 2, hh % 2), 32:48, broad(t)] = value[at : at + 16]
        return carry

    lax.fori_loop(0, width // 512, out_grad_step, 0)
    sum_tile(3)

    def back_pair(m, g):
        q_rows, k_media, k_latent, p_media, p_latent = probabilities(m, g)
        v_media = kv_media[m, :, tile(g + 2)]
        v_latent = kv_latent[m, :, tile(g + 2)]
        up_rows = spread(attg_v[m, :, tile(g)])
        g_media = contract_cols(up_rows, v_media)
        g_latent = contract_cols(up_rows, v_latent)
        dotted = jnp.sum(g_media * p_media, axis=-1, keepdims=True) + jnp.sum(
            g_latent * p_latent, axis=-1, keepdims=True
        )
        d_media = (p_media * (g_media - dotted)).astype(bf16)
        d_latent = (p_latent * (g_latent - dotted)).astype(bf16)
        qgrad_v[m, :, tile(g)] = fold(dot_nn(d_media, k_media) + dot_nn(d_latent, k_latent)).astype(bf16)
        kv_media[m, :, tile(g)] = contract_rows(d_media, q_rows).astype(bf16)
        kv_latent[m, :, tile(g)] = contract_rows(d_latent, q_rows).astype(bf16)
        kv_media[m, :, tile(g + 2)] = contract_rows(p_media.astype(bf16), up_rows).astype(bf16)
        kv_latent[m, :, tile(g + 2)] = contract_rows(p_latent.astype(bf16), up_rows).astype(bf16)

    def back_image(m, carry):
        back_pair(m, 0)
        back_pair(m, 1)
        return carry

    lax.fori_loop(0, slots, back_image, 0)

    sum_tile(4)

    gcr = hid
    gyr_v = media_n

    def kv_grad_chunk(zz):
        rows = pl.ds(pl.multiple_of(zz * 256, 256), 256)
        left_media = media_t[rows, :]
        left_latent = latent_t[rows, :]

        value = dot_nn(left_media, kv_media[...].reshape(groups * 256, width)) + dot_nn(
            left_latent, kv_latent[...].reshape(rows_latent, width)
        )
        value = value.astype(bf16)
        value_q = dot_nn(left_latent, qgrad_v[...].reshape(rows_latent, inner)) * scale
        value_q = value_q.astype(bf16)
        for xx in range(2):
            for hh in range(4):
                at = (xx * 4 + hh) * 32
                uu = gunit(zz * n_x + xx, hh // 2, hh % 2)
                gslab[uu, 0:32, :] = value[at : at + 32]
                gslab[uu, 48:64, 0:inner] = value_q[at : at + 16]
                gslab[uu, 48:64, inner:width] = value_q[at + 16 : at + 32]
        for xx in range(2):
            ii = zz * n_x + xx
            send(
                gslab.at[pl.ds(ii * 4 + cp * 2, 2)],
                gcr.at[pl.ds(ii * 2, 2)],
                sent.at[13],
                ra_c.at[ii],
                cdev,
            )

    def stage_y(zz):
        for xx in (xp, x):
            ii = zz * n_x + xx
            arrived(gcr.at[pl.ds(ii * 2, 2)], ra_c.at[ii])
            uu = gunit(ii, yp, c)
            gslab[uu] = (gslab[uu].astype(f32) + gcr[ii * 2 + yp].astype(f32)).astype(bf16)
            send(gslab.at[uu], gyr_v.at[ii], sent.at[14], ra_y.at[ii], ydev)

    def upto_y(ii):
        return (
            gslab[gunit(ii, y, c)].astype(f32) + gcr[ii * 2 + y].astype(f32) + gyr_v[ii].astype(f32)
        )

    def stage_x(zz):
        ii = zz * n_x + xp
        arrived(gyr_v.at[ii], ra_y.at[ii])
        uu = gunit(ii, y, c)
        gslab[uu] = upto_y(ii).astype(bf16)
        send(gslab.at[uu], gyr_v.at[8 + zz], sent.at[15], ra_x.at[zz], xdev)

    def stage_z(zz, last):
        ii = zz * n_x + x
        arrived(gyr_v.at[ii], ra_y.at[ii])
        arrived(gyr_v.at[8 + zz], ra_x.at[zz])
        if last:
            return upto_y(ii) + gyr_v[8 + zz].astype(f32)
        uu = gunit(ii, y, c)
        gslab[uu] = (upto_y(ii) + gyr_v[8 + zz].astype(f32)).astype(bf16)
        send(gslab.at[uu], gzr_v.at[z], sent.at[16], ra_z.at[z], zdev(zz))
        return None

    chunk = [zat(1), zat(3), zat(2), z]
    kv_grad_chunk(chunk[0])
    kv_grad_chunk(chunk[1])
    stage_y(chunk[0])
    kv_grad_chunk(chunk[2])
    stage_y(chunk[1])
    kv_grad_chunk(chunk[3])
    stage_y(chunk[2])
    sum_tile(5)

    arrived(hyrecv.at[1], hp_y.at[1])
    new_v = delta_v

    for m in range(slots):
        keep = jnp.clip(filled - m, 0, 1).astype(f32)
        for r in range(2):
            rows = slice(r * half, (r + 1) * half)
            branch = hown[1, m, rows, :] + jnp.concatenate(
                [hyrecv[1, 0, m, rows, :], hyrecv[1, 1, m, rows, :]], axis=-1
            ).astype(f32)
            new_v[m, rows, :] = ((mid_v[m, rows, :] + branch) * keep).astype(bf16)
    stage_y(chunk[3])

    def media_back(m, carry):
        hown[1, 0:4] = contract_cols(kv_media[m], kv_tile(slice(0, width))).reshape(4, 64, width)

        def over_rows(r, carry2):
            block = m * 4 + r
            back = norm_back(media_v[block].astype(f32), 0, hown[1, r])
            media_v[block] = back.astype(bf16)
            return carry2

        lax.fori_loop(0, 4, over_rows, 0)
        return carry

    def latent_back_tiles(t, carry):
        weight = slab[pl.ds(t * 16, 16), 0:32, :].reshape(512, width)
        query_weight = query_full[pl.ds(t * 16, 16)].reshape(512, inner)
        hown[1, :, :, broad(t)] = (
            contract_cols(kv_latent[...].reshape(rows_latent, width), weight)
            + contract_cols(qgrad_v[...].reshape(rows_latent, inner), query_weight) * scale
        ).reshape(slots, queries, 512)
        return carry

    def latent_back(m, carry):
        back = norm_back(latent_v[m].astype(f32), 1, hown[1, m])
        latent_v[m] = (hown[0, m] + back).astype(bf16)
        return carry

    lax.fori_loop(0, width // 512, latent_back_tiles, 0)
    lax.fori_loop(0, slots, latent_back, 0)
    sum_tile(6)
    lax.fori_loop(0, 2, media_back, 0)
    sum_tile(7)
    stage_x(chunk[0])
    lax.fori_loop(2, 4, media_back, 0)
    stage_x(chunk[1])
    stage_z(chunk[0], False)
    lax.fori_loop(4, 5, media_back, 0)

    for j in range(6):
        gsend[0, j : j + 1, :] = jnp.sum(gacc[j], axis=0, keepdims=True)
    gsend[0, 6:8, :] = jnp.zeros((2, width), f32)
    send(gsend.at[0], gyr.at[0], sent.at[17], gr_c.at[0], cdev)
    arrived(gyr.at[0], gr_c.at[0])
    gsend[1] = gsend[0] + gyr[0]
    send(gsend.at[1], gyr.at[1], sent.at[17], gr_c.at[1], xdev)
    stage_z(chunk[1], False)
    arrived(gyr.at[1], gr_c.at[1])
    gsend[2] = gsend[1] + gyr[1]
    for k in near:
        zz = zat(k)
        send(gsend.at[2, :, lanes(zz * n_x + x)], gzr.at[z], sent.at[18], gr_z.at[z], zdev(zz))
    stage_x(chunk[2])
    total = gsend[2, :, lanes(img)]
    for k in near:
        zz = zat(k)
        arrived(gzr.at[zz], gr_z.at[zz])
        total = total + gzr[zz]
    gsend[3, :, 0:128] = total
    send(gsend.at[3, :, 0:128], gyr.at[2, :, 0:128], sent.at[17], gr_c.at[2], ydev)

    for part in range(2):
        for k in range(3):
            arrived(zrecv.at[k, part], rf_z.at[k, part])

    def own_sum(part, q):
        value = grads[q, part, x, z].astype(f32) + xrecv[q, part, z].astype(f32)
        for k in range(3):
            value = value + zrecv[k, part, q].astype(f32)
        return value

    def last_sums(q, carry):
        up_out[:, tile(q)] = own_sum(0, q)
        value = own_sum(1, q)
        for j in range(2):
            rows = pl.ds(pl.multiple_of(q * 256 + j * 128, 128), 128)
            down_out[rows, :] = tpose(value[:, j * 128 : (j + 1) * 128])
        return carry

    lax.fori_loop(0, hidden // 256, last_sums, 0)

    stage_x(chunk[3])
    stage_z(chunk[2], False)
    arrived(gyr.at[2, :, 0:128], gr_c.at[2])
    norm_out[...] = gsend[3, :, 0:128] + gyr[2, :, 0:128]
    final = stage_z(chunk[3], True)
    for k in near:
        zz = zat(k)
        arrived(gzr_v.at[zz], ra_z.at[zz])
        final = final + gzr_v[zz].astype(f32)
    key_value_out[...] = final[0:32]
    output_out[...] = final[32:48]
    query_out[0:16, :] = final[48:64, 0:inner]
    query_out[16:32, :] = final[48:64, inner:width]

    arrived(normg.at[0, :, 0:384], sent.at[0])
    arrived(slab.at[0:29], sent.at[1])

    @pl.when(mid)
    def _():
        arrived(slab.at[0:4], sent.at[1])
        arrived(wide.at[0], sent.at[5])

    arrived(normg.at[0, :, 0:512], sent.at[2])
    arrived(normg.at[0], sent.at[3])
    arrived(normg.at[0:2], sent.at[4])
    arrived(wide.at[0], sent.at[5])
    arrived(wide.at[0:2], sent.at[6])
    arrived(cotr.at[0 : 3 * slots], sent.at[7])
    arrived(hsend, sent.at[9])
    arrived(hysend, sent.at[10])
    arrived(xrecv, sent.at[11])
    arrived(zrecv, sent.at[12])
    arrived(gcr.at[0:16], sent.at[13])
    arrived(gyr_v.at[0:8], sent.at[14])
    arrived(gyr_v.at[0:4], sent.at[15])
    arrived(gyr_v.at[0:3], sent.at[16])
    arrived(gyr.at[0:2], sent.at[17])
    arrived(gyr.at[2, :, 0:128], sent.at[17])
    arrived(gzr.at[0:3], sent.at[18])


def finish_kernel(norms, *refs):
    sources, gains_out, biases_out, targets, sems = refs[:8], refs[8], refs[9], refs[10:18], refs[18]
    copies = [pltpu.make_async_copy(sources[i], targets[i], sems.at[i]) for i in range(8)]
    for copy in copies:
        copy.start()
    part = gains_out.shape[1]
    head = lax.axis_index("head")
    rolled = pltpu.roll(norms[...], (128 - head * part) % 128, 1)
    gains_out[...] = rolled[0:3, 0:part]
    biases_out[...] = rolled[3:6, 0:part]
    for copy in copies:
        copy.wait()


def block_plan(
    media_patches,
    latent_rows,
    media_counts,
    norm_gains,
    norm_biases,
    query_weight,
    key_value_weight,
    output_weight,
    up_weight,
    down_weight,
    cotangent,
):
    slots, patches, width = media_patches.shape[1:]
    queries = latent_rows.shape[2]
    inner = query_weight.shape[1]
    hidden = up_weight.shape[1]
    rows_up = up_weight.shape[0]
    part = norm_gains.shape[1]
    blocks = slots * patches // 64
    bf16, f32 = jnp.bfloat16, jnp.float32
    shape = jax.ShapeDtypeStruct
    hbm = pl.BlockSpec(memory_space=pl.ANY)
    vmem = pl.BlockSpec(memory_space=pltpu.VMEM)
    smem = pl.BlockSpec(memory_space=pltpu.SMEM)
    dma = pltpu.SemaphoreType.DMA
    all_rows = 4 * slots * queries
    rows_latent = slots * queries
    outs = pl.pallas_call(
        block_kernel,
        out_shape=(
            pltpu.VMEM((slots, queries, width), bf16),
            pltpu.VMEM((blocks, 64, width), bf16),
            pltpu.VMEM((slots, queries, width), bf16),
            pltpu.VMEM((8, 128), f32),
            pltpu.VMEM(query_weight.shape, f32),
            pltpu.VMEM(key_value_weight.shape, f32),
            pltpu.VMEM(output_weight.shape, f32),
            pltpu.VMEM(up_weight.shape, f32),
            pltpu.VMEM(down_weight.shape, f32),
        ),
        in_specs=[smem] + [hbm] * 7 + [vmem] * 3,
        out_specs=(vmem,) * 9,
        scratch_shapes=[
            pltpu.VMEM((32, 64, width), bf16),
            pltpu.VMEM((32, 2, 16, inner), bf16),
            pltpu.VMEM((4, 8, rows_up, 512), bf16),
            pltpu.VMEM((4 * slots, queries, width), bf16),
            pltpu.VMEM((4 * slots, queries, width), bf16),
            pltpu.VMEM((2, width, all_rows), bf16),
            pltpu.VMEM((blocks, 64, width), bf16),
            pltpu.VMEM((slots, queries, width), bf16),
            pltpu.VMEM((width, slots * patches), bf16),
            pltpu.VMEM((width, rows_latent), bf16),
            pltpu.VMEM((slots, patches, 2 * inner), bf16),
            pltpu.VMEM((slots, queries, 2 * inner), bf16),
            pltpu.VMEM((slots, queries, inner), bf16),
            pltpu.VMEM((slots, queries, inner), bf16),
            pltpu.VMEM((inner, rows_latent), bf16),
            pltpu.VMEM((slots, queries, width), f32),
            pltpu.VMEM((8 * slots, queries, width), bf16),
            pltpu.VMEM((4, 2, 2, 4, rows_up, 256), bf16),
            pltpu.VMEM((4, 2, 4, rows_up, 256), bf16),
            pltpu.VMEM((3, 2, 4, rows_up, 256), bf16),
            pltpu.VMEM((2, slots, queries, width), bf16),
            pltpu.VMEM((2, 2, slots, queries, width), bf16),
            pltpu.VMEM((2, 2, slots, queries, width // 2), bf16),
            pltpu.VMEM((2, 2, slots, queries, width // 2), bf16),
            pltpu.VMEM((2, slots, queries, width), f32),
            pltpu.VMEM((slots, queries, inner), bf16),
            pltpu.VMEM((slots, queries, inner), bf16),
            pltpu.VMEM((4, 8, width), f32),
            pltpu.VMEM((8, width), f32),
            pltpu.VMEM((6, 8, width), f32),
            pltpu.VMEM((4, 8, width), f32),
            pltpu.VMEM((3, 8, width), f32),
            pltpu.VMEM((4, 8, 128), f32),
            pltpu.VMEM((4, 64, width), bf16),
            dma((11,)),
            dma((4, 2)),
            dma((1,)),
            dma((8,)),
            dma((8, 2)),
            dma((4, 4)),
            dma((4, 4)),
            dma((4,)),
            dma((4,)),
            dma((1,)),
            dma((2,)),
            dma((slots,)),
            dma((slots,)),
            dma((slots,)),
            dma((1,)),
            dma((2,)),
            dma((2, 2)),
            dma((2,)),
            dma((4, 2)),
            dma((4, 2)),
            dma((8,)),
            dma((8,)),
            dma((4,)),
            dma((4,)),
            dma((3,)),
            dma((4,)),
            dma((19,)),
        ],
        compiler_params=pltpu.CompilerParams(
            collective_id=0, has_side_effects=True, vmem_limit_bytes=61796352
        ),
    )(
        media_counts,
        media_patches.reshape(blocks, 64, width),
        latent_rows.reshape(slots, queries, width),
        cotangent.reshape(slots, queries, width),
        query_weight,
        key_value_weight,
        output_weight,
        up_weight,
        down_weight,
        norm_gains,
        norm_biases,
    )
    norms = outs[3]
    rest = outs[:3] + outs[4:]
    done = pl.pallas_call(
        finish_kernel,
        out_shape=(shape((3, part), f32), shape((3, part), f32)) + tuple(shape(v.shape, v.dtype) for v in rest),
        in_specs=[vmem] * 9,
        out_specs=(vmem, vmem) + (hbm,) * 8,
        scratch_shapes=[dma((8,))],
        compiler_params=pltpu.CompilerParams(vmem_limit_bytes=4194304),
    )(norms, *rest)
    gains_grad, biases_grad, new, media_grad, latent_grad = done[:5]
    return (
        new.reshape(latent_rows.shape),
        media_grad.reshape(media_patches.shape),
        latent_grad.reshape(latent_rows.shape),
        gains_grad,
        biases_grad,
    ) + tuple(done[5:])


def block_fits(mesh):
    return mesh.shape["img"] == 8 and mesh.shape["head"] == 4


def solution(mesh):
    return jax.shard_map(
        block_plan if block_fits(mesh) else gathered_plan,
        mesh=mesh,
        in_specs=(
            P(("img", "head"), None, None, None),
            P(("img", "head"), None, None, None),
            P(("img", "head")),
            P(None, ("img", "head")),
            P(None, ("img", "head")),
            P(("img", "head"), None),
            P(("img", "head"), None),
            P(("img", "head"), None),
            P("img", "head"),
            P("head", "img"),
            P(("img", "head"), None, None, None),
        ),
        out_specs=(
            P(("img", "head"), None, None, None),
            P(("img", "head"), None, None, None),
            P(("img", "head"), None, None, None),
            P(None, ("img", "head")),
            P(None, ("img", "head")),
            P(("img", "head"), None),
            P(("img", "head"), None),
            P(("img", "head"), None),
            P("img", "head"),
            P("head", "img"),
        ),
        check_vma=False,
    )
```
